32 devices in a mesh: groups: 2 (over y), points: 4 (over z), centers: 4 (over x, core).
Axes of the slice: x: 2, y: 2, z: 4, core: 2. Of those that a mesh axis runs over, the one named last changes fastest.
Arguments:
- train_points: bfloat16 [8192, 512], P(('groups', 'points')), parts along dimension 0, may hold values from -6 to 6
- saved_preds: float32 [8192, 128], P(('groups', 'points')), parts along dimension 0, may hold values from -6 to 6
- targets: float32 [8192, 128], P(('groups', 'points')), parts along dimension 0, may hold values from -6 to 6
- huber_delta: float32 [256], P('groups'), parts along dimension 0, may hold values from 0.3 to 3
- center_pos: bfloat16 [16384, 512], P(('groups', 'points', 'centers')), parts along dimension 0, may hold values from -6 to 6
- coefficients: bfloat16 [16384, 128], P(('groups', 'points', 'centers')), parts along dimension 0, may hold values from -0.8984375 to 0.8984375
- spread: bfloat16 [16384], P(('groups', 'points', 'centers')), parts along dimension 0, may hold values from 0.5 to 2
Outputs:
- grad_centers: float32 [16384, 512], P(('groups', 'points', 'centers')), parts along dimension 0
- grad_coef: float32 [16384, 128], P(('groups', 'points', 'centers')), parts along dimension 0
The draws below stay inside these ranges and needn't reach their ends.
There are 2 independent parts, one for each index of `groups`. The reference program is written for one: setup_inputs(seed, part) draws one part's arguments, and reference() takes and returns one part's arrays. A program takes and returns all parts, laid end to end along the dimension named above; each array names one. Nothing has to cross between parts.
All inputs are finite; a program needn't handle non-finite values.
Results may differ from the reference program's by a relative error of at most 0.0003.
Values may be sent and summed in bfloat16 or wider, within the bound.
No kernel may reach another device: no remote copies, remote signals or barrier semaphores. Data moves between devices by JAX's collectives and lax.ppermute only.
A program may use at most 64 MiB of HBM per device.

```python
import math
import jax
import jax.numpy as jnp
from jax import lax

DIN = 512
DOUT = 128
PTS_DEV = 1024
NPTS = 4096
NC = 8192
N_POINTS = 4


def block_scale(own_key, extent, split, low, largest):
    loudness = 1.0
    for dim, shards_of in split:
        steps = jax.random.uniform(jax.random.fold_in(jax.random.fold_in(own_key, 6), dim), (shards_of,), jnp.float32, low / len(split), largest / len(split))
        loudness = loudness * jnp.repeat(jnp.exp(steps), extent[dim] // shards_of).reshape((-1,) + (1,) * (len(extent) - 1 - dim))
    return loudness


def centred(stream_key, dims, scale, limit, shards=(), held_as=jnp.bfloat16):
    drawn = scale * jax.random.normal(stream_key, dims, jnp.float32)
    if shards:
        drawn = drawn * block_scale(stream_key, dims, shards, -0.22, 0.18)
    return jnp.clip(drawn, -limit, limit).astype(held_as)


def setup_inputs(seed: int = 0, part: int = 0) -> dict:
    splits = jax.random.split(jax.random.key(seed), 8)
    own_keys = jax.random.split(jax.random.fold_in(splits[7], part), 8)
    train_points = centred(own_keys[0], (NPTS, DIN), 1.0, 6.0, ((0, 4),))
    saved_preds = centred(own_keys[1], (NPTS, DOUT), 1.0, 6.0, ((0, 4),), jnp.float32)
    targets = centred(own_keys[2], (NPTS, DOUT), 1.0, 6.0, ((0, 4),), jnp.float32)
    huber_delta = jnp.clip(jnp.exp(jax.random.uniform(own_keys[3], (DOUT,), jnp.float32, math.log(0.3), math.log(3.0))), 0.3, 3.0)
    center_pos = centred(own_keys[4], (NC, DIN), 1.0, 6.0, ((0, 16),))
    coefficients = centred(own_keys[5], (NC, DOUT), 0.15, 0.8984375, ((0, 16),))
    spread = jnp.clip(jnp.exp(math.log(2.0) - 1.3862944 * jax.random.uniform(own_keys[6], (NC,), jnp.float32) ** block_scale(own_keys[6], (NC,), ((0, 16),), -0.2, 0.2)), 0.5, 2.0).astype(jnp.bfloat16)
    return dict(train_points=train_points, saved_preds=saved_preds, targets=targets, huber_delta=huber_delta, center_pos=center_pos, coefficients=coefficients, spread=spread)


def reference(train_points, saved_preds, targets, huber_delta, center_pos, coefficients, spread):
    in_width = train_points.shape[1]
    center_sq = lax.optimization_barrier(jnp.sum(jnp.square(center_pos.astype(jnp.float32)), axis=1))
    rates = spread.astype(jnp.float32)
    point_blocks = train_points.reshape(N_POINTS, PTS_DEV, DIN)
    saved_blocks = saved_preds.reshape(N_POINTS, PTS_DEV, DOUT)
    target_blocks = targets.reshape(N_POINTS, PTS_DEV, DOUT)

    def accumulate(totals, inputs):
        coef_acc, moment, row_totals = totals
        row_block, saved_blk, target_blk = inputs
        point_sq = lax.optimization_barrier(jnp.sum(jnp.square(row_block.astype(jnp.float32)), axis=1))
        cross = jnp.dot(row_block, center_pos.T, preferred_element_type=jnp.float32)
        dist = point_sq[:, None] + center_sq[None, :] - 2.0 * cross
        kernel = jnp.exp(-rates[None, :] * dist / in_width).astype(jnp.bfloat16)
        panel_pred = jnp.dot(kernel, coefficients, preferred_element_type=jnp.float32)
        residual = panel_pred + saved_blk - target_blk
        cotangent = (residual / jnp.sqrt(1.0 + jnp.square(residual / huber_delta[None, :]))).astype(jnp.bfloat16)
        coef_acc = coef_acc + jnp.dot(kernel.T, cotangent, preferred_element_type=jnp.float32)
        mixing = jnp.dot(cotangent, coefficients.T, preferred_element_type=jnp.float32)
        weights = (kernel.astype(jnp.float32) * mixing).astype(jnp.bfloat16)
        row_totals = row_totals + lax.optimization_barrier(jnp.sum(weights.astype(jnp.float32), axis=0))
        moment = moment + jnp.dot(weights.T, row_block, preferred_element_type=jnp.float32)
        return ((coef_acc, moment, row_totals), None)
    start = (jnp.zeros((NC, DOUT), jnp.float32), jnp.zeros((NC, DIN), jnp.float32), jnp.zeros((NC,), jnp.float32))
    (grad_coef, moment, row_totals), _ = lax.scan(accumulate, start, (point_blocks, saved_blocks, target_blocks))
    grad_centers = (2.0 * rates / in_width)[:, None] * (moment - row_totals[:, None] * center_pos.astype(jnp.float32))
    return (grad_centers, grad_coef)
```

```python
import jax
import jax.numpy as jnp
from jax import lax
from jax.sharding import PartitionSpec as P


def swap(a, axis, size, d):
    return lax.ppermute(a, axis, [(i, i ^ d) for i in range(size)])


def solution(mesh):
    nz, nc = mesh.shape["points"], mesh.shape["centers"]

    def per_device(train_points, saved_preds, targets, huber_delta, center_pos, coefficients, spread):
        n_rows, in_width = train_points.shape
        own_centers, out_width = coefficients.shape
        piece = n_rows // nc
        c = lax.axis_index("centers")

        def row_piece(a, d):
            return lax.dynamic_slice_in_dim(a, (c ^ d) * piece, piece)

        own = row_piece(train_points, 0)
        layer = {dz: own if dz == 0 else swap(own, "points", nz, dz) for dz in range(nz)}

        spread_rows = own_centers // 128
        side = jnp.concatenate(
            [coefficients, jnp.pad(spread.reshape(spread_rows, 128), ((0, 16 - spread_rows), (0, 0)))]
        )
        pos, extra = {0: center_pos}, {0: side}
        for d in range(2, nc, 2):
            pos[d], extra[d] = swap(center_pos, "centers", nc, d), swap(side, "centers", nc, d)
        for d in range(0, nc, 2):
            pos[d + 1], extra[d + 1] = swap(pos[d], "centers", nc, 1), swap(extra[d], "centers", nc, 1)
        coef = {d: extra[d][:own_centers] for d in range(nc)}
        rate = {
            d: extra[d][own_centers : own_centers + spread_rows].reshape(own_centers).astype(jnp.float32)
            for d in range(nc)
        }
        center_sq = {d: jnp.sum(jnp.square(pos[d].astype(jnp.float32)), axis=1) for d in range(nc)}

        def partial_pred(rows):
            row_sq = jnp.sum(jnp.square(rows.astype(jnp.float32)), axis=1)
            total = 0.0
            for d in range(nc):
                cross = lax.dot_general(
                    rows, pos[d], (((1,), (1,)), ((), ())), preferred_element_type=jnp.float32
                )
                dist = row_sq[:, None] + center_sq[d][None, :] - 2.0 * cross
                kernel = jnp.exp(-rate[d][None, :] * dist / in_width).astype(jnp.bfloat16)
                total = total + jnp.dot(kernel, coef[d], preferred_element_type=jnp.float32)
            return total

        pred = partial_pred(own)
        for dz in range(1, nz):
            pred = pred + swap(partial_pred(layer[dz]), "points", nz, dz)
        residual = pred + row_piece(saved_preds, 0) - row_piece(targets, 0)
        cot = (residual / jnp.sqrt(1.0 + jnp.square(residual / huber_delta[None, :]))).astype(jnp.bfloat16)

        xs, cots = {}, {}
        for dz in range(nz):
            z_cot = cot if dz == 0 else swap(cot, "points", nz, dz)
            for d in range(0, nc, 2):
                cots[dz, d] = z_cot if d == 0 else swap(z_cot, "centers", nc, d)
                if dz:
                    xs[dz, d] = layer[dz] if d == 0 else swap(layer[dz], "centers", nc, d)
            for d in range(0, nc, 2):
                cots[dz, d + 1] = swap(cots[dz, d], "centers", nc, 1)
                if dz:
                    xs[dz, d + 1] = swap(xs[dz, d], "centers", nc, 1)
            if dz == 0:
                for d in range(nc):
                    xs[0, d] = row_piece(train_points, d)
        order = sorted(xs)
        all_x = jnp.concatenate([xs[k] for k in order])
        all_cot = jnp.concatenate([cots[k] for k in order])

        nt = (((1,), (1,)), ((), ()))
        all_sq = jnp.sum(jnp.square(all_x.astype(jnp.float32)), axis=1)
        cross = lax.dot_general(center_pos, all_x, nt, preferred_element_type=jnp.float32)
        dist = all_sq[None, :] + center_sq[0][:, None] - 2.0 * cross
        own_rate = spread.astype(jnp.float32)
        kernel = jnp.exp(-own_rate[:, None] * dist / in_width).astype(jnp.bfloat16)
        grad_coef = jnp.dot(kernel, all_cot, preferred_element_type=jnp.float32)
        mixing = lax.dot_general(coefficients, all_cot, nt, preferred_element_type=jnp.float32)
        weights = (kernel.astype(jnp.float32) * mixing).astype(jnp.bfloat16)
        totals = jnp.sum(weights.astype(jnp.float32), axis=1)
        moment = jnp.dot(weights, all_x, preferred_element_type=jnp.float32)
        grad_centers = (2.0 * own_rate / in_width)[:, None] * (
            moment - totals[:, None] * center_pos.astype(jnp.float32)
        )
        return (grad_centers, grad_coef)

    return jax.shard_map(
        per_device,
        mesh=mesh,
        in_specs=(
            P(("groups", "points"), None),
            P(("groups", "points"), None),
            P(("groups", "points"), None),
            P("groups"),
            P(("groups", "points", "centers"), None),
            P(("groups", "points", "centers"), None),
            P(("groups", "points", "centers")),
        ),
        out_specs=(
            P(("groups", "points", "centers"), None),
            P(("groups", "points", "centers"), None),
        ),
        check_vma=False,
    )
```

```python
import functools
import math

import jax
import jax.numpy as jnp
from jax import lax
from jax.experimental import pallas as pl
from jax.experimental.pallas import tpu as pltpu
from jax.sharding import PartitionSpec as P

F32, BF16 = jnp.float32, jnp.bfloat16
ANY = pl.BlockSpec(memory_space=pl.ANY)
VMEM = pl.BlockSpec(memory_space=pltpu.VMEM)
NT = (((1,), (1,)), ((), ()))
LOG2E = math.log2(math.e)


def swap(a, axis, size, d):
    return lax.ppermute(a, axis, [(i, i ^ d) for i in range(size)])


def lane_groups(a):
    total = None
    for k in range(0, a.shape[1], 128):
        part = jnp.square(a[:, k : k + 128].astype(F32))
        total = part if total is None else total + part
    return total


def half_sq_row(a):
    return 0.5 * jnp.sum(lane_groups(a).T, axis=0, keepdims=True)


def half_sq_column(a):
    return 0.5 * jnp.sum(lane_groups(a), axis=1, keepdims=True)


def rate_row(side, n, in_width):
    rows = side[n : n + 16].astype(F32)
    row = jnp.concatenate([rows[k : k + 1] for k in range(n // 128)], axis=1)
    return row * (-2.0 * LOG2E / in_width)


def copies(pairs, sems):
    made = [pltpu.make_async_copy(src, dst, sems.at[k]) for k, (src, dst) in enumerate(pairs)]
    for copy in made:
        copy.start()
    return made


def forward(rows, blocks, sides, stats=None):
    nb, (n, in_width), out_width = len(blocks), blocks[0].shape, sides[0].shape[1]
    first = stats is None

    def body(*refs):
        rows_ref, block_refs, side_refs = refs[0], refs[1 : 1 + nb], refs[1 + nb : 1 + 2 * nb]
        if first:
            out_ref, stats_ref, pos, side, sems = refs[1 + 2 * nb :]
        else:
            stats_ref, out_ref, pos, side, sems = refs[1 + 2 * nb :]
        pairs = []
        for b in range(nb):
            pairs += [(block_refs[b], pos.at[b]), (side_refs[b], side.at[b])]
        made = copies(pairs, sems)
        x = rows_ref[...]
        row_sq = half_sq_column(x)
        total = jnp.zeros(out_ref.shape, F32)
        for b in range(nb):
            made[2 * b].wait()
            made[2 * b + 1].wait()
            if first:
                stats_ref[b, 0:1] = half_sq_row(pos[b])
                stats_ref[b, 1:2] = rate_row(side[b], n, in_width)
            cross = lax.dot_general(x, pos[b], NT, preferred_element_type=F32)
            power = (row_sq + stats_ref[b, 0:1] - cross) * stats_ref[b, 1:2]
            kernel = jnp.exp2(power).astype(BF16)
            total += jnp.dot(kernel, side[b, :n], preferred_element_type=F32)
        out_ref[...] = total

    part = jax.ShapeDtypeStruct((rows.shape[0], out_width), F32)
    stat = jax.ShapeDtypeStruct((nb, 8, n), F32)
    work = rows.shape[0] * nb * n
    return pl.pallas_call(
        body,
        out_shape=(part, stat) if first else part,
        in_specs=[VMEM] + [ANY] * (2 * nb) + ([] if first else [VMEM]),
        out_specs=(VMEM, VMEM) if first else VMEM,
        scratch_shapes=[
            pltpu.VMEM((nb, n, in_width), BF16),
            pltpu.VMEM((nb,) + sides[0].shape, BF16),
            pltpu.SemaphoreType.DMA((2 * nb,)),
        ],
        compiler_params=pltpu.CompilerParams(vmem_limit_bytes=24 << 20),
        cost_estimate=pl.CostEstimate(
            flops=2 * work * (in_width + out_width), bytes_accessed=3 << 20, transcendentals=work
        ),
        name="forward",
    )(rows, *blocks, *sides, *([] if first else [stats]))


def own_kernel(center_pos, side, local, far):
    n, in_width = center_pos.shape
    near_rows, far_rows = local.shape[0], far.shape[0]

    def body(pos_ref, side_ref, local_ref, far_ref, out_ref):
        pos = pos_ref[...]
        center_sq = half_sq_column(pos)
        rate = jnp.broadcast_to(rate_row(side_ref[...], n, in_width), (128, n)).T[:, :1]
        step = near_rows
        for start in range(0, near_rows + far_rows, step):
            x = local_ref[...] if start == 0 else far_ref[start - near_rows : start - near_rows + step]
            cross = lax.dot_general(pos, x, NT, preferred_element_type=F32)
            power = (center_sq + half_sq_row(x) - cross) * rate
            out_ref[:, start : start + step] = jnp.exp2(power).astype(BF16)

    work = n * (near_rows + far_rows)
    return pl.pallas_call(
        body,
        out_shape=jax.ShapeDtypeStruct((n, near_rows + far_rows), BF16),
        in_specs=[VMEM] * 4,
        out_specs=VMEM,
        compiler_params=pltpu.CompilerParams(vmem_limit_bytes=24 << 20),
        cost_estimate=pl.CostEstimate(
            flops=2 * work * in_width, bytes_accessed=3 << 20, transcendentals=work
        ),
        name="own_kernel",
    )(center_pos, side, local, far)


def backward(center_pos, side, locals_, fars, kernels, cots, before=None, last=False):
    n, in_width = center_pos.shape
    out_width = side.shape[1]
    groups, near_rows, points = len(kernels), locals_[0].shape[0], kernels[0].shape[1]

    def body(*refs):
        refs = list(refs)
        pos_ref, side_ref = refs[:2]
        del refs[:2]
        local_refs, far_refs, kernel_refs, cot_refs = (
            refs[k * groups : (k + 1) * groups] for k in range(4)
        )
        del refs[: 4 * groups]
        before_refs = None
        if before is not None:
            before_refs = refs[:3]
            del refs[:3]
        moment_ref, coef_ref = refs[:2]
        del refs[:2]
        if not last:
            total_ref = refs.pop(0)
        x, kernel, cot, sems = refs
        pairs = []
        for g in range(groups):
            pairs += [
                (cot_refs[g], cot.at[g]),
                (kernel_refs[g], kernel.at[g]),
                (local_refs[g], x.at[g, :near_rows]),
                (far_refs[g], x.at[g, near_rows:]),
            ]
        made = copies(pairs, sems)
        coef = side_ref[:n]
        ones = jnp.ones((points, 128), BF16)
        if before_refs is None:
            moment, grad_coef, total = 0.0, 0.0, 0.0
        else:
            moment, grad_coef, total = (ref[...] for ref in before_refs)
        for g in range(groups):
            for copy in made[4 * g : 4 * g + 4]:
                copy.wait()
            mixing = lax.dot_general(coef, cot[g], NT, preferred_element_type=F32)
            weights = (kernel[g].astype(F32) * mixing).astype(BF16)
            grad_coef += jnp.dot(kernel[g], cot[g], preferred_element_type=F32)
            total += jnp.dot(weights, ones, preferred_element_type=F32)
            moment += jnp.dot(weights, x[g], preferred_element_type=F32)
        coef_ref[...] = grad_coef
        if last:
            rate = jnp.broadcast_to(rate_row(side_ref[...], n, 2.0 * LOG2E), (128, n)).T
            scale = rate * (-2.0 / in_width)
            for k in range(0, in_width, 128):
                pos = pos_ref[:, k : k + 128].astype(F32)
                moment_ref[:, k : k + 128] = scale * (moment[:, k : k + 128] - total * pos)
        else:
            moment_ref[...] = moment
            total_ref[...] = total

    shapes = [
        jax.ShapeDtypeStruct((n, in_width), F32),
        jax.ShapeDtypeStruct((n, out_width), F32),
        jax.ShapeDtypeStruct((n, 128), F32),
    ]
    outs = 2 if last else 3
    work = n * points * groups
    return pl.pallas_call(
        body,
        out_shape=tuple(shapes[:outs]),
        in_specs=[VMEM] * 2 + [ANY] * (4 * groups) + ([] if before is None else [VMEM] * 3),
        out_specs=(VMEM,) * outs,
        scratch_shapes=[
            pltpu.VMEM((groups, points, in_width), BF16),
            pltpu.VMEM((groups, n, points), BF16),
            pltpu.VMEM((groups, points, out_width), BF16),
            pltpu.SemaphoreType.DMA((4 * groups,)),
        ],
        compiler_params=pltpu.CompilerParams(vmem_limit_bytes=40 << 20),
        cost_estimate=pl.CostEstimate(
            flops=2 * work * (in_width + 2 * out_width + 128), bytes_accessed=6 << 20, transcendentals=0
        ),
        name="backward",
    )(center_pos, side, *locals_, *fars, *kernels, *cots, *([] if before is None else before))


def solution(mesh):
    nz, nc = mesh.shape["points"], mesh.shape["centers"]

    def per_device(train_points, saved_preds, targets, huber_delta, center_pos, coefficients, spread):
        n_rows = train_points.shape[0]
        own_centers = coefficients.shape[0]
        piece = n_rows // nc
        c = lax.axis_index("centers")

        def row_piece(a, d):
            return lax.dynamic_slice_in_dim(a, (c ^ d) * piece, piece)

        own = row_piece(train_points, 0)
        layer = {dz: swap(own, "points", nz, dz) for dz in range(1, nz)}

        spread_rows = own_centers // 128
        side = jnp.concatenate(
            [coefficients, jnp.pad(spread.reshape(spread_rows, 128), ((0, 16 - spread_rows), (0, 0)))]
        )
        pos, sides = {0: center_pos}, {0: side}
        for d in range(2, nc, 2):
            pos[d], sides[d] = swap(center_pos, "centers", nc, d), swap(side, "centers", nc, d)
        for d in range(0, nc, 2):
            pos[d + 1], sides[d + 1] = swap(pos[d], "centers", nc, 1), swap(sides[d], "centers", nc, 1)
        blocks, sides = [pos[d] for d in range(nc)], [sides[d] for d in range(nc)]

        pred, stats = forward(own, blocks, sides)
        for dz in range(1, nz):
            pred = pred + swap(forward(layer[dz], blocks, sides, stats), "points", nz, dz)
        residual = pred + row_piece(saved_preds, 0) - row_piece(targets, 0)
        cot = (residual / jnp.sqrt(1.0 + jnp.square(residual / huber_delta[None, :]))).astype(BF16)

        local = {d: own if d == 0 else row_piece(train_points, d) for d in range(nc)}
        far = {0: jnp.concatenate([layer[dz] for dz in range(1, nz)])}
        cots = {0: jnp.concatenate([cot] + [swap(cot, "points", nz, dz) for dz in range(1, nz)])}
        for d in range(2, nc, 2):
            far[d], cots[d] = swap(far[0], "centers", nc, d), swap(cots[0], "centers", nc, d)
        for d in range(0, nc, 2):
            far[d + 1], cots[d + 1] = swap(far[d], "centers", nc, 1), swap(cots[d], "centers", nc, 1)

        kernels = {d: own_kernel(center_pos, side, local[d], far[d]) for d in range(nc)}
        sums = None
        for d in range(0, nc, 2):
            near = [d, d + 1]
            sums = backward(
                center_pos,
                side,
                *([group[k] for k in near] for group in (local, far, kernels, cots)),
                before=sums,
                last=d + 2 == nc,
            )
        return sums

    return jax.shard_map(
        per_device,
        mesh=mesh,
        in_specs=(
            P(("groups", "points"), None),
            P(("groups", "points"), None),
            P(("groups", "points"), None),
            P("groups"),
            P(("groups", "points", "centers"), None),
            P(("groups", "points", "centers"), None),
            P(("groups", "points", "centers")),
        ),
        out_specs=(
            P(("groups", "points", "centers"), None),
            P(("groups", "points", "centers"), None),
        ),
        check_vma=False,
    )
```

```python
import math

import jax
import jax.numpy as jnp
from jax import lax
from jax.experimental import pallas as pl
from jax.experimental.pallas import tpu as pltpu
from jax.sharding import PartitionSpec as P

F32, BF16 = jnp.float32, jnp.bfloat16
HBM = pl.BlockSpec(memory_space=pltpu.HBM)
VMEM = pl.BlockSpec(memory_space=pltpu.VMEM)
NT = (((1,), (1,)), ((), ()))
LOG2E = math.log2(math.e)


def swap(a, axis, size, d):
    return lax.ppermute(a, axis, [(i, i ^ d) for i in range(size)])


def lane_groups(a):
    total = None
    for k in range(0, a.shape[1], 128):
        part = jnp.square(a[:, k : k + 128].astype(F32))
        total = part if total is None else total + part
    return total


def half_sq_row(a):
    return 0.5 * jnp.sum(lane_groups(a).T, axis=0, keepdims=True)


def half_sq_column(a):
    return 0.5 * jnp.sum(lane_groups(a), axis=1, keepdims=True)


def column(row):
    return jnp.broadcast_to(row, (128, row.shape[1])).T


def params(mib):
    return pltpu.CompilerParams(vmem_limit_bytes=mib << 20)


def pack(train_points, center_pos, coefficients, spread, piece):
    n, in_width = center_pos.shape
    out_width = coefficients.shape[1]
    across = in_width // out_width
    q = n // across

    def body(points_ref, pos_ref, coef_ref, spread_ref, own_ref, out_ref, sem):
        start = pl.multiple_of(lax.axis_index("centers") * piece, piece)
        copy = pltpu.make_async_copy(points_ref.at[pl.ds(start, piece)], own_ref, sem)
        copy.start()
        pos = pos_ref[...]
        out_ref[:n] = pos
        for k in range(across):
            out_ref[n : n + q, k * out_width : (k + 1) * out_width] = coef_ref[k * q : (k + 1) * q]
        half = half_sq_row(pos)
        high = half.astype(BF16)
        rest = half - high.astype(F32)
        middle = rest.astype(BF16)
        low = (rest - middle.astype(F32)).astype(BF16)
        rows = [r.astype(F32) for r in (spread_ref[...], high, middle, low)]
        tail = jnp.concatenate(rows + [jnp.zeros((12, n), F32)]).astype(BF16)
        if n < in_width:
            tail = jnp.concatenate([tail, jnp.zeros((16, in_width - n), BF16)], axis=1)
        out_ref[n + q :] = tail
        copy.wait()

    return pl.pallas_call(
        body,
        out_shape=(
            jax.ShapeDtypeStruct((piece, in_width), BF16),
            jax.ShapeDtypeStruct((n + q + 16, in_width), BF16),
        ),
        in_specs=[HBM, VMEM, VMEM, VMEM],
        out_specs=(VMEM, VMEM),
        scratch_shapes=[pltpu.SemaphoreType.DMA],
        compiler_params=params(16),
        cost_estimate=pl.CostEstimate(flops=1 << 20, bytes_accessed=2 << 20, transcendentals=0),
        name="pack",
    )(train_points, center_pos, coefficients, spread.reshape(1, n))


def take(arrays, offsets, piece):
    def body(*refs):
        ins, outs, sems = refs[: len(arrays)], refs[len(arrays) : -1], refs[-1]
        made = []
        for k, d in enumerate(offsets):
            start = pl.multiple_of((lax.axis_index("centers") ^ d) * piece, piece)
            made.append(pltpu.make_async_copy(ins[k].at[pl.ds(start, piece)], outs[k], sems.at[k]))
            made[-1].start()
        for copy in made:
            copy.wait()

    return pl.pallas_call(
        body,
        out_shape=tuple(jax.ShapeDtypeStruct((piece, a.shape[1]), a.dtype) for a in arrays),
        in_specs=[HBM] * len(arrays),
        out_specs=(VMEM,) * len(arrays),
        scratch_shapes=[pltpu.SemaphoreType.DMA((len(arrays),))],
        compiler_params=params(16),
        cost_estimate=pl.CostEstimate(flops=0, bytes_accessed=2 << 20, transcendentals=0),
        name="take",
    )(*arrays)


def forward(rows, payloads, n, out_width):
    in_width = rows.shape[1]
    q = n * out_width // in_width

    def body(rows_ref, *refs):
        out_ref = refs[-1]
        x = rows_ref[...]
        row_sq = half_sq_column(x)
        total = jnp.zeros(out_ref.shape, F32)
        for ref in refs[:-1]:
            packed = ref[n : n + q]
            coef = jnp.concatenate(
                [packed[:, k : k + out_width] for k in range(0, in_width, out_width)]
            )
            tail = ref[n + q :, :n].astype(F32)
            center_sq = tail[1:2] + tail[2:3] + tail[3:4]
            rate = tail[0:1] * (-2.0 * LOG2E / in_width)
            cross = lax.dot_general(x, ref[:n], NT, preferred_element_type=F32)
            power = (row_sq + center_sq - cross) * rate
            kernel = jnp.exp2(power).astype(BF16)
            total += jnp.dot(kernel, coef, preferred_element_type=F32)
        out_ref[...] = total

    work = rows.shape[0] * len(payloads) * n
    return pl.pallas_call(
        body,
        out_shape=jax.ShapeDtypeStruct((rows.shape[0], out_width), F32),
        in_specs=[VMEM] * (1 + len(payloads)),
        out_specs=VMEM,
        compiler_params=params(16),
        cost_estimate=pl.CostEstimate(
            flops=2 * work * (in_width + out_width), bytes_accessed=3 << 20, transcendentals=work
        ),
        name="forward",
    )(rows, *payloads)


def own_kernel(center_pos, spread, blocks):
    n, in_width = center_pos.shape
    points = sum(b.shape[0] for b in blocks)

    def body(pos_ref, spread_ref, *refs):
        out_ref = refs[-1]
        pos = pos_ref[...]
        center_sq = half_sq_column(pos)
        rate = column(spread_ref[...].astype(F32) * (-2.0 * LOG2E / in_width))[:, :1]
        at = 0
        for ref in refs[:-1]:
            step = min(256, ref.shape[0])
            for start in range(0, ref.shape[0], step):
                x = ref[start : start + step]
                cross = lax.dot_general(pos, x, NT, preferred_element_type=F32)
                power = (center_sq + half_sq_row(x) - cross) * rate
                out_ref[:, at : at + step] = jnp.exp2(power).astype(BF16)
                at += step

    work = n * points
    return pl.pallas_call(
        body,
        out_shape=jax.ShapeDtypeStruct((n, points), BF16),
        in_specs=[VMEM] * (2 + len(blocks)),
        out_specs=VMEM,
        compiler_params=params(16),
        cost_estimate=pl.CostEstimate(
            flops=2 * work * in_width, bytes_accessed=3 << 20, transcendentals=work
        ),
        name="own_kernel",
    )(center_pos, spread.reshape(1, n), *blocks)


def cotangent(parts, saved, target, delta):
    def body(*refs):
        saved_ref, target_ref, delta_ref, out_ref = refs[-4:]
        pred = refs[0][...]
        for ref in refs[1:-4]:
            pred += ref[...]
        residual = pred + saved_ref[...] - target_ref[...]
        ratio = residual / delta_ref[...]
        out_ref[...] = (residual / jnp.sqrt(1.0 + ratio * ratio)).astype(BF16)

    return pl.pallas_call(
        body,
        out_shape=jax.ShapeDtypeStruct(saved.shape, BF16),
        in_specs=[VMEM] * (len(parts) + 3),
        out_specs=VMEM,
        compiler_params=params(16),
        cost_estimate=pl.CostEstimate(flops=1 << 18, bytes_accessed=1 << 20, transcendentals=1 << 16),
        name="cotangent",
    )(*parts, saved, target, delta.reshape(1, -1))


def backward(center_pos, coefficients, spread, groups, before=None, last=False):
    n, in_width = center_pos.shape
    out_width = coefficients.shape[1]
    flat = []
    for kernel, xs, cots in groups:
        flat += [kernel, *xs, *cots]
    carried = [] if before is None else list(before)
    outs = 2 if last else 3
    points = sum(kernel.shape[1] for kernel, _, _ in groups)

    def body(pos_ref, coef_in, spread_ref, *refs):
        refs, out_refs = list(refs[:-outs]), refs[-outs:]
        coef = coef_in[...]
        moment = grad_coef = total = 0.0
        if carried:
            moment, grad_coef, total = (ref[...] for ref in refs[-3:])
        for _, xs, cots in groups:
            kernel_ref = refs.pop(0)
            x_refs = [refs.pop(0) for _ in xs]
            cot_refs = [refs.pop(0) for _ in cots]
            cot = jnp.concatenate([ref[...] for ref in cot_refs])
            kernel = kernel_ref[...]
            mixing = lax.dot_general(coef, cot, NT, preferred_element_type=F32)
            weights = (kernel.astype(F32) * mixing).astype(BF16)
            ones = jnp.ones((kernel.shape[1], 128), BF16)
            grad_coef += jnp.dot(kernel, cot, preferred_element_type=F32)
            total += jnp.dot(weights, ones, preferred_element_type=F32)
            x = jnp.concatenate([ref[...] for ref in x_refs])
            moment += jnp.dot(weights, x, preferred_element_type=F32)
        out_refs[1][...] = grad_coef
        if last:
            scale = column(spread_ref[...].astype(F32)) * (2.0 / in_width)
            for k in range(0, in_width, 128):
                pos = pos_ref[:, k : k + 128].astype(F32)
                out_refs[0][:, k : k + 128] = scale * (moment[:, k : k + 128] - total * pos)
        else:
            out_refs[0][...] = moment
            out_refs[2][...] = total

    shapes = [
        jax.ShapeDtypeStruct((n, in_width), F32),
        jax.ShapeDtypeStruct((n, out_width), F32),
        jax.ShapeDtypeStruct((n, 128), F32),
    ]
    work = n * points
    return pl.pallas_call(
        body,
        out_shape=tuple(shapes[:outs]),
        in_specs=[VMEM] * (3 + len(flat) + len(carried)),
        out_specs=(VMEM,) * outs,
        compiler_params=params(24),
        cost_estimate=pl.CostEstimate(
            flops=2 * work * (in_width + 2 * out_width + 128), bytes_accessed=6 << 20, transcendentals=0
        ),
        name="backward",
    )(center_pos, coefficients, spread.reshape(1, n), *flat, *carried)


def solution(mesh):
    nz, nc = mesh.shape["points"], mesh.shape["centers"]

    def per_device(train_points, saved_preds, targets, huber_delta, center_pos, coefficients, spread):
        n_rows = train_points.shape[0]
        n, out_width = coefficients.shape
        piece = n_rows // nc

        own, payload = pack(train_points, center_pos, coefficients, spread, piece)

        layer = {0: own}
        for dz in range(2, nz, 2):
            layer[dz] = swap(own, "points", nz, dz)
        for dz in range(1, nz, 2):
            layer[dz] = swap(layer[dz - 1], "points", nz, 1)

        payloads = {0: payload}
        for d in range(2, nc, 2):
            payloads[d] = swap(payload, "centers", nc, d)
        for d in range(0, nc, 2):
            payloads[d + 1] = swap(payloads[d], "centers", nc, 1)
        payloads = [payloads[d] for d in range(nc)]

        saved, target, *local = take(
            [saved_preds, targets] + [train_points] * (nc - 1), [0, 0, *range(1, nc)], piece
        )
        local = [own, *local]

        parts = [forward(layer[dz], payloads, n, out_width) for dz in range(nz)]
        parts = [parts[0]] + [swap(parts[dz], "points", nz, dz) for dz in range(1, nz)]
        cot = cotangent(parts, saved, target, huber_delta)

        far = {0: jnp.concatenate([layer[dz] for dz in range(1, nz)])}
        cots = {0: jnp.concatenate([cot] + [swap(cot, "points", nz, dz) for dz in range(1, nz)])}
        for d in range(2, nc, 2):
            far[d], cots[d] = swap(far[0], "centers", nc, d), swap(cots[0], "centers", nc, d)
        for d in range(0, nc, 2):
            far[d + 1], cots[d + 1] = swap(far[d], "centers", nc, 1), swap(cots[d], "centers", nc, 1)

        kernels = {d: own_kernel(center_pos, spread, [local[d], far[d]]) for d in range(nc)}
        sums = None
        for d in range(0, nc, 2):
            groups = [(kernels[k], [local[k], far[k]], [cots[k]]) for k in (d, d + 1)]
            sums = backward(center_pos, coefficients, spread, groups, before=sums, last=d + 2 == nc)
        return sums

    return jax.shard_map(
        per_device,
        mesh=mesh,
        in_specs=(
            P(("groups", "points"), None),
            P(("groups", "points"), None),
            P(("groups", "points"), None),
            P("groups"),
            P(("groups", "points", "centers"), None),
            P(("groups", "points", "centers"), None),
            P(("groups", "points", "centers")),
        ),
        out_specs=(
            P(("groups", "points", "centers"), None),
            P(("groups", "points", "centers"), None),
        ),
        check_vma=False,
    )
```

```python
import math

import jax
import jax.numpy as jnp
from jax import lax
from jax.experimental import pallas as pl
from jax.experimental.pallas import tpu as pltpu
from jax.sharding import PartitionSpec as P

F32, BF16 = jnp.float32, jnp.bfloat16
HBM = pl.BlockSpec(memory_space=pltpu.HBM)
VMEM = pl.BlockSpec(memory_space=pltpu.VMEM)
NT = (((1,), (1,)), ((), ()))
LOG2E = math.log2(math.e)
COVER = 8
BRIEF = pl.CostEstimate(flops=1, bytes_accessed=1, transcendentals=0)


def swap(a, axis, size, d):
    return lax.ppermute(a, axis, [(i, i ^ d) for i in range(size)])


def after(a, *others):
    return lax.optimization_barrier((a, *others))[0]


def lane_groups(a):
    total = None
    for k in range(0, a.shape[1], 128):
        part = jnp.square(a[:, k : k + 128].astype(F32))
        total = part if total is None else total + part
    return total


def half_sq_row(a):
    return 0.5 * jnp.sum(lane_groups(a).T, axis=0, keepdims=True)


def half_sq_column(a):
    return 0.5 * jnp.sum(lane_groups(a), axis=1, keepdims=True)


def column(row):
    return jnp.broadcast_to(row, (128, row.shape[1])).T


def params(mib):
    return pltpu.CompilerParams(vmem_limit_bytes=mib << 20)


def pack(train_points, center_pos, coefficients, spread, piece):
    n, in_width = center_pos.shape
    out_width = coefficients.shape[1]
    across = in_width // out_width
    q = n // across

    def body(points_ref, pos_in, coef_in, spread_ref, own_ref, out_ref, coef_ref, sems):
        start = pl.multiple_of(lax.axis_index("centers") * piece, piece)
        pairs = [
            (pos_in, out_ref.at[:n]),
            (coef_in, coef_ref),
            (points_ref.at[pl.ds(start, piece)], own_ref),
        ]
        made = [pltpu.make_async_copy(*pair, sems.at[k]) for k, pair in enumerate(pairs)]
        for copy in made:
            copy.start()
        for copy in made:
            copy.wait()
        pos = out_ref[:n]
        for k in range(across):
            out_ref[n : n + q, k * out_width : (k + 1) * out_width] = coef_ref[k * q : (k + 1) * q]
        half = half_sq_row(pos)
        high = half.astype(BF16)
        rest = half - high.astype(F32)
        middle = rest.astype(BF16)
        low = (rest - middle.astype(F32)).astype(BF16)
        rows = [r.astype(F32) for r in (spread_ref[...], high, middle, low)]
        tail = jnp.concatenate(rows + [jnp.zeros((12, n), F32)]).astype(BF16)
        if n < in_width:
            tail = jnp.concatenate([tail, jnp.zeros((16, in_width - n), BF16)], axis=1)
        out_ref[n + q :] = tail

    return pl.pallas_call(
        body,
        out_shape=(
            jax.ShapeDtypeStruct((piece, in_width), BF16),
            jax.ShapeDtypeStruct((n + q + 16, in_width), BF16),
        ),
        in_specs=[HBM, HBM, HBM, VMEM],
        out_specs=(VMEM, VMEM),
        scratch_shapes=[pltpu.VMEM((n, out_width), BF16), pltpu.SemaphoreType.DMA((3,))],
        compiler_params=params(62),
        cost_estimate=BRIEF,
        name="pack",
    )(train_points, center_pos, coefficients, spread.reshape(1, n))


def take(arrays, offsets, piece, row):
    def body(*refs):
        row_ref, ins, outs, sems = refs[0], refs[1 : len(arrays) + 1], refs[len(arrays) + 1 : -1], refs[-1]
        made = []
        for k, d in enumerate(offsets):
            start = pl.multiple_of((lax.axis_index("centers") ^ d) * piece, piece)
            made.append(pltpu.make_async_copy(ins[k].at[pl.ds(start, piece)], outs[k], sems.at[k]))
            made[-1].start()
        outs[-1][...] = row_ref[...]
        for copy in made:
            copy.wait()

    return pl.pallas_call(
        body,
        out_shape=tuple(jax.ShapeDtypeStruct((piece, a.shape[1]), a.dtype) for a in arrays)
        + (jax.ShapeDtypeStruct((1, row.shape[0]), row.dtype),),
        in_specs=[VMEM] + [HBM] * len(arrays),
        out_specs=(VMEM,) * (len(arrays) + 1),
        scratch_shapes=[pltpu.SemaphoreType.DMA((len(arrays),))],
        compiler_params=params(16),
        cost_estimate=BRIEF,
        name="take",
    )(row.reshape(1, -1), *arrays)


def forward(rows, payloads, n, out_width, before=()):
    in_width = rows.shape[1]
    q = n * out_width // in_width

    def body(rows_ref, *refs):
        out_ref = refs[-1]
        x = rows_ref[...]
        row_sq = half_sq_column(x)
        total = jnp.zeros(out_ref.shape, F32)
        for ref in refs[len(payloads) : -1]:
            total += ref[...]
        for ref in refs[: len(payloads)]:
            packed = ref[n : n + q]
            coef = jnp.concatenate(
                [packed[:, k : k + out_width] for k in range(0, in_width, out_width)]
            )
            tail = ref[n + q :, :n].astype(F32)
            center_sq = tail[1:2] + tail[2:3] + tail[3:4]
            rate = tail[0:1] * (-2.0 * LOG2E / in_width)
            cross = lax.dot_general(x, ref[:n], NT, preferred_element_type=F32)
            power = (row_sq + center_sq - cross) * rate
            kernel = jnp.exp2(power).astype(BF16)
            total += jnp.dot(kernel, coef, preferred_element_type=F32)
        out_ref[...] = total

    work = rows.shape[0] * len(payloads) * n
    return pl.pallas_call(
        body,
        out_shape=jax.ShapeDtypeStruct((rows.shape[0], out_width), F32),
        in_specs=[VMEM] * (1 + len(payloads) + len(before)),
        out_specs=VMEM,
        compiler_params=params(16),
        cost_estimate=pl.CostEstimate(
            flops=COVER * 2 * work * (in_width + out_width), bytes_accessed=3 << 20, transcendentals=work
        ),
        name="forward",
    )(rows, *payloads, *before)


def own_kernel(center_pos, spread, blocks):
    n, in_width = center_pos.shape
    points = sum(b.shape[0] for b in blocks)

    def body(pos_ref, spread_ref, *refs):
        out_ref = refs[-1]
        pos = pos_ref[...]
        center_sq = half_sq_column(pos)
        rate = column(spread_ref[...].astype(F32) * (-2.0 * LOG2E / in_width))[:, :1]
        at = 0
        for ref in refs[:-1]:
            step = min(256, ref.shape[0])
            for start in range(0, ref.shape[0], step):
                x = ref[start : start + step]
                cross = lax.dot_general(pos, x, NT, preferred_element_type=F32)
                power = (center_sq + half_sq_row(x) - cross) * rate
                out_ref[:, at : at + step] = jnp.exp2(power).astype(BF16)
                at += step

    return pl.pallas_call(
        body,
        out_shape=jax.ShapeDtypeStruct((n, points), BF16),
        in_specs=[VMEM] * (2 + len(blocks)),
        out_specs=VMEM,
        compiler_params=params(16),
        cost_estimate=BRIEF,
        name="own_kernel",
    )(center_pos, spread.reshape(1, n), *blocks)


def cotangent(parts, saved, target, delta):
    def body(*refs):
        saved_ref, target_ref, delta_ref, out_ref = refs[-4:]
        pred = refs[0][...]
        for ref in refs[1:-4]:
            pred += ref[...]
        residual = pred + saved_ref[...] - target_ref[...]
        ratio = residual / delta_ref[...]
        out_ref[...] = (residual / jnp.sqrt(1.0 + ratio * ratio)).astype(BF16)

    return pl.pallas_call(
        body,
        out_shape=jax.ShapeDtypeStruct(saved.shape, BF16),
        in_specs=[VMEM] * (len(parts) + 3),
        out_specs=VMEM,
        compiler_params=params(16),
        cost_estimate=BRIEF,
        name="cotangent",
    )(*parts, saved, target, delta)


def backward(center_pos, coefficients, spread, groups, before=None, last=False):
    n, in_width = center_pos.shape
    out_width = coefficients.shape[1]
    flat = []
    for kernel, xs, cots in groups:
        flat += [kernel, *xs, *cots]
    carried = [] if before is None else list(before)
    outs = 2 if last else 3
    points = sum(kernel.shape[1] for kernel, _, _ in groups)

    def body(pos_ref, coef_in, spread_ref, *refs):
        refs, out_refs = list(refs[:-outs]), refs[-outs:]
        coef = coef_in[...]
        moment = grad_coef = total = 0.0
        if carried:
            moment, grad_coef, total = (ref[...] for ref in refs[-3:])
        for _, xs, cots in groups:
            kernel_ref = refs.pop(0)
            x_refs = [refs.pop(0) for _ in xs]
            cot_refs = [refs.pop(0) for _ in cots]
            cot = jnp.concatenate([ref[...] for ref in cot_refs])
            kernel = kernel_ref[...]
            mixing = lax.dot_general(coef, cot, NT, preferred_element_type=F32)
            weights = (kernel.astype(F32) * mixing).astype(BF16)
            ones = jnp.ones((kernel.shape[1], 128), BF16)
            grad_coef += jnp.dot(kernel, cot, preferred_element_type=F32)
            total += jnp.dot(weights, ones, preferred_element_type=F32)
            x = jnp.concatenate([ref[...] for ref in x_refs])
            moment += jnp.dot(weights, x, preferred_element_type=F32)
        out_refs[1][...] = grad_coef
        if last:
            scale = column(spread_ref[...].astype(F32)) * (2.0 / in_width)
            for k in range(0, in_width, 128):
                pos = pos_ref[:, k : k + 128].astype(F32)
                out_refs[0][:, k : k + 128] = scale * (moment[:, k : k + 128] - total * pos)
        else:
            out_refs[0][...] = moment
            out_refs[2][...] = total

    shapes = [
        jax.ShapeDtypeStruct((n, in_width), F32),
        jax.ShapeDtypeStruct((n, out_width), F32),
        jax.ShapeDtypeStruct((n, 128), F32),
    ]
    return pl.pallas_call(
        body,
        out_shape=tuple(shapes[:outs]),
        in_specs=[VMEM] * (3 + len(flat) + len(carried)),
        out_specs=(VMEM,) * outs,
        compiler_params=params(24),
        cost_estimate=BRIEF,
        name="backward",
    )(center_pos, coefficients, spread.reshape(1, n), *flat, *carried)


def solution(mesh):
    nz, nc = mesh.shape["points"], mesh.shape["centers"]

    def per_device(train_points, saved_preds, targets, huber_delta, center_pos, coefficients, spread):
        n_rows = train_points.shape[0]
        n, out_width = coefficients.shape
        piece = n_rows // nc

        own, payload = pack(train_points, center_pos, coefficients, spread, piece)

        layer = {0: own}
        for dz in range(2, nz, 2):
            layer[dz] = swap(own, "points", nz, dz)
        layer[1] = swap(own, "points", nz, 1)

        payloads = {0: payload}
        for d in range(2, nc, 2):
            payloads[d] = swap(payload, "centers", nc, d)
        payloads[1] = swap(payload, "centers", nc, 1)
        near = [payloads[0], payloads[1]]
        parts = {dz: forward(layer[dz], near, n, out_width) for dz in (*range(2, nz, 2), 1)}
        for dz in range(3, nz, 2):
            layer[dz] = swap(layer[dz - 1], "points", nz, 1)
        for d in range(2, nc, 2):
            payloads[d + 1] = swap(after(payloads[d], layer[2]), "centers", nc, 1)
        rest = [payloads[d] for d in range(2, nc)]

        saved, target, *local, delta = take(
            [saved_preds, targets] + [train_points] * (nc - 1), [0, 0, *range(1, nc)], piece, huber_delta
        )
        local = [own, *local]

        received = {}
        for dz in range(2, nz, 2):
            parts[dz] = forward(layer[dz], rest, n, out_width, [parts[dz]])
            received[dz] = swap(parts[dz], "points", nz, dz)
        for dz in range(3, nz, 2):
            parts[dz] = forward(after(layer[dz], parts[dz - 1]), near + rest, n, out_width)
            received[dz] = swap(parts[dz], "points", nz, dz)
        parts[1] = forward(layer[1], rest, n, out_width, [after(parts[1], parts[nz - 1])])
        received[1] = swap(parts[1], "points", nz, 1)
        soon = [received.pop(dz) for dz in range(2, nz, 2)]
        parts[0] = forward(after(own, parts[1]), near + rest, n, out_width, soon)

        early = {0: jnp.concatenate([layer[dz] for dz in range(1, nz - 1)])}
        late = {0: after(layer[nz - 1], parts[0])}
        for d in range(2, nc, 2):
            early[d] = swap(after(early[0], payloads[d]), "centers", nc, d)
            late[d] = swap(late[0], "centers", nc, d)
        early[1] = swap(after(early[0], payloads[nc - 1]), "centers", nc, 1)
        late[1] = swap(late[0], "centers", nc, 1)
        kernels = {d: own_kernel(center_pos, spread, [local[d], early[d], late[d]]) for d in (0, 1)}

        cot = cotangent([parts[0], *received.values()], saved, target, delta)

        for d in range(2, nc, 2):
            early[d + 1] = swap(after(early[d], cot), "centers", nc, 1)
            late[d + 1] = swap(after(late[d], cot), "centers", nc, 1)
            for k in (d, d + 1):
                kernels[k] = own_kernel(center_pos, spread, [local[k], early[k], late[k]])

        cots = {0: [cot] + [swap(cot, "points", nz, dz) for dz in range(1, nz)]}
        for d in range(2, nc, 2):
            held = after(cots[0][2], kernels[0], kernels[1])
            cots[d] = [swap(a, "centers", nc, d) for a in (*cots[0][:2], held, *cots[0][3:])]
        for d in range(0, nc, 2):
            cots[d + 1] = [swap(jnp.concatenate(cots[d]), "centers", nc, 1)]

        def group(d):
            return (kernels[d], [local[d], early[d], late[d]], cots[d])

        kernels[0] = after(kernels[0], *(kernels[d] for d in range(1, nc)))
        sums = backward(center_pos, coefficients, spread, [group(0), group(1)])
        for d in range(2, nc):
            sums = backward(center_pos, coefficients, spread, [group(d)], before=sums, last=d + 1 == nc)
        return sums

    return jax.shard_map(
        per_device,
        mesh=mesh,
        in_specs=(
            P(("groups", "points"), None),
            P(("groups", "points"), None),
            P(("groups", "points"), None),
            P("groups"),
            P(("groups", "points", "centers"), None),
            P(("groups", "points", "centers"), None),
            P(("groups", "points", "centers")),
        ),
        out_specs=(
            P(("groups", "points", "centers"), None),
            P(("groups", "points", "centers"), None),
        ),
        check_vma=False,
    )
```

```python
import math

import jax
import jax.numpy as jnp
from jax import lax
from jax.experimental import pallas as pl
from jax.experimental.pallas import tpu as pltpu
from jax.sharding import PartitionSpec as P

F32, BF16 = jnp.float32, jnp.bfloat16
HBM = pl.BlockSpec(memory_space=pltpu.HBM)
VMEM = pl.BlockSpec(memory_space=pltpu.VMEM)
NT = (((1,), (1,)), ((), ()))
LOG2E = math.log2(math.e)
COVER = pl.CostEstimate(flops=1 << 34, bytes_accessed=1 << 20, transcendentals=1 << 20)
BRIEF = pl.CostEstimate(flops=1, bytes_accessed=1, transcendentals=0)


def swap(a, axis, size, d):
    return lax.ppermute(a, axis, [(i, i ^ d) for i in range(size)])


def after(a, *others):
    return lax.optimization_barrier((a, *others))[0]


def lane_groups(a):
    total = None
    for k in range(0, a.shape[1], 128):
        part = jnp.square(a[:, k : k + 128].astype(F32))
        total = part if total is None else total + part
    return total


def half_sq_row(a):
    return 0.5 * jnp.sum(lane_groups(a).T, axis=0, keepdims=True)


def half_sq_column(a):
    return 0.5 * jnp.sum(lane_groups(a), axis=1, keepdims=True)


def column(row):
    return jnp.broadcast_to(row, (128, row.shape[1])).T


def params(mib):
    return pltpu.CompilerParams(vmem_limit_bytes=mib << 20)


def pack(train_points, center_pos, coefficients, spread, piece):
    n, in_width = center_pos.shape
    out_width = coefficients.shape[1]
    across = in_width // out_width
    q = n // across

    def body(points_ref, pos_in, coef_in, spread_ref, own_ref, out_ref, coef_ref, sems):
        start = pl.multiple_of(lax.axis_index("centers") * piece, piece)
        pairs = [
            (pos_in, out_ref.at[:n]),
            (coef_in, coef_ref),
            (points_ref.at[pl.ds(start, piece)], own_ref),
        ]
        made = [pltpu.make_async_copy(*pair, sems.at[k]) for k, pair in enumerate(pairs)]
        for copy in made:
            copy.start()
        for copy in made:
            copy.wait()
        pos = out_ref[:n]
        for k in range(across):
            out_ref[n : n + q, k * out_width : (k + 1) * out_width] = coef_ref[k * q : (k + 1) * q]
        half = half_sq_row(pos)
        high = half.astype(BF16)
        rest = half - high.astype(F32)
        middle = rest.astype(BF16)
        low = (rest - middle.astype(F32)).astype(BF16)
        rows = [r.astype(F32) for r in (spread_ref[...], high, middle, low)]
        tail = jnp.concatenate(rows + [jnp.zeros((12, n), F32)]).astype(BF16)
        if n < in_width:
            tail = jnp.concatenate([tail, jnp.zeros((16, in_width - n), BF16)], axis=1)
        out_ref[n + q :] = tail

    return pl.pallas_call(
        body,
        out_shape=(
            jax.ShapeDtypeStruct((piece, in_width), BF16),
            jax.ShapeDtypeStruct((n + q + 16, in_width), BF16),
        ),
        in_specs=[HBM, HBM, HBM, VMEM],
        out_specs=(VMEM, VMEM),
        scratch_shapes=[pltpu.VMEM((n, out_width), BF16), pltpu.SemaphoreType.DMA((3,))],
        compiler_params=params(62),
        cost_estimate=BRIEF,
        name="pack",
    )(train_points, center_pos, coefficients, spread.reshape(1, n))


def take(arrays, offsets, piece, row):
    def body(*refs):
        row_ref, ins, outs, sems = refs[0], refs[1 : len(arrays) + 1], refs[len(arrays) + 1 : -1], refs[-1]
        made = []
        for k, d in enumerate(offsets):
            start = pl.multiple_of((lax.axis_index("centers") ^ d) * piece, piece)
            made.append(pltpu.make_async_copy(ins[k].at[pl.ds(start, piece)], outs[k], sems.at[k]))
            made[-1].start()
        outs[-1][...] = row_ref[...]
        for copy in made:
            copy.wait()

    return pl.pallas_call(
        body,
        out_shape=tuple(jax.ShapeDtypeStruct((piece, a.shape[1]), a.dtype) for a in arrays)
        + (jax.ShapeDtypeStruct((1, row.shape[0]), row.dtype),),
        in_specs=[VMEM] + [HBM] * len(arrays),
        out_specs=(VMEM,) * (len(arrays) + 1),
        scratch_shapes=[pltpu.SemaphoreType.DMA((len(arrays),))],
        compiler_params=params(16),
        cost_estimate=BRIEF,
        name="take",
    )(row.reshape(1, -1), *arrays)


def partial_pred(x, refs, n, out_width, total):
    in_width = x.shape[1]
    q = n * out_width // in_width
    row_sq = half_sq_column(x)
    for ref in refs:
        packed = ref[n : n + q]
        coef = jnp.concatenate([packed[:, k : k + out_width] for k in range(0, in_width, out_width)])
        tail = ref[n + q :, :n].astype(F32)
        center_sq = tail[1:2] + tail[2:3] + tail[3:4]
        rate = tail[0:1] * (-2.0 * LOG2E / in_width)
        cross = lax.dot_general(x, ref[:n], NT, preferred_element_type=F32)
        power = (row_sq + center_sq - cross) * rate
        kernel = jnp.exp2(power).astype(BF16)
        new = jnp.dot(kernel, coef, preferred_element_type=F32)
        total = new if total is None else total + new
    return total


def own_values(pos_ref, spread_ref, refs, out_ref):
    pos = pos_ref[...]
    center_sq = half_sq_column(pos)
    rate = column(spread_ref[...].astype(F32) * (-2.0 * LOG2E / pos.shape[1]))[:, :1]
    at = 0
    for ref in refs:
        step = min(256, ref.shape[0])
        for start in range(0, ref.shape[0], step):
            x = ref[start : start + step]
            cross = lax.dot_general(pos, x, NT, preferred_element_type=F32)
            power = (center_sq + half_sq_row(x) - cross) * rate
            out_ref[:, at : at + step] = jnp.exp2(power).astype(BF16)
            at += step


def forward(rows, payloads, n, out_width):
    def body(rows_ref, *refs):
        refs[-1][...] = partial_pred(rows_ref[...], refs[:-1], n, out_width, None)

    return pl.pallas_call(
        body,
        out_shape=jax.ShapeDtypeStruct((rows.shape[0], out_width), F32),
        in_specs=[VMEM] * (1 + len(payloads)),
        out_specs=VMEM,
        compiler_params=params(16),
        cost_estimate=COVER,
        name="forward",
    )(rows, *payloads)


def own_kernel(center_pos, spread, blocks):
    n = center_pos.shape[0]
    points = sum(b.shape[0] for b in blocks)

    def body(pos_ref, spread_ref, *refs):
        own_values(pos_ref, spread_ref, refs[:-1], refs[-1])

    return pl.pallas_call(
        body,
        out_shape=jax.ShapeDtypeStruct((n, points), BF16),
        in_specs=[VMEM] * (2 + len(blocks)),
        out_specs=VMEM,
        compiler_params=params(16),
        cost_estimate=BRIEF,
        name="own_kernel",
    )(center_pos, spread.reshape(1, n), *blocks)


def own_rows(rows, payloads, out_width, received, center_pos, spread, blocks):
    n = center_pos.shape[0]
    points = sum(b.shape[0] for b in blocks)
    ends = [1, 1 + len(payloads)]
    ends.append(ends[-1] + len(received))

    def body(*refs):
        total = None
        for ref in refs[ends[1] : ends[2]]:
            total = ref[...] if total is None else total + ref[...]
        refs[-2][...] = partial_pred(refs[0][...], refs[1 : ends[1]], n, out_width, total)
        pos_ref, spread_ref, *block_refs = refs[ends[2] : -2]
        own_values(pos_ref, spread_ref, block_refs, refs[-1])

    ins = [rows, *payloads, *received, center_pos, spread.reshape(1, n), *blocks]
    return pl.pallas_call(
        body,
        out_shape=(
            jax.ShapeDtypeStruct((rows.shape[0], out_width), F32),
            jax.ShapeDtypeStruct((n, points), BF16),
        ),
        in_specs=[VMEM] * len(ins),
        out_specs=(VMEM, VMEM),
        compiler_params=params(16),
        cost_estimate=COVER,
        name="own_rows",
    )(*ins)


def cotangent(parts, saved, target, delta):
    def body(*refs):
        saved_ref, target_ref, delta_ref, out_ref = refs[-4:]
        pred = refs[0][...]
        for ref in refs[1:-4]:
            pred += ref[...]
        residual = pred + saved_ref[...] - target_ref[...]
        ratio = residual / delta_ref[...]
        out_ref[...] = (residual / jnp.sqrt(1.0 + ratio * ratio)).astype(BF16)

    return pl.pallas_call(
        body,
        out_shape=jax.ShapeDtypeStruct(saved.shape, BF16),
        in_specs=[VMEM] * (len(parts) + 3),
        out_specs=VMEM,
        compiler_params=params(16),
        cost_estimate=BRIEF,
        name="cotangent",
    )(*parts, saved, target, delta)


def backward(center_pos, coefficients, spread, groups, before=None, last=False):
    n, in_width = center_pos.shape
    out_width = coefficients.shape[1]
    flat = []
    for kernel, xs, cots in groups:
        flat += [kernel, *xs, *cots]
    carried = [] if before is None else list(before)
    outs = 2 if last else 3
    points = sum(kernel.shape[1] for kernel, _, _ in groups)

    def body(pos_ref, coef_in, spread_ref, *refs):
        refs, out_refs = list(refs[:-outs]), refs[-outs:]
        coef = coef_in[...]
        moment = grad_coef = total = None
        if carried:
            moment, grad_coef, total = refs[-3:]

        def plus(old, new):
            return new if old is None else old[...] + new

        for _, xs, cots in groups:
            kernel_ref = refs.pop(0)
            x_refs = [refs.pop(0) for _ in xs]
            cot_refs = [refs.pop(0) for _ in cots]
            cot = jnp.concatenate([ref[...] for ref in cot_refs])
            kernel = kernel_ref[...]
            mixing = lax.dot_general(coef, cot, NT, preferred_element_type=F32)
            weights = (kernel.astype(F32) * mixing).astype(BF16)
            grad_coef = plus(grad_coef, jnp.dot(kernel, cot, preferred_element_type=F32))
            lanes = weights[:, :128].astype(F32)
            for k in range(128, kernel.shape[1], 128):
                lanes += weights[:, k : k + 128].astype(F32)
            total = plus(total, lanes)
            x = jnp.concatenate([ref[...] for ref in x_refs])
            moment = plus(moment, jnp.dot(weights, x, preferred_element_type=F32))
        out_refs[1][...] = grad_coef
        if last:
            scale = column(spread_ref[...].astype(F32)) * (2.0 / in_width)
            total = jnp.sum(total, axis=1, keepdims=True)
            for k in range(0, in_width, 128):
                pos = pos_ref[:, k : k + 128].astype(F32)
                out_refs[0][:, k : k + 128] = scale * (moment[:, k : k + 128] - total * pos)
        else:
            out_refs[0][...] = moment
            out_refs[2][...] = total

    shapes = [
        jax.ShapeDtypeStruct((n, in_width), F32),
        jax.ShapeDtypeStruct((n, out_width), F32),
        jax.ShapeDtypeStruct((n, 128), F32),
    ]
    return pl.pallas_call(
        body,
        out_shape=tuple(shapes[:outs]),
        in_specs=[VMEM] * (3 + len(flat) + len(carried)),
        out_specs=(VMEM,) * outs,
        compiler_params=params(24),
        cost_estimate=BRIEF,
        name="backward",
    )(center_pos, coefficients, spread.reshape(1, n), *flat, *carried)


def solution(mesh):
    nz, nc = mesh.shape["points"], mesh.shape["centers"]

    def per_device(train_points, saved_preds, targets, huber_delta, center_pos, coefficients, spread):
        n_rows = train_points.shape[0]
        n, out_width = coefficients.shape
        piece = n_rows // nc

        own, payload = pack(train_points, center_pos, coefficients, spread, piece)

        layer = {0: own}
        for dz in range(2, nz, 2):
            layer[dz] = swap(own, "points", nz, dz)
        layer[1] = swap(own, "points", nz, 1)

        payloads = {0: payload}
        for d in range(2, nc, 2):
            payloads[d] = swap(payload, "centers", nc, d)
        payloads[1] = swap(payload, "centers", nc, 1)
        for dz in range(3, nz, 2):
            layer[dz] = swap(layer[dz - 1], "points", nz, 1)
        for d in range(2, nc, 2):
            payloads[d + 1] = swap(after(payloads[d], layer[1], layer[2]), "centers", nc, 1)
        blocks = [payloads[d] for d in range(nc)]

        saved, target, *local, delta = take(
            [saved_preds, targets] + [train_points] * (nc - 1), [0, 0, *range(1, nc)], piece, huber_delta
        )
        local = [own, *local]

        early = {0: jnp.concatenate([layer[dz] for dz in range(1, nz - 1)])}
        for d in range(2, nc, 2):
            early[d] = swap(after(early[0], payloads[d]), "centers", nc, d)
        early[1] = swap(after(early[0], payloads[2]), "centers", nc, 1)

        parts, received = {}, {}
        for dz in range(2, nz, 2):
            parts[dz] = forward(after(layer[dz], saved), blocks, n, out_width)
            received[dz] = swap(parts[dz], "points", nz, dz)
        for dz in range(3, nz, 2):
            parts[dz] = forward(after(layer[dz], parts[dz - 1], early[1]), blocks, n, out_width)
            received[dz] = swap(parts[dz], "points", nz, dz)
        parts[1] = forward(after(layer[1], parts[nz - 1]), blocks, n, out_width)
        received[1] = swap(parts[1], "points", nz, 1)
        soon = [received.pop(dz) for dz in range(2, nz, 2)]
        own = after(own, parts[1])
        kernels, late = {}, {0: layer[nz - 1]}
        parts[0], kernels[0] = own_rows(
            own, blocks, out_width, soon, center_pos, spread, [local[0], early[0], late[0]]
        )
        late[0] = after(late[0], parts[0])
        for d in (1, *range(2, nc, 2)):
            late[d] = swap(late[0], "centers", nc, d)
        for d in range(2, nc, 2):
            early[d + 1] = swap(after(early[d], parts[0]), "centers", nc, 1)
        cot = cotangent([parts[0], *received.values()], saved, target, delta)

        kernels[1] = own_kernel(center_pos, spread, [local[1], early[1], late[1]])
        far = [swap(cot, "points", nz, dz) for dz in range(2, nz)]
        far = jnp.concatenate([swap(after(cot, kernels[1]), "points", nz, 1), *far])
        cots = {0: [cot, far]}
        for d in range(2, nc, 2):
            cots[d] = [swap(a, "centers", nc, d) for a in (cot, far)]
        cots[1] = [swap(jnp.concatenate(cots[0]), "centers", nc, 1)]

        sums = None
        for d in range(nc):
            if d == 2:
                ready = [sums[0], *(kernels[k] for k in range(2, nc))]
                for k in range(2, nc, 2):
                    cots[k] = [after(a, *ready) for a in cots[k]]
                    cots[k + 1] = [swap(jnp.concatenate(cots[k]), "centers", nc, 1)]
            group = (kernels[d], [local[d], early[d], late[d]], cots[d])
            sums = backward(
                center_pos, coefficients, spread, [group], before=sums, last=d + 1 == nc
            )
            if d == 0:
                for k in range(2, nc, 2):
                    late[k + 1] = swap(after(late[k], sums[0]), "centers", nc, 1)
                    for j in (k, k + 1):
                        kernels[j] = own_kernel(center_pos, spread, [local[j], early[j], late[j]])
        return sums

    return jax.shard_map(
        per_device,
        mesh=mesh,
        in_specs=(
            P(("groups", "points"), None),
            P(("groups", "points"), None),
            P(("groups", "points"), None),
            P("groups"),
            P(("groups", "points", "centers"), None),
            P(("groups", "points", "centers"), None),
            P(("groups", "points", "centers")),
        ),
        out_specs=(
            P(("groups", "points", "centers"), None),
            P(("groups", "points", "centers"), None),
        ),
        check_vma=False,
    )
```

```python
import math

import jax
import jax.numpy as jnp
from jax import lax
from jax.experimental import pallas as pl
from jax.experimental.pallas import tpu as pltpu
from jax.sharding import PartitionSpec as P

F32, BF16 = jnp.float32, jnp.bfloat16
HBM = pl.BlockSpec(memory_space=pltpu.HBM)
VMEM = pl.BlockSpec(memory_space=pltpu.VMEM)
NT = (((1,), (1,)), ((), ()))
LOG2E = math.log2(math.e)
COVER = pl.CostEstimate(flops=1 << 34, bytes_accessed=1 << 20, transcendentals=1 << 20)
BRIEF = pl.CostEstimate(flops=1, bytes_accessed=1, transcendentals=0)


def swap(a, axis, size, d):
    return lax.ppermute(a, axis, [(i, i ^ d) for i in range(size)])


def after(a, *others):
    return lax.optimization_barrier((a, *others))[0]


def lane_groups(a):
    total = None
    for k in range(0, a.shape[1], 128):
        part = jnp.square(a[:, k : k + 128].astype(F32))
        total = part if total is None else total + part
    return total


def half_sq_row(a):
    return 0.5 * jnp.sum(lane_groups(a).T, axis=0, keepdims=True)


def half_sq_column(a):
    return 0.5 * jnp.sum(lane_groups(a), axis=1, keepdims=True)


def column(row):
    return jnp.broadcast_to(row, (128, row.shape[1])).T


def params(mib):
    return pltpu.CompilerParams(vmem_limit_bytes=mib << 20)


def pack(center_pos, coefficients, spread, delta):
    n, in_width = center_pos.shape
    out_width = coefficients.shape[1]
    across = in_width // out_width
    q = n // across

    def body(pos_ref, coef_ref, spread_ref, delta_ref, out_ref, row_ref):
        row_ref[...] = delta_ref[...]
        for k in range(across):
            out_ref[:q, k * out_width : (k + 1) * out_width] = coef_ref[k * q : (k + 1) * q]
        half = half_sq_row(pos_ref[...])
        high = half.astype(BF16)
        rest = half - high.astype(F32)
        middle = rest.astype(BF16)
        low = (rest - middle.astype(F32)).astype(BF16)
        rows = [r.astype(F32) for r in (spread_ref[...], high, middle, low)]
        tail = jnp.concatenate(rows + [jnp.zeros((12, n), F32)]).astype(BF16)
        if n < in_width:
            tail = jnp.concatenate([tail, jnp.zeros((16, in_width - n), BF16)], axis=1)
        out_ref[q:] = tail

    return pl.pallas_call(
        body,
        out_shape=(
            jax.ShapeDtypeStruct((q + 16, in_width), BF16),
            jax.ShapeDtypeStruct((1, delta.shape[0]), F32),
        ),
        in_specs=[VMEM] * 4,
        out_specs=(VMEM, VMEM),
        compiler_params=params(16),
        cost_estimate=BRIEF,
        name="pack",
    )(center_pos, coefficients, spread.reshape(1, n), delta.reshape(1, -1))


def take(arrays, offsets, piece, mib=16):
    def body(*refs):
        ins, outs, sems = refs[: len(arrays)], refs[len(arrays) : -1], refs[-1]
        made = []
        for k, d in enumerate(offsets):
            start = pl.multiple_of((lax.axis_index("centers") ^ d) * piece, piece)
            made.append(pltpu.make_async_copy(ins[k].at[pl.ds(start, piece)], outs[k], sems.at[k]))
            made[-1].start()
        for copy in made:
            copy.wait()

    return pl.pallas_call(
        body,
        out_shape=tuple(jax.ShapeDtypeStruct((piece, a.shape[1]), a.dtype) for a in arrays),
        in_specs=[HBM] * len(arrays),
        out_specs=(VMEM,) * len(arrays),
        scratch_shapes=[pltpu.SemaphoreType.DMA((len(arrays),))],
        compiler_params=params(mib),
        cost_estimate=BRIEF,
        name="take",
    )(*arrays)


def partial_pred(x, refs, total):
    in_width = x.shape[1]
    row_sq = half_sq_column(x)
    for pos_ref, side_ref in zip(refs[::2], refs[1::2]):
        n, q = pos_ref.shape[0], side_ref.shape[0] - 16
        out_width = q * in_width // n
        packed = side_ref[:q]
        coef = jnp.concatenate([packed[:, k : k + out_width] for k in range(0, in_width, out_width)])
        tail = side_ref[q:, :n].astype(F32)
        center_sq = tail[1:2] + tail[2:3] + tail[3:4]
        rate = tail[0:1] * (-2.0 * LOG2E / in_width)
        cross = lax.dot_general(x, pos_ref[...], NT, preferred_element_type=F32)
        power = (row_sq + center_sq - cross) * rate
        kernel = jnp.exp2(power).astype(BF16)
        new = jnp.dot(kernel, coef, preferred_element_type=F32)
        total = new if total is None else total + new
    return total


def own_values(pos_ref, spread_ref, refs, out_ref):
    pos = pos_ref[...]
    center_sq = half_sq_column(pos)
    rate = column(spread_ref[...].astype(F32) * (-2.0 * LOG2E / pos.shape[1]))[:, :1]
    at = 0
    for ref in refs:
        step = min(256, ref.shape[0])
        for start in range(0, ref.shape[0], step):
            x = ref[start : start + step]
            cross = lax.dot_general(pos, x, NT, preferred_element_type=F32)
            power = (center_sq + half_sq_row(x) - cross) * rate
            out_ref[:, at : at + step] = jnp.exp2(power).astype(BF16)
            at += step


def forward(rows, centers, out_width, cost):
    counts = [r.shape[0] for r in rows]

    def body(*refs):
        row_refs, refs, outs = refs[: len(rows)], refs[len(rows) : -len(rows)], refs[-len(rows) :]
        x = jnp.concatenate([ref[...] for ref in row_refs])
        total = partial_pred(x, refs, None)
        at = 0
        for ref, count in zip(outs, counts):
            ref[...] = total[at : at + count]
            at += count

    return pl.pallas_call(
        body,
        out_shape=tuple(jax.ShapeDtypeStruct((count, out_width), F32) for count in counts),
        in_specs=[VMEM] * (len(rows) + len(centers)),
        out_specs=(VMEM,) * len(rows),
        compiler_params=params(24),
        cost_estimate=cost,
        name="forward",
    )(*rows, *centers)


def own_kernel(center_pos, spread, blocks):
    n = center_pos.shape[0]
    points = sum(b.shape[0] for b in blocks)

    def body(pos_ref, spread_ref, *refs):
        own_values(pos_ref, spread_ref, refs[:-1], refs[-1])

    return pl.pallas_call(
        body,
        out_shape=jax.ShapeDtypeStruct((n, points), BF16),
        in_specs=[VMEM] * (2 + len(blocks)),
        out_specs=VMEM,
        compiler_params=params(16),
        cost_estimate=BRIEF,
        name="own_kernel",
    )(center_pos, spread.reshape(1, n), *blocks)


def own_rows(rows, centers, out_width, received, center_pos, spread, more):
    n = center_pos.shape[0]
    ends = [1, 1 + len(centers)]
    ends.append(ends[-1] + len(received))

    def body(*refs):
        outs, refs = refs[-1 - len(more) :], refs[: -1 - len(more)]
        total = None
        for ref in refs[ends[1] : ends[2]]:
            total = ref[...] if total is None else total + ref[...]
        outs[0][...] = partial_pred(refs[0][...], refs[1 : ends[1]], total)
        pos_ref, spread_ref, *block_refs = refs[ends[2] :]
        for k, blocks in enumerate(more):
            own_values(pos_ref, spread_ref, block_refs[: len(blocks)], outs[1 + k])
            del block_refs[: len(blocks)]

    ins = [rows, *centers, *received, center_pos, spread.reshape(1, n)]
    ins += [block for blocks in more for block in blocks]
    return pl.pallas_call(
        body,
        out_shape=(jax.ShapeDtypeStruct((rows.shape[0], out_width), F32),)
        + tuple(jax.ShapeDtypeStruct((n, sum(b.shape[0] for b in blocks)), BF16) for blocks in more),
        in_specs=[VMEM] * len(ins),
        out_specs=(VMEM,) * (1 + len(more)),
        compiler_params=params(16),
        cost_estimate=COVER,
        name="own_rows",
    )(*ins)


def cotangent(parts, saved, target, delta):
    def body(*refs):
        saved_ref, target_ref, delta_ref, out_ref = refs[-4:]
        pred = refs[0][...]
        for ref in refs[1:-4]:
            pred += ref[...]
        residual = pred + saved_ref[...] - target_ref[...]
        ratio = residual / delta_ref[...]
        out_ref[...] = (residual / jnp.sqrt(1.0 + ratio * ratio)).astype(BF16)

    return pl.pallas_call(
        body,
        out_shape=jax.ShapeDtypeStruct(saved.shape, BF16),
        in_specs=[VMEM] * (len(parts) + 3),
        out_specs=VMEM,
        compiler_params=params(16),
        cost_estimate=BRIEF,
        name="cotangent",
    )(*parts, saved, target, delta)


def backward(center_pos, coefficients, spread, groups, before=None, last=False, more=()):
    n, in_width = center_pos.shape
    out_width = coefficients.shape[1]
    flat = []
    for kernel, xs, cots in groups:
        flat += [kernel, *xs, *cots]
    carried = [] if before is None else list(before)
    outs = (2 if last else 3) + len(more)
    wanted = [block for blocks in more for block in blocks]
    points = sum(kernel.shape[1] for kernel, _, _ in groups)

    def body(pos_ref, coef_in, spread_ref, *refs):
        refs, out_refs = list(refs[:-outs]), refs[-outs:]
        coef = coef_in[...]
        moment = grad_coef = total = None
        if carried:
            moment, grad_coef, total = refs[len(flat) : len(flat) + 3]
        block_refs = refs[len(flat) + len(carried) :]
        for k, blocks in enumerate(more):
            own_values(pos_ref, spread_ref, block_refs[: len(blocks)], out_refs[3 + k])
            del block_refs[: len(blocks)]

        def plus(old, new):
            return new if old is None else old[...] + new

        for _, xs, cots in groups:
            kernel_ref = refs.pop(0)
            x_refs = [refs.pop(0) for _ in xs]
            cot_refs = [refs.pop(0) for _ in cots]
            cot = jnp.concatenate([ref[...] for ref in cot_refs])
            kernel = kernel_ref[...]
            mixing = lax.dot_general(coef, cot, NT, preferred_element_type=F32)
            weights = (kernel.astype(F32) * mixing).astype(BF16)
            grad_coef = plus(grad_coef, jnp.dot(kernel, cot, preferred_element_type=F32))
            lanes = weights[:, :128].astype(F32)
            for k in range(128, kernel.shape[1], 128):
                lanes += weights[:, k : k + 128].astype(F32)
            total = plus(total, lanes)
            x = jnp.concatenate([ref[...] for ref in x_refs])
            moment = plus(moment, jnp.dot(weights, x, preferred_element_type=F32))
        out_refs[1][...] = grad_coef
        if last:
            scale = column(spread_ref[...].astype(F32)) * (2.0 / in_width)
            total = jnp.sum(total, axis=1, keepdims=True)
            for k in range(0, in_width, 128):
                pos = pos_ref[:, k : k + 128].astype(F32)
                out_refs[0][:, k : k + 128] = scale * (moment[:, k : k + 128] - total * pos)
        else:
            out_refs[0][...] = moment
            out_refs[2][...] = total

    shapes = [
        jax.ShapeDtypeStruct((n, in_width), F32),
        jax.ShapeDtypeStruct((n, out_width), F32),
        jax.ShapeDtypeStruct((n, 128), F32),
    ]
    return pl.pallas_call(
        body,
        out_shape=tuple(shapes[: 2 if last else 3])
        + tuple(jax.ShapeDtypeStruct((n, sum(b.shape[0] for b in blocks)), BF16) for blocks in more),
        in_specs=[VMEM] * (3 + len(flat) + len(carried) + len(wanted)),
        out_specs=(VMEM,) * outs,
        compiler_params=params(24),
        cost_estimate=COVER if more else BRIEF,
        name="backward",
    )(center_pos, coefficients, spread.reshape(1, n), *flat, *carried, *wanted)


def solution(mesh):
    nz, nc = mesh.shape["points"], mesh.shape["centers"]

    def per_device(train_points, saved_preds, targets, huber_delta, center_pos, coefficients, spread):
        n_rows = train_points.shape[0]
        n, out_width = coefficients.shape
        piece = n_rows // nc

        (own,) = take([train_points], [0], piece, 62)

        layer = {0: own}
        for dz in range(2, nz, 2):
            layer[dz] = swap(own, "points", nz, dz)
        layer[1] = swap(own, "points", nz, 1)

        pos, side = {0: center_pos}, {}
        for d in range(2, nc, 2):
            pos[d] = swap(center_pos, "centers", nc, d)
        pos[1] = swap(center_pos, "centers", nc, 1)
        side[0], delta = pack(after(center_pos, own), coefficients, spread, huber_delta)
        for d in range(2, nc, 2):
            side[d] = swap(side[0], "centers", nc, d)
        side[1] = swap(side[0], "centers", nc, 1)
        for dz in range(3, nz, 2):
            layer[dz] = swap(layer[dz - 1], "points", nz, 1)
        for d in range(2, nc, 2):
            here = (layer[1], layer[2], side[d])
            pos[d + 1] = swap(after(pos[d], *here), "centers", nc, 1)
            side[d + 1] = swap(after(side[d], *here), "centers", nc, 1)
        centers = [a for d in range(nc) for a in (pos[d], side[d])]

        saved, target, *local = take(
            [saved_preds, targets] + [train_points] * (nc - 1), [0, 0, *range(1, nc)], piece
        )
        local = [own, *local]

        early = {0: jnp.concatenate([layer[dz] for dz in range(1, nz - 1)])}
        for d in range(2, nc, 2):
            early[d] = swap(after(early[0], side[d]), "centers", nc, d)
        early[1] = swap(after(early[0], side[nc - 1]), "centers", nc, 1)

        first, second = [*range(2, nz, 2), 1], range(3, nz, 2)
        rows = [after(layer[dz], saved) for dz in first]
        parts = dict(zip(first, forward(rows, centers, out_width, BRIEF)))
        rows = [after(layer[dz], *parts.values(), early[1]) for dz in second]
        received = {dz: swap(parts[dz], "points", nz, dz) for dz in first}
        parts.update(zip(second, forward(rows, centers, out_width, COVER)))
        soon = list(received.values())
        received = [swap(parts[dz], "points", nz, dz) for dz in second]
        last = parts[nz - 1]
        late = {0: layer[nz - 1]}
        for d in (1, *range(2, nc, 2)):
            late[d] = swap(after(late[0], last, *soon), "centers", nc, d)
        near = [[local[d], early[d], late[d]] for d in (0, 1)]
        kernels = {}
        parts[0], kernels[0], kernels[1] = own_rows(
            after(own, last), centers, out_width, soon, center_pos, spread, near
        )
        for d in range(2, nc, 2):
            early[d + 1] = swap(after(early[d], last), "centers", nc, 1)
        cot = cotangent([parts[0], *received], saved, target, delta)

        far = [swap(cot, "points", nz, dz) for dz in range(1, nz)]
        cots = {0: [jnp.concatenate([cot, *far])]}
        for d in range(2, nc, 2):
            cots[d] = [swap(cots[0][0], "centers", nc, d)]
            late[d + 1] = swap(after(late[d], far[0]), "centers", nc, 1)
        cots[1] = [swap(cots[0][0], "centers", nc, 1)]

        points = {d: [local[d], early[d], late[d]] for d in range(nc)}
        groups = [(kernels[d], points[d], cots[d]) for d in (0, 1)]
        rest = range(2, nc)
        *sums, a, b = backward(
            center_pos, coefficients, spread, groups, more=[points[2], points[3]]
        )
        kernels[2], kernels[3] = a, b
        for d in range(4, nc):
            kernels[d] = own_kernel(center_pos, spread, points[d])
        for d in range(2, nc, 2):
            cots[d] = [after(cots[d][0], sums[0])]
            cots[d + 1] = [swap(cots[d][0], "centers", nc, 1)]
        for d in rest:
            group = (kernels[d], points[d], cots[d])
            sums = backward(
                center_pos, coefficients, spread, [group], before=sums, last=d + 1 == nc
            )
        return sums

    return jax.shard_map(
        per_device,
        mesh=mesh,
        in_specs=(
            P(("groups", "points"), None),
            P(("groups", "points"), None),
            P(("groups", "points"), None),
            P("groups"),
            P(("groups", "points", "centers"), None),
            P(("groups", "points", "centers"), None),
            P(("groups", "points", "centers")),
        ),
        out_specs=(
            P(("groups", "points", "centers"), None),
            P(("groups", "points", "centers"), None),
        ),
        check_vma=False,
    )
```

```python
import math

import jax
import jax.numpy as jnp
from jax import lax
from jax.experimental import pallas as pl
from jax.experimental.pallas import tpu as pltpu
from jax.sharding import PartitionSpec as P

F32, BF16 = jnp.float32, jnp.bfloat16
HBM = pl.BlockSpec(memory_space=pltpu.HBM)
VMEM = pl.BlockSpec(memory_space=pltpu.VMEM)
NT = (((1,), (1,)), ((), ()))
LOG2E = math.log2(math.e)
COVER = pl.CostEstimate(flops=1 << 34, bytes_accessed=1 << 20, transcendentals=1 << 20)
BRIEF = pl.CostEstimate(flops=1, bytes_accessed=1, transcendentals=0)


def swap(a, axis, size, d):
    return lax.ppermute(a, axis, [(i, i ^ d) for i in range(size)])


def after(a, *others):
    return lax.optimization_barrier((a, *others))[0]


def lane_groups(a):
    total = None
    for k in range(0, a.shape[1], 128):
        part = jnp.square(a[:, k : k + 128].astype(F32))
        total = part if total is None else total + part
    return total


def half_sq_row(a):
    return 0.5 * jnp.sum(lane_groups(a).T, axis=0, keepdims=True)


def half_sq_column(a):
    return 0.5 * jnp.sum(lane_groups(a), axis=1, keepdims=True)


def column(row):
    return jnp.broadcast_to(row, (128, row.shape[1])).T


def params(mib):
    return pltpu.CompilerParams(vmem_limit_bytes=mib << 20)


def pack(center_pos, coefficients, spread, delta):
    n, in_width = center_pos.shape
    out_width = coefficients.shape[1]
    across = in_width // out_width
    q = n // across

    def body(pos_ref, coef_ref, spread_ref, delta_ref, out_ref, row_ref):
        row_ref[...] = delta_ref[...]
        for k in range(across):
            out_ref[:q, k * out_width : (k + 1) * out_width] = coef_ref[k * q : (k + 1) * q]
        half = half_sq_row(pos_ref[...])
        high = half.astype(BF16)
        rest = half - high.astype(F32)
        middle = rest.astype(BF16)
        low = (rest - middle.astype(F32)).astype(BF16)
        rows = [r.astype(F32) for r in (spread_ref[...], high, middle, low)]
        tail = jnp.concatenate(rows + [jnp.zeros((12, n), F32)]).astype(BF16)
        if n < in_width:
            tail = jnp.concatenate([tail, jnp.zeros((16, in_width - n), BF16)], axis=1)
        out_ref[q:] = tail

    return pl.pallas_call(
        body,
        out_shape=(
            jax.ShapeDtypeStruct((q + 16, in_width), BF16),
            jax.ShapeDtypeStruct((1, delta.shape[0]), F32),
        ),
        in_specs=[VMEM] * 4,
        out_specs=(VMEM, VMEM),
        compiler_params=params(16),
        cost_estimate=BRIEF,
        name="pack",
    )(center_pos, coefficients, spread.reshape(1, n), delta.reshape(1, -1))


def take(arrays, offsets, piece, space=VMEM):
    def body(*refs):
        ins, outs, sems = refs[: len(arrays)], refs[len(arrays) : -1], refs[-1]
        made = []
        for k, d in enumerate(offsets):
            start = pl.multiple_of((lax.axis_index("centers") ^ d) * piece, piece)
            made.append(pltpu.make_async_copy(ins[k].at[pl.ds(start, piece)], outs[k], sems.at[k]))
            made[-1].start()
        for copy in made:
            copy.wait()

    return pl.pallas_call(
        body,
        out_shape=tuple(jax.ShapeDtypeStruct((piece, a.shape[1]), a.dtype) for a in arrays),
        in_specs=[HBM] * len(arrays),
        out_specs=(space,) * len(arrays),
        scratch_shapes=[pltpu.SemaphoreType.DMA((len(arrays),))],
        compiler_params=params(16 if space is VMEM else 62),
        cost_estimate=BRIEF,
        name="take",
    )(*arrays)


def partial_pred(x, refs, total):
    in_width = x.shape[1]
    row_sq = half_sq_column(x)
    for pos_ref, side_ref in zip(refs[::2], refs[1::2]):
        n, q = pos_ref.shape[0], side_ref.shape[0] - 16
        out_width = q * in_width // n
        packed = side_ref[:q]
        coef = jnp.concatenate([packed[:, k : k + out_width] for k in range(0, in_width, out_width)])
        tail = side_ref[q:, :n].astype(F32)
        center_sq = tail[1:2] + tail[2:3] + tail[3:4]
        rate = tail[0:1] * (-2.0 * LOG2E / in_width)
        cross = lax.dot_general(x, pos_ref[...], NT, preferred_element_type=F32)
        power = (row_sq + center_sq - cross) * rate
        kernel = jnp.exp2(power).astype(BF16)
        new = jnp.dot(kernel, coef, preferred_element_type=F32)
        total = new if total is None else total + new
    return total


def own_values(pos_ref, spread_ref, refs):
    pos = pos_ref[...]
    center_sq = half_sq_column(pos)
    rate = column(spread_ref[...].astype(F32) * (-2.0 * LOG2E / pos.shape[1]))[:, :1]
    for ref in refs:
        step = min(256, ref.shape[0])
        for start in range(0, ref.shape[0], step):
            x = ref[start : start + step]
            cross = lax.dot_general(pos, x, NT, preferred_element_type=F32)
            power = (center_sq + half_sq_row(x) - cross) * rate
            yield jnp.exp2(power).astype(BF16)


def store_values(pos_ref, spread_ref, refs, out_ref):
    at = 0
    for part in own_values(pos_ref, spread_ref, refs):
        out_ref[:, at : at + part.shape[1]] = part
        at += part.shape[1]


def forward(rows, centers, out_width, cost):
    counts = [r.shape[0] for r in rows]

    def body(*refs):
        row_refs, refs, outs = refs[: len(rows)], refs[len(rows) : -len(rows)], refs[-len(rows) :]
        x = jnp.concatenate([ref[...] for ref in row_refs])
        total = partial_pred(x, refs, None)
        at = 0
        for ref, count in zip(outs, counts):
            ref[...] = total[at : at + count]
            at += count

    return pl.pallas_call(
        body,
        out_shape=tuple(jax.ShapeDtypeStruct((count, out_width), F32) for count in counts),
        in_specs=[VMEM] * (len(rows) + len(centers)),
        out_specs=(VMEM,) * len(rows),
        compiler_params=params(24),
        cost_estimate=cost,
        name="forward",
    )(*rows, *centers)


def own_kernel(center_pos, spread, blocks):
    n = center_pos.shape[0]
    points = sum(b.shape[0] for b in blocks)

    def body(pos_ref, spread_ref, *refs):
        store_values(pos_ref, spread_ref, refs[:-1], refs[-1])

    return pl.pallas_call(
        body,
        out_shape=jax.ShapeDtypeStruct((n, points), BF16),
        in_specs=[VMEM] * (2 + len(blocks)),
        out_specs=VMEM,
        compiler_params=params(16),
        cost_estimate=BRIEF,
        name="own_kernel",
    )(center_pos, spread.reshape(1, n), *blocks)


def own_rows(rows, centers, out_width, received, center_pos, spread, more):
    n = center_pos.shape[0]
    ends = [1, 1 + len(centers)]
    ends.append(ends[-1] + len(received))

    def body(*refs):
        outs, refs = refs[-1 - len(more) :], refs[: -1 - len(more)]
        total = None
        for ref in refs[ends[1] : ends[2]]:
            total = ref[...] if total is None else total + ref[...]
        outs[0][...] = partial_pred(refs[0][...], refs[1 : ends[1]], total)
        pos_ref, spread_ref, *block_refs = refs[ends[2] :]
        for k, blocks in enumerate(more):
            store_values(pos_ref, spread_ref, block_refs[: len(blocks)], outs[1 + k])
            del block_refs[: len(blocks)]

    ins = [rows, *centers, *received, center_pos, spread.reshape(1, n)]
    ins += [block for blocks in more for block in blocks]
    return pl.pallas_call(
        body,
        out_shape=(jax.ShapeDtypeStruct((rows.shape[0], out_width), F32),)
        + tuple(jax.ShapeDtypeStruct((n, sum(b.shape[0] for b in blocks)), BF16) for blocks in more),
        in_specs=[VMEM] * len(ins),
        out_specs=(VMEM,) * (1 + len(more)),
        compiler_params=params(16),
        cost_estimate=COVER,
        name="own_rows",
    )(*ins)


def cotangent(parts, saved, target, delta):
    def body(*refs):
        saved_ref, target_ref, delta_ref, out_ref = refs[-4:]
        pred = refs[0][...]
        for ref in refs[1:-4]:
            pred += ref[...]
        residual = pred + saved_ref[...] - target_ref[...]
        ratio = residual / delta_ref[...]
        out_ref[...] = (residual / jnp.sqrt(1.0 + ratio * ratio)).astype(BF16)

    return pl.pallas_call(
        body,
        out_shape=jax.ShapeDtypeStruct(saved.shape, BF16),
        in_specs=[VMEM] * (len(parts) + 3),
        out_specs=VMEM,
        compiler_params=params(16),
        cost_estimate=BRIEF,
        name="cotangent",
    )(*parts, saved, target, delta)


def group_terms(coef, kernel, x, cot):
    mixing = lax.dot_general(coef, cot, NT, preferred_element_type=F32)
    weights = (kernel.astype(F32) * mixing).astype(BF16)
    lanes = weights[:, :128].astype(F32)
    for k in range(128, kernel.shape[1], 128):
        lanes += weights[:, k : k + 128].astype(F32)
    return (
        jnp.dot(weights, x, preferred_element_type=F32),
        jnp.dot(kernel, cot, preferred_element_type=F32),
        lanes,
    )


def backward(center_pos, coefficients, spread, groups, before=None, more=()):
    n, in_width = center_pos.shape
    out_width = coefficients.shape[1]
    flat = []
    for kernel, xs, cot in groups:
        flat += [*xs, cot] if kernel is None else [kernel, *xs, cot]
    carried = [] if before is None else list(before)
    outs = 3 + len(more)
    wanted = [block for blocks in more for block in blocks]

    def body(pos_ref, coef_ref, spread_ref, *refs):
        refs, out_refs = list(refs[:-outs]), refs[-outs:]
        coef = coef_ref[...]
        sums = [ref[...] for ref in refs[len(flat) : len(flat) + 3]] if carried else None
        block_refs = refs[len(flat) + len(carried) :]
        for k, blocks in enumerate(more):
            store_values(pos_ref, spread_ref, block_refs[: len(blocks)], out_refs[3 + k])
            del block_refs[: len(blocks)]
        for given, xs, _ in groups:
            kernel = None if given is None else refs.pop(0)[...]
            x_refs = [refs.pop(0) for _ in xs]
            if given is None:
                kernel = jnp.concatenate(list(own_values(pos_ref, spread_ref, x_refs)), axis=1)
            x = jnp.concatenate([ref[...] for ref in x_refs])
            terms = group_terms(coef, kernel, x, refs.pop(0)[...])
            sums = terms if sums is None else [a + b for a, b in zip(sums, terms)]
        for ref, value in zip(out_refs[:3], sums):
            ref[...] = value

    return pl.pallas_call(
        body,
        out_shape=tuple(jax.ShapeDtypeStruct((n, width), F32) for width in (in_width, out_width, 128))
        + tuple(jax.ShapeDtypeStruct((n, sum(b.shape[0] for b in blocks)), BF16) for blocks in more),
        in_specs=[VMEM] * (3 + len(flat) + len(carried) + len(wanted)),
        out_specs=(VMEM,) * outs,
        compiler_params=params(24),
        cost_estimate=COVER if more else BRIEF,
        name="backward",
    )(center_pos, coefficients, spread.reshape(1, n), *flat, *carried, *wanted)


def finish(center_pos, coefficients, spread, group, before):
    n, in_width = center_pos.shape
    out_width = coefficients.shape[1]
    kernel, xs, cot = group
    step = min(n, 256)

    def body(pos_ref, coef_ref, spread_ref, kernel_ref, cot_ref, *refs):
        x_refs, refs = refs[: len(xs)], refs[len(xs) :]
        moment_ref, grad_ref, lanes_ref, centers_out, coef_out, centers_buf, coef_buf, sems = refs
        x = jnp.concatenate([ref[...] for ref in x_refs])
        cot = cot_ref[...]
        scale = column(spread_ref[...].astype(F32)) * (2.0 / in_width)
        made = []
        for k, start in enumerate(range(0, n, step)):
            rows = slice(start, start + step)
            moment, grad, lanes = group_terms(coef_ref[rows], kernel_ref[rows], x, cot)
            coef_buf[rows] = grad_ref[rows] + grad
            moment += moment_ref[rows]
            total = jnp.sum(lanes_ref[rows] + lanes, axis=1, keepdims=True)
            for at in range(0, in_width, 128):
                pos = pos_ref[rows, at : at + 128].astype(F32)
                centers_buf[rows, at : at + 128] = scale[rows] * (moment[:, at : at + 128] - total * pos)
            pairs = [(centers_buf, centers_out), (coef_buf, coef_out)]
            for j, (src, dst) in enumerate(pairs):
                copy = pltpu.make_async_copy(src.at[rows], dst.at[rows], sems.at[2 * k + j])
                copy.start()
                made.append(copy)
        for copy in made:
            copy.wait()

    ins = [center_pos, coefficients, spread.reshape(1, n), kernel, cot, *xs, *before]
    return pl.pallas_call(
        body,
        out_shape=tuple(jax.ShapeDtypeStruct((n, width), F32) for width in (in_width, out_width)),
        in_specs=[VMEM] * len(ins),
        out_specs=(HBM, HBM),
        scratch_shapes=[
            pltpu.VMEM((n, in_width), F32),
            pltpu.VMEM((n, out_width), F32),
            pltpu.SemaphoreType.DMA((2 * pl.cdiv(n, step),)),
        ],
        compiler_params=params(24),
        cost_estimate=BRIEF,
        name="finish",
    )(*ins)


def solution(mesh):
    nz, nc = mesh.shape["points"], mesh.shape["centers"]

    def per_device(train_points, saved_preds, targets, huber_delta, center_pos, coefficients, spread):
        n_rows = train_points.shape[0]
        n, out_width = coefficients.shape
        piece = n_rows // nc

        (own,) = take([train_points], [0], piece, HBM)

        layer = {0: own}
        for dz in range(2, nz, 2):
            layer[dz] = swap(own, "points", nz, dz)
        layer[1] = swap(own, "points", nz, 1)

        pos, side = {0: center_pos}, {}
        for d in range(2, nc, 2):
            pos[d] = swap(center_pos, "centers", nc, d)
        pos[1] = swap(center_pos, "centers", nc, 1)
        side[0], delta = pack(after(center_pos, own), coefficients, spread, huber_delta)
        for d in range(2, nc, 2):
            side[d] = swap(side[0], "centers", nc, d)
        side[1] = swap(side[0], "centers", nc, 1)
        for dz in range(3, nz, 2):
            layer[dz] = swap(layer[dz - 1], "points", nz, 1)
        for d in range(2, nc, 2):
            here = (layer[1], layer[2], side[d])
            pos[d + 1] = swap(after(pos[d], *here), "centers", nc, 1)
            side[d + 1] = swap(after(side[d], *here), "centers", nc, 1)
        centers = [a for d in range(nc) for a in (pos[d], side[d])]

        saved, target, *local = take(
            [saved_preds, targets] + [train_points] * (nc - 1), [0, 0, *range(1, nc)], piece
        )
        local = [own, *local]

        early = {0: jnp.concatenate([layer[dz] for dz in range(1, nz - 1)])}
        for d in range(2, nc, 2):
            early[d] = swap(after(early[0], side[d]), "centers", nc, d)
        early[1] = swap(after(early[0], side[nc - 1]), "centers", nc, 1)

        first, second = [*range(2, nz, 2), 1], range(3, nz, 2)
        rows = [after(layer[dz], saved) for dz in first]
        parts = dict(zip(first, forward(rows, centers, out_width, BRIEF)))
        rows = [after(layer[dz], *parts.values(), early[1]) for dz in second]
        received = {dz: swap(parts[dz], "points", nz, dz) for dz in first}
        parts.update(zip(second, forward(rows, centers, out_width, COVER)))
        soon = list(received.values())
        received = [swap(parts[dz], "points", nz, dz) for dz in second]
        last = parts[nz - 1]
        kernels, late = {1: None}, {0: layer[nz - 1]}
        parts[0], kernels[0] = own_rows(
            after(own, last),
            centers,
            out_width,
            soon,
            center_pos,
            spread,
            [[local[0], early[0], late[0]]],
        )
        for d in range(2, nc, 2):
            late[d] = swap(after(late[0], parts[0]), "centers", nc, d)
            early[d + 1] = swap(after(early[d], parts[0]), "centers", nc, 1)
        late[1] = swap(after(late[0], parts[0]), "centers", nc, 1)
        cot = cotangent([parts[0], *received], saved, target, delta)

        far = [swap(cot, "points", nz, dz) for dz in range(1, nz)]
        cots = {0: jnp.concatenate([cot, *far])}
        for d in range(2, nc, 2):
            cots[d] = swap(cots[0], "centers", nc, d)
            late[d + 1] = swap(after(late[d], far[0]), "centers", nc, 1)
        cots[1] = swap(cots[0], "centers", nc, 1)

        points = {d: [local[d], early[d], late[d]] for d in range(nc)}
        groups = [(kernels[d], points[d], cots[d]) for d in (0, 1)]
        *sums, kernels[2], kernels[3] = backward(
            center_pos, coefficients, spread, groups, more=[points[2], points[3]]
        )
        for d in range(4, nc):
            kernels[d] = own_kernel(center_pos, spread, points[d])
        for d in range(2, nc, 2):
            cots[d] = after(cots[d], sums[0])
            cots[d + 1] = swap(cots[d], "centers", nc, 1)
        for d in range(2, nc - 1):
            group = (kernels[d], points[d], cots[d])
            sums = backward(center_pos, coefficients, spread, [group], before=sums)
        group = (kernels[nc - 1], points[nc - 1], cots[nc - 1])
        return finish(center_pos, coefficients, spread, group, sums)

    return jax.shard_map(
        per_device,
        mesh=mesh,
        in_specs=(
            P(("groups", "points"), None),
            P(("groups", "points"), None),
            P(("groups", "points"), None),
            P("groups"),
            P(("groups", "points", "centers"), None),
            P(("groups", "points", "centers"), None),
            P(("groups", "points", "centers")),
        ),
        out_specs=(
            P(("groups", "points", "centers"), None),
            P(("groups", "points", "centers"), None),
        ),
        check_vma=False,
    )
```

```python
import math

import jax
import jax.numpy as jnp
from jax import lax
from jax.experimental import pallas as pl
from jax.experimental.pallas import tpu as pltpu
from jax.sharding import PartitionSpec as P

F32, BF16 = jnp.float32, jnp.bfloat16
HBM = pl.BlockSpec(memory_space=pltpu.HBM)
VMEM = pl.BlockSpec(memory_space=pltpu.VMEM)
NT = (((1,), (1,)), ((), ()))
LOG2E = math.log2(math.e)
COVER = pl.CostEstimate(flops=1 << 34, bytes_accessed=1 << 20, transcendentals=1 << 20)
BRIEF = pl.CostEstimate(flops=1, bytes_accessed=1, transcendentals=0)


def swap(a, axis, size, d):
    return lax.ppermute(a, axis, [(i, i ^ d) for i in range(size)])


def after(a, *others):
    return lax.optimization_barrier((a, *others))[0]


def lane_groups(a):
    total = None
    for k in range(0, a.shape[1], 128):
        part = jnp.square(a[:, k : k + 128].astype(F32))
        total = part if total is None else total + part
    return total


def half_sq_row(a):
    return 0.5 * jnp.sum(lane_groups(a).T, axis=0, keepdims=True)


def half_sq_column(a):
    return 0.5 * jnp.sum(lane_groups(a), axis=1, keepdims=True)


def column(row):
    return jnp.broadcast_to(row, (128, row.shape[1])).T


def params(mib):
    return pltpu.CompilerParams(vmem_limit_bytes=mib << 20)


def pack(center_pos, coefficients, spread, delta):
    n, in_width = center_pos.shape
    out_width = coefficients.shape[1]
    across = in_width // out_width
    q = n // across

    def body(pos_ref, coef_ref, spread_ref, delta_ref, out_ref, row_ref):
        row_ref[...] = delta_ref[...]
        for k in range(across):
            out_ref[:q, k * out_width : (k + 1) * out_width] = coef_ref[k * q : (k + 1) * q]
        half = half_sq_row(pos_ref[...])
        high = half.astype(BF16)
        rest = half - high.astype(F32)
        middle = rest.astype(BF16)
        low = (rest - middle.astype(F32)).astype(BF16)
        rows = [r.astype(F32) for r in (spread_ref[...], high, middle, low)]
        tail = jnp.concatenate(rows + [jnp.zeros((12, n), F32)]).astype(BF16)
        if n < in_width:
            tail = jnp.concatenate([tail, jnp.zeros((16, in_width - n), BF16)], axis=1)
        out_ref[q:] = tail

    return pl.pallas_call(
        body,
        out_shape=(
            jax.ShapeDtypeStruct((q + 16, in_width), BF16),
            jax.ShapeDtypeStruct((1, delta.shape[0]), F32),
        ),
        in_specs=[VMEM] * 4,
        out_specs=(VMEM, VMEM),
        compiler_params=params(16),
        cost_estimate=BRIEF,
        name="pack",
    )(center_pos, coefficients, spread.reshape(1, n), delta.reshape(1, -1))


def take(arrays, offsets, piece):
    def body(*refs):
        ins, outs, sems = refs[: len(arrays)], refs[len(arrays) : -1], refs[-1]
        made = []
        for k, d in enumerate(offsets):
            start = pl.multiple_of((lax.axis_index("centers") ^ d) * piece, piece)
            made.append(pltpu.make_async_copy(ins[k].at[pl.ds(start, piece)], outs[k], sems.at[k]))
            made[-1].start()
        for copy in made:
            copy.wait()

    return pl.pallas_call(
        body,
        out_shape=tuple(jax.ShapeDtypeStruct((piece, a.shape[1]), a.dtype) for a in arrays),
        in_specs=[HBM] * len(arrays),
        out_specs=(VMEM,) * len(arrays),
        scratch_shapes=[pltpu.SemaphoreType.DMA((len(arrays),))],
        compiler_params=params(16),
        cost_estimate=BRIEF,
        name="take",
    )(*arrays)


def partial_pred(x, refs, total):
    in_width = x.shape[1]
    row_sq = half_sq_column(x)
    for pos_ref, side_ref in zip(refs[::2], refs[1::2]):
        n, q = pos_ref.shape[0], side_ref.shape[0] - 16
        out_width = q * in_width // n
        packed = side_ref[:q]
        coef = jnp.concatenate([packed[:, k : k + out_width] for k in range(0, in_width, out_width)])
        tail = side_ref[q:, :n].astype(F32)
        center_sq = tail[1:2] + tail[2:3] + tail[3:4]
        rate = tail[0:1] * (-2.0 * LOG2E / in_width)
        cross = lax.dot_general(x, pos_ref[...], NT, preferred_element_type=F32)
        power = (row_sq + center_sq - cross) * rate
        kernel = jnp.exp2(power).astype(BF16)
        new = jnp.dot(kernel, coef, preferred_element_type=F32)
        total = new if total is None else total + new
    return total


def own_values(pos_ref, spread_ref, refs):
    pos = pos_ref[...]
    center_sq = half_sq_column(pos)
    rate = column(spread_ref[...].astype(F32) * (-2.0 * LOG2E / pos.shape[1]))[:, :1]
    for ref in refs:
        step = min(256, ref.shape[0])
        for start in range(0, ref.shape[0], step):
            x = ref[start : start + step]
            cross = lax.dot_general(pos, x, NT, preferred_element_type=F32)
            power = (center_sq + half_sq_row(x) - cross) * rate
            yield jnp.exp2(power).astype(BF16)


def store_values(pos_ref, spread_ref, refs, out_ref):
    at = 0
    for part in own_values(pos_ref, spread_ref, refs):
        out_ref[:, at : at + part.shape[1]] = part
        at += part.shape[1]


def forward(rows, centers, out_width, cost):
    counts = [r.shape[0] for r in rows]

    def body(*refs):
        row_refs, refs, outs = refs[: len(rows)], refs[len(rows) : -len(rows)], refs[-len(rows) :]
        x = jnp.concatenate([ref[...] for ref in row_refs])
        total = partial_pred(x, refs, None)
        at = 0
        for ref, count in zip(outs, counts):
            ref[...] = total[at : at + count]
            at += count

    return pl.pallas_call(
        body,
        out_shape=tuple(jax.ShapeDtypeStruct((count, out_width), F32) for count in counts),
        in_specs=[VMEM] * (len(rows) + len(centers)),
        out_specs=(VMEM,) * len(rows),
        compiler_params=params(24),
        cost_estimate=cost,
        name="forward",
    )(*rows, *centers)


def own_kernel(center_pos, spread, blocks):
    n = center_pos.shape[0]
    points = sum(b.shape[0] for b in blocks)

    def body(pos_ref, spread_ref, *refs):
        store_values(pos_ref, spread_ref, refs[:-1], refs[-1])

    return pl.pallas_call(
        body,
        out_shape=jax.ShapeDtypeStruct((n, points), BF16),
        in_specs=[VMEM] * (2 + len(blocks)),
        out_specs=VMEM,
        compiler_params=params(16),
        cost_estimate=BRIEF,
        name="own_kernel",
    )(center_pos, spread.reshape(1, n), *blocks)


def own_rows(rows, centers, out_width, received, center_pos, spread, more):
    n = center_pos.shape[0]
    ends = [1, 1 + len(centers)]
    ends.append(ends[-1] + len(received))

    def body(*refs):
        outs, refs = refs[-1 - len(more) :], refs[: -1 - len(more)]
        total = None
        for ref in refs[ends[1] : ends[2]]:
            total = ref[...] if total is None else total + ref[...]
        outs[0][...] = partial_pred(refs[0][...], refs[1 : ends[1]], total)
        pos_ref, spread_ref, *block_refs = refs[ends[2] :]
        for k, blocks in enumerate(more):
            store_values(pos_ref, spread_ref, block_refs[: len(blocks)], outs[1 + k])
            del block_refs[: len(blocks)]

    ins = [rows, *centers, *received, center_pos, spread.reshape(1, n)]
    ins += [block for blocks in more for block in blocks]
    return pl.pallas_call(
        body,
        out_shape=(jax.ShapeDtypeStruct((rows.shape[0], out_width), F32),)
        + tuple(jax.ShapeDtypeStruct((n, sum(b.shape[0] for b in blocks)), BF16) for blocks in more),
        in_specs=[VMEM] * len(ins),
        out_specs=(VMEM,) * (1 + len(more)),
        compiler_params=params(16),
        cost_estimate=COVER,
        name="own_rows",
    )(*ins)


def cotangent(parts, saved, target, delta):
    def body(*refs):
        saved_ref, target_ref, delta_ref, out_ref = refs[-4:]
        pred = refs[0][...]
        for ref in refs[1:-4]:
            pred += ref[...]
        residual = pred + saved_ref[...] - target_ref[...]
        ratio = residual / delta_ref[...]
        out_ref[...] = (residual / jnp.sqrt(1.0 + ratio * ratio)).astype(BF16)

    return pl.pallas_call(
        body,
        out_shape=jax.ShapeDtypeStruct(saved.shape, BF16),
        in_specs=[VMEM] * (len(parts) + 3),
        out_specs=VMEM,
        compiler_params=params(16),
        cost_estimate=BRIEF,
        name="cotangent",
    )(*parts, saved, target, delta)


def group_terms(coef, kernel, x, cot):
    mixing = lax.dot_general(coef, cot, NT, preferred_element_type=F32)
    weights = (kernel.astype(F32) * mixing).astype(BF16)
    lanes = weights[:, :128].astype(F32)
    for k in range(128, kernel.shape[1], 128):
        lanes += weights[:, k : k + 128].astype(F32)
    return (
        jnp.dot(weights, x, preferred_element_type=F32),
        jnp.dot(kernel, cot, preferred_element_type=F32),
        lanes,
    )


def backward(center_pos, coefficients, spread, groups, before=None, more=()):
    n, in_width = center_pos.shape
    out_width = coefficients.shape[1]
    flat = []
    for kernel, xs, cot in groups:
        flat += [*xs, cot] if kernel is None else [kernel, *xs, cot]
    carried = [] if before is None else list(before)
    outs = 3 + len(more)
    wanted = [block for blocks in more for block in blocks]

    def body(pos_ref, coef_ref, spread_ref, *refs):
        refs, out_refs = list(refs[:-outs]), refs[-outs:]
        coef = coef_ref[...]
        sums = [ref[...] for ref in refs[len(flat) : len(flat) + 3]] if carried else None
        block_refs = refs[len(flat) + len(carried) :]
        for k, blocks in enumerate(more):
            store_values(pos_ref, spread_ref, block_refs[: len(blocks)], out_refs[3 + k])
            del block_refs[: len(blocks)]
        for given, xs, _ in groups:
            kernel = None if given is None else refs.pop(0)[...]
            x_refs = [refs.pop(0) for _ in xs]
            if given is None:
                kernel = jnp.concatenate(list(own_values(pos_ref, spread_ref, x_refs)), axis=1)
            x = jnp.concatenate([ref[...] for ref in x_refs])
            terms = group_terms(coef, kernel, x, refs.pop(0)[...])
            sums = terms if sums is None else [a + b for a, b in zip(sums, terms)]
        for ref, value in zip(out_refs[:3], sums):
            ref[...] = value

    return pl.pallas_call(
        body,
        out_shape=tuple(jax.ShapeDtypeStruct((n, width), F32) for width in (in_width, out_width, 128))
        + tuple(jax.ShapeDtypeStruct((n, sum(b.shape[0] for b in blocks)), BF16) for blocks in more),
        in_specs=[VMEM] * (3 + len(flat) + len(carried) + len(wanted)),
        out_specs=(VMEM,) * outs,
        compiler_params=params(24),
        cost_estimate=COVER if more else BRIEF,
        name="backward",
    )(center_pos, coefficients, spread.reshape(1, n), *flat, *carried, *wanted)


def finish(center_pos, coefficients, spread, group, before):
    n, in_width = center_pos.shape
    out_width = coefficients.shape[1]
    kernel, xs, cot = group
    step = min(n, 256)

    def body(pos_ref, coef_ref, spread_ref, kernel_ref, cot_ref, *refs):
        x_refs, refs = refs[: len(xs)], refs[len(xs) :]
        moment_ref, grad_ref, lanes_ref, centers_out, coef_out, centers_buf, coef_buf, sems = refs
        x = jnp.concatenate([ref[...] for ref in x_refs])
        cot = cot_ref[...]
        scale = column(spread_ref[...].astype(F32)) * (2.0 / in_width)
        made = []
        for k, start in enumerate(range(0, n, step)):
            rows = slice(start, start + step)
            moment, grad, lanes = group_terms(coef_ref[rows], kernel_ref[rows], x, cot)
            coef_buf[rows] = grad_ref[rows] + grad
            moment += moment_ref[rows]
            total = jnp.sum(lanes_ref[rows] + lanes, axis=1, keepdims=True)
            for at in range(0, in_width, 128):
                pos = pos_ref[rows, at : at + 128].astype(F32)
                centers_buf[rows, at : at + 128] = scale[rows] * (moment[:, at : at + 128] - total * pos)
            pairs = [(centers_buf, centers_out), (coef_buf, coef_out)]
            for j, (src, dst) in enumerate(pairs):
                copy = pltpu.make_async_copy(src.at[rows], dst.at[rows], sems.at[2 * k + j])
                copy.start()
                made.append(copy)
        for copy in made:
            copy.wait()

    ins = [center_pos, coefficients, spread.reshape(1, n), kernel, cot, *xs, *before]
    return pl.pallas_call(
        body,
        out_shape=tuple(jax.ShapeDtypeStruct((n, width), F32) for width in (in_width, out_width)),
        in_specs=[VMEM] * len(ins),
        out_specs=(HBM, HBM),
        scratch_shapes=[
            pltpu.VMEM((n, in_width), F32),
            pltpu.VMEM((n, out_width), F32),
            pltpu.SemaphoreType.DMA((2 * pl.cdiv(n, step),)),
        ],
        compiler_params=params(24),
        cost_estimate=BRIEF,
        name="finish",
    )(*ins)


def solution(mesh):
    nz, nc = mesh.shape["points"], mesh.shape["centers"]

    def per_device(train_points, saved_preds, targets, huber_delta, center_pos, coefficients, spread):
        n_rows = train_points.shape[0]
        n, out_width = coefficients.shape
        piece = n_rows // nc

        own = lax.dynamic_slice_in_dim(train_points, lax.axis_index("centers") * piece, piece)

        layer = {0: own}
        for dz in range(2, nz, 2):
            layer[dz] = swap(own, "points", nz, dz)
        layer[1] = swap(own, "points", nz, 1)

        pos, side = {0: center_pos}, {}
        for d in range(2, nc, 2):
            pos[d] = swap(center_pos, "centers", nc, d)
        pos[1] = swap(center_pos, "centers", nc, 1)
        side[0], delta = pack(after(center_pos, own), coefficients, spread, huber_delta)
        for d in range(2, nc, 2):
            side[d] = swap(side[0], "centers", nc, d)
        side[1] = swap(side[0], "centers", nc, 1)
        for dz in range(3, nz, 2):
            layer[dz] = swap(layer[dz - 1], "points", nz, 1)
        for d in range(2, nc, 2):
            here = (layer[1], layer[2], side[d])
            pos[d + 1] = swap(after(pos[d], *here), "centers", nc, 1)
            side[d + 1] = swap(after(side[d], *here), "centers", nc, 1)
        centers = [a for d in range(nc) for a in (pos[d], side[d])]

        saved, target, *local = take(
            [saved_preds, targets] + [train_points] * (nc - 1), [0, 0, *range(1, nc)], piece
        )
        local = [own, *local]

        early = {0: jnp.concatenate([layer[dz] for dz in range(1, nz - 1)])}
        for d in range(2, nc, 2):
            early[d] = swap(after(early[0], side[d]), "centers", nc, d)
        early[1] = swap(after(early[0], side[nc - 1]), "centers", nc, 1)

        first, second = [*range(2, nz, 2), 1], range(3, nz, 2)
        rows = [after(layer[dz], saved) for dz in first]
        parts = dict(zip(first, forward(rows, centers, out_width, BRIEF)))
        rows = [after(layer[dz], *parts.values(), early[1]) for dz in second]
        received = {dz: swap(parts[dz], "points", nz, dz) for dz in first}
        parts.update(zip(second, forward(rows, centers, out_width, COVER)))
        soon = list(received.values())
        received = [swap(parts[dz], "points", nz, dz) for dz in second]
        last = parts[nz - 1]
        kernels, late = {1: None}, {0: layer[nz - 1]}
        parts[0], kernels[0] = own_rows(
            after(own, last),
            centers,
            out_width,
            soon,
            center_pos,
            spread,
            [[local[0], early[0], late[0]]],
        )
        for d in range(2, nc, 2):
            late[d] = swap(after(late[0], last, *soon), "centers", nc, d)
            early[d + 1] = swap(after(early[d], parts[0]), "centers", nc, 1)
        late[1] = swap(after(late[0], parts[0]), "centers", nc, 1)
        cot = cotangent([parts[0], *received], saved, target, delta)

        far = {dz: swap(cot, "points", nz, dz) for dz in range(2, nz, 2)}
        held = after(cot, *(late[d] for d in range(2, nc, 2)))
        far[1] = swap(held, "points", nz, 1)
        far.update({dz: swap(far[dz - 1], "points", nz, 1) for dz in range(3, nz, 2)})
        ahead = {d: swap(cot, "centers", nc, d) for d in range(2, nc, 2)}
        far[1] = after(far[1], *ahead.values())
        far = jnp.concatenate([far[dz] for dz in range(1, nz)])
        cots = {0: jnp.concatenate([cot, far])}
        across = {}
        for d in range(2, nc, 2):
            across[d] = [ahead[d], swap(far, "centers", nc, d)]
            late[d + 1] = swap(after(late[d], far), "centers", nc, 1)
        cots[1] = swap(cots[0], "centers", nc, 1)

        points = {d: [local[d], early[d], late[d]] for d in range(nc)}
        groups = [(kernels[d], points[d], cots[d]) for d in (0, 1)]
        *sums, kernels[2], kernels[3] = backward(
            center_pos, coefficients, spread, groups, more=[points[2], points[3]]
        )
        for d in range(4, nc):
            kernels[d] = own_kernel(center_pos, spread, points[d])
        for d in range(2, nc, 2):
            cots[d] = jnp.concatenate([after(a, sums[0]) for a in across[d]])
            cots[d + 1] = swap(cots[d], "centers", nc, 1)
        for d in range(2, nc - 1):
            group = (kernels[d], points[d], cots[d])
            sums = backward(center_pos, coefficients, spread, [group], before=sums)
        group = (kernels[nc - 1], points[nc - 1], cots[nc - 1])
        return finish(center_pos, coefficients, spread, group, sums)

    return jax.shard_map(
        per_device,
        mesh=mesh,
        in_specs=(
            P(("groups", "points"), None),
            P(("groups", "points"), None),
            P(("groups", "points"), None),
            P("groups"),
            P(("groups", "points", "centers"), None),
            P(("groups", "points", "centers"), None),
            P(("groups", "points", "centers")),
        ),
        out_specs=(
            P(("groups", "points", "centers"), None),
            P(("groups", "points", "centers"), None),
        ),
        check_vma=False,
    )
```

```python
import math

import jax
import jax.numpy as jnp
from jax import lax
from jax.experimental import pallas as pl
from jax.experimental.pallas import tpu as pltpu
from jax.sharding import PartitionSpec as P

F32, BF16 = jnp.float32, jnp.bfloat16
HBM = pl.BlockSpec(memory_space=pltpu.HBM)
VMEM = pl.BlockSpec(memory_space=pltpu.VMEM)
NT = (((1,), (1,)), ((), ()))
LOG2E = math.log2(math.e)
COVER = pl.CostEstimate(flops=1 << 34, bytes_accessed=1 << 20, transcendentals=1 << 20)
BRIEF = pl.CostEstimate(flops=1, bytes_accessed=1, transcendentals=0)


def swap(a, axis, size, d):
    return lax.ppermute(a, axis, [(i, i ^ d) for i in range(size)])


def after(a, *others):
    return lax.optimization_barrier((a, *others))[0]


def lane_groups(a):
    total = None
    for k in range(0, a.shape[1], 128):
        part = jnp.square(a[:, k : k + 128].astype(F32))
        total = part if total is None else total + part
    return total


def half_sq_row(a):
    return 0.5 * jnp.sum(lane_groups(a).T, axis=0, keepdims=True)


def half_sq_column(a):
    return 0.5 * jnp.sum(lane_groups(a), axis=1, keepdims=True)


def column(row):
    return jnp.broadcast_to(row, (128, row.shape[1])).T


def params(mib):
    return pltpu.CompilerParams(vmem_limit_bytes=mib << 20)


def pack(center_pos, coefficients, spread, delta):
    n, in_width = center_pos.shape
    out_width = coefficients.shape[1]
    across = in_width // out_width
    q = n // across

    def body(pos_ref, coef_ref, spread_ref, delta_ref, out_ref, row_ref):
        row_ref[...] = delta_ref[...]
        for k in range(across):
            out_ref[:q, k * out_width : (k + 1) * out_width] = coef_ref[k * q : (k + 1) * q]
        half = half_sq_row(pos_ref[...])
        high = half.astype(BF16)
        rest = half - high.astype(F32)
        middle = rest.astype(BF16)
        low = (rest - middle.astype(F32)).astype(BF16)
        rows = [r.astype(F32) for r in (spread_ref[...], high, middle, low)]
        tail = jnp.concatenate(rows + [jnp.zeros((12, n), F32)]).astype(BF16)
        if n < in_width:
            tail = jnp.concatenate([tail, jnp.zeros((16, in_width - n), BF16)], axis=1)
        out_ref[q:] = tail

    return pl.pallas_call(
        body,
        out_shape=(
            jax.ShapeDtypeStruct((q + 16, in_width), BF16),
            jax.ShapeDtypeStruct((1, delta.shape[0]), F32),
        ),
        in_specs=[VMEM] * 4,
        out_specs=(VMEM, VMEM),
        compiler_params=params(16),
        cost_estimate=BRIEF,
        name="pack",
    )(center_pos, coefficients, spread.reshape(1, n), delta.reshape(1, -1))


def take(arrays, offsets, piece):
    def body(*refs):
        ins, outs, sems = refs[: len(arrays)], refs[len(arrays) : -1], refs[-1]
        made = []
        for k, d in enumerate(offsets):
            start = pl.multiple_of((lax.axis_index("centers") ^ d) * piece, piece)
            made.append(pltpu.make_async_copy(ins[k].at[pl.ds(start, piece)], outs[k], sems.at[k]))
            made[-1].start()
        for copy in made:
            copy.wait()

    return pl.pallas_call(
        body,
        out_shape=tuple(jax.ShapeDtypeStruct((piece, a.shape[1]), a.dtype) for a in arrays),
        in_specs=[HBM] * len(arrays),
        out_specs=(VMEM,) * len(arrays),
        scratch_shapes=[pltpu.SemaphoreType.DMA((len(arrays),))],
        compiler_params=params(16),
        cost_estimate=BRIEF,
        name="take",
    )(*arrays)


def partial_pred(x, refs, total):
    in_width = x.shape[1]
    row_sq = half_sq_column(x)
    for pos_ref, side_ref in zip(refs[::2], refs[1::2]):
        n, q = pos_ref.shape[0], side_ref.shape[0] - 16
        out_width = q * in_width // n
        packed = side_ref[:q]
        coef = jnp.concatenate([packed[:, k : k + out_width] for k in range(0, in_width, out_width)])
        tail = side_ref[q:, :n].astype(F32)
        center_sq = tail[1:2] + tail[2:3] + tail[3:4]
        rate = tail[0:1] * (-2.0 * LOG2E / in_width)
        cross = lax.dot_general(x, pos_ref[...], NT, preferred_element_type=F32)
        power = (row_sq + center_sq - cross) * rate
        kernel = jnp.exp2(power).astype(BF16)
        new = jnp.dot(kernel, coef, preferred_element_type=F32)
        total = new if total is None else total + new
    return total


def own_values(pos_ref, spread_ref, refs):
    pos = pos_ref[...]
    center_sq = half_sq_column(pos)
    rate = column(spread_ref[...].astype(F32) * (-2.0 * LOG2E / pos.shape[1]))[:, :1]
    for ref in refs:
        step = min(256, ref.shape[0])
        for start in range(0, ref.shape[0], step):
            x = ref[start : start + step]
            cross = lax.dot_general(pos, x, NT, preferred_element_type=F32)
            power = (center_sq + half_sq_row(x) - cross) * rate
            yield jnp.exp2(power).astype(BF16)


def store_values(pos_ref, spread_ref, refs, out_ref):
    at = 0
    for part in own_values(pos_ref, spread_ref, refs):
        out_ref[:, at : at + part.shape[1]] = part
        at += part.shape[1]


def forward(rows, centers, out_width, cost):
    counts = [r.shape[0] for r in rows]

    def body(*refs):
        row_refs, refs, outs = refs[: len(rows)], refs[len(rows) : -len(rows)], refs[-len(rows) :]
        x = jnp.concatenate([ref[...] for ref in row_refs])
        total = partial_pred(x, refs, None)
        at = 0
        for ref, count in zip(outs, counts):
            ref[...] = total[at : at + count]
            at += count

    return pl.pallas_call(
        body,
        out_shape=tuple(jax.ShapeDtypeStruct((count, out_width), F32) for count in counts),
        in_specs=[VMEM] * (len(rows) + len(centers)),
        out_specs=(VMEM,) * len(rows),
        compiler_params=params(24),
        cost_estimate=cost,
        name="forward",
    )(*rows, *centers)


def own_kernel(center_pos, spread, blocks):
    n = center_pos.shape[0]
    points = sum(b.shape[0] for b in blocks)

    def body(pos_ref, spread_ref, *refs):
        store_values(pos_ref, spread_ref, refs[:-1], refs[-1])

    return pl.pallas_call(
        body,
        out_shape=jax.ShapeDtypeStruct((n, points), BF16),
        in_specs=[VMEM] * (2 + len(blocks)),
        out_specs=VMEM,
        compiler_params=params(16),
        cost_estimate=BRIEF,
        name="own_kernel",
    )(center_pos, spread.reshape(1, n), *blocks)


def own_rows(rows, centers, out_width, received, center_pos, spread, more):
    n = center_pos.shape[0]
    ends = [1, 1 + len(centers)]
    ends.append(ends[-1] + len(received))

    def body(*refs):
        outs, refs = refs[-1 - len(more) :], refs[: -1 - len(more)]
        total = None
        for ref in refs[ends[1] : ends[2]]:
            total = ref[...] if total is None else total + ref[...]
        outs[0][...] = partial_pred(refs[0][...], refs[1 : ends[1]], total)
        pos_ref, spread_ref, *block_refs = refs[ends[2] :]
        for k, blocks in enumerate(more):
            store_values(pos_ref, spread_ref, block_refs[: len(blocks)], outs[1 + k])
            del block_refs[: len(blocks)]

    ins = [rows, *centers, *received, center_pos, spread.reshape(1, n)]
    ins += [block for blocks in more for block in blocks]
    return pl.pallas_call(
        body,
        out_shape=(jax.ShapeDtypeStruct((rows.shape[0], out_width), F32),)
        + tuple(jax.ShapeDtypeStruct((n, sum(b.shape[0] for b in blocks)), BF16) for blocks in more),
        in_specs=[VMEM] * len(ins),
        out_specs=(VMEM,) * (1 + len(more)),
        compiler_params=params(16),
        cost_estimate=COVER,
        name="own_rows",
    )(*ins)


def cotangent(parts, saved, target, delta):
    def body(*refs):
        saved_ref, target_ref, delta_ref, out_ref = refs[-4:]
        pred = refs[0][...]
        for ref in refs[1:-4]:
            pred += ref[...]
        residual = pred + saved_ref[...] - target_ref[...]
        ratio = residual / delta_ref[...]
        out_ref[...] = (residual / jnp.sqrt(1.0 + ratio * ratio)).astype(BF16)

    return pl.pallas_call(
        body,
        out_shape=jax.ShapeDtypeStruct(saved.shape, BF16),
        in_specs=[VMEM] * (len(parts) + 3),
        out_specs=VMEM,
        compiler_params=params(16),
        cost_estimate=BRIEF,
        name="cotangent",
    )(*parts, saved, target, delta)


def group_terms(coef, kernel, x, cot):
    mixing = lax.dot_general(coef, cot, NT, preferred_element_type=F32)
    weights = (kernel.astype(F32) * mixing).astype(BF16)
    lanes = weights[:, :128].astype(F32)
    for k in range(128, kernel.shape[1], 128):
        lanes += weights[:, k : k + 128].astype(F32)
    return (
        jnp.dot(weights, x, preferred_element_type=F32),
        jnp.dot(kernel, cot, preferred_element_type=F32),
        lanes,
    )


def backward(center_pos, coefficients, spread, groups, before=None, more=()):
    n, in_width = center_pos.shape
    out_width = coefficients.shape[1]
    flat = []
    for kernel, xs, cot in groups:
        flat += [*xs, cot] if kernel is None else [kernel, *xs, cot]
    carried = [] if before is None else list(before)
    outs = 3 + len(more)
    wanted = [block for blocks in more for block in blocks]

    def body(pos_ref, coef_ref, spread_ref, *refs):
        refs, out_refs = list(refs[:-outs]), refs[-outs:]
        coef = coef_ref[...]
        sums = [ref[...] for ref in refs[len(flat) : len(flat) + 3]] if carried else None
        block_refs = refs[len(flat) + len(carried) :]
        for k, blocks in enumerate(more):
            store_values(pos_ref, spread_ref, block_refs[: len(blocks)], out_refs[3 + k])
            del block_refs[: len(blocks)]
        for given, xs, _ in groups:
            kernel = None if given is None else refs.pop(0)[...]
            x_refs = [refs.pop(0) for _ in xs]
            if given is None:
                kernel = jnp.concatenate(list(own_values(pos_ref, spread_ref, x_refs)), axis=1)
            x = jnp.concatenate([ref[...] for ref in x_refs])
            terms = group_terms(coef, kernel, x, refs.pop(0)[...])
            sums = terms if sums is None else [a + b for a, b in zip(sums, terms)]
        for ref, value in zip(out_refs[:3], sums):
            ref[...] = value

    return pl.pallas_call(
        body,
        out_shape=tuple(jax.ShapeDtypeStruct((n, width), F32) for width in (in_width, out_width, 128))
        + tuple(jax.ShapeDtypeStruct((n, sum(b.shape[0] for b in blocks)), BF16) for blocks in more),
        in_specs=[VMEM] * (3 + len(flat) + len(carried) + len(wanted)),
        out_specs=(VMEM,) * outs,
        compiler_params=params(24),
        cost_estimate=COVER if more else BRIEF,
        name="backward",
    )(center_pos, coefficients, spread.reshape(1, n), *flat, *carried, *wanted)


def finish(center_pos, coefficients, spread, group, before):
    n, in_width = center_pos.shape
    out_width = coefficients.shape[1]
    kernel, xs, cot = group
    step = min(n, 256)

    def body(pos_ref, coef_ref, spread_ref, kernel_ref, cot_ref, *refs):
        x_refs, refs = refs[: len(xs)], refs[len(xs) :]
        moment_ref, grad_ref, lanes_ref, centers_out, coef_out, centers_buf, coef_buf, sems = refs
        x = jnp.concatenate([ref[...] for ref in x_refs])
        cot = cot_ref[...]
        scale = column(spread_ref[...].astype(F32)) * (2.0 / in_width)
        made = []
        for k, start in enumerate(range(0, n, step)):
            rows = slice(start, start + step)
            moment, grad, lanes = group_terms(coef_ref[rows], kernel_ref[rows], x, cot)
            coef_buf[rows] = grad_ref[rows] + grad
            moment += moment_ref[rows]
            total = jnp.sum(lanes_ref[rows] + lanes, axis=1, keepdims=True)
            for at in range(0, in_width, 128):
                pos = pos_ref[rows, at : at + 128].astype(F32)
                centers_buf[rows, at : at + 128] = scale[rows] * (moment[:, at : at + 128] - total * pos)
            pairs = [(centers_buf, centers_out), (coef_buf, coef_out)]
            for j, (src, dst) in enumerate(pairs):
                copy = pltpu.make_async_copy(src.at[rows], dst.at[rows], sems.at[2 * k + j])
                copy.start()
                made.append(copy)
        for copy in made:
            copy.wait()

    ins = [center_pos, coefficients, spread.reshape(1, n), kernel, cot, *xs, *before]
    return pl.pallas_call(
        body,
        out_shape=tuple(jax.ShapeDtypeStruct((n, width), F32) for width in (in_width, out_width)),
        in_specs=[VMEM] * len(ins),
        out_specs=(HBM, HBM),
        scratch_shapes=[
            pltpu.VMEM((n, in_width), F32),
            pltpu.VMEM((n, out_width), F32),
            pltpu.SemaphoreType.DMA((2 * pl.cdiv(n, step),)),
        ],
        compiler_params=params(24),
        cost_estimate=BRIEF,
        name="finish",
    )(*ins)


def solution(mesh):
    nz, nc = mesh.shape["points"], mesh.shape["centers"]

    def per_device(train_points, saved_preds, targets, huber_delta, center_pos, coefficients, spread):
        n_rows = train_points.shape[0]
        n, out_width = coefficients.shape
        piece = n_rows // nc

        own = lax.dynamic_slice_in_dim(train_points, lax.axis_index("centers") * piece, piece)

        layer = {0: own}
        for dz in range(2, nz, 2):
            layer[dz] = swap(own, "points", nz, dz)
        layer[1] = swap(own, "points", nz, 1)

        pos, side = {0: center_pos}, {}
        for d in range(2, nc, 2):
            pos[d] = swap(center_pos, "centers", nc, d)
        pos[1] = swap(center_pos, "centers", nc, 1)
        side[0], delta = pack(after(center_pos, own), coefficients, spread, huber_delta)
        for d in range(2, nc, 2):
            side[d] = swap(side[0], "centers", nc, d)
        side[1] = swap(side[0], "centers", nc, 1)
        for dz in range(3, nz, 2):
            layer[dz] = swap(layer[dz - 1], "points", nz, 1)
        saved, target, *local = take(
            [saved_preds, targets] + [train_points] * (nc - 1), [0, 0, *range(1, nc)], piece
        )
        local = [own, *local]
        for d in range(2, nc, 2):
            pos[d + 1] = swap(after(pos[d], layer[1], saved), "centers", nc, 1)
            side[d + 1] = swap(after(side[d], layer[2]), "centers", nc, 1)
        centers = [a for d in range(nc) for a in (pos[d], side[d])]

        early = {0: jnp.concatenate([layer[dz] for dz in range(1, nz - 1)])}
        for d in range(2, nc, 2):
            early[d] = swap(after(early[0], side[d]), "centers", nc, d)
        early[1] = swap(after(early[0], side[nc - 1]), "centers", nc, 1)

        first, second = [*range(2, nz, 2), 1], range(3, nz, 2)
        rows = [layer[dz] for dz in first]
        parts = dict(zip(first, forward(rows, centers, out_width, BRIEF)))
        rows = [after(layer[dz], *parts.values(), early[1]) for dz in second]
        received = {dz: swap(parts[dz], "points", nz, dz) for dz in first}
        parts.update(zip(second, forward(rows, centers, out_width, COVER)))
        soon = [received[dz] for dz in range(2, nz, 2)]
        received = [received[1]] + [swap(parts[dz], "points", nz, dz) for dz in second]
        last = parts[nz - 1]
        kernels, late = {1: None}, {0: layer[nz - 1]}
        parts[0], kernels[0] = own_rows(
            after(own, last),
            centers,
            out_width,
            soon,
            center_pos,
            spread,
            [[local[0], early[0], late[0]]],
        )
        for d in range(2, nc, 2):
            late[d] = swap(after(late[0], parts[0]), "centers", nc, d)
            early[d + 1] = swap(after(early[d], parts[0]), "centers", nc, 1)
        late[1] = swap(after(late[0], parts[0]), "centers", nc, 1)
        cot = cotangent([parts[0], *received], saved, target, delta)

        far = {dz: swap(cot, "points", nz, dz) for dz in range(2, nz, 2)}
        far[1] = swap(cot, "points", nz, 1)
        far.update({dz: swap(far[dz - 1], "points", nz, 1) for dz in range(3, nz, 2)})
        ahead = {d: swap(cot, "centers", nc, d) for d in range(2, nc, 2)}
        far[1] = after(far[1], *ahead.values())
        far = jnp.concatenate([far[dz] for dz in range(1, nz)])
        cots = {0: jnp.concatenate([cot, far])}
        across = {}
        for d in range(2, nc, 2):
            across[d] = [ahead[d], swap(far, "centers", nc, d)]
            late[d + 1] = swap(after(late[d], far), "centers", nc, 1)
        cots[1] = swap(cots[0], "centers", nc, 1)

        points = {d: [local[d], early[d], late[d]] for d in range(nc)}
        groups = [(kernels[d], points[d], cots[d]) for d in (0, 1)]
        *sums, kernels[2], kernels[3] = backward(
            center_pos, coefficients, spread, groups, more=[points[2], points[3]]
        )
        for d in range(4, nc):
            kernels[d] = own_kernel(center_pos, spread, points[d])
        for d in range(2, nc, 2):
            cots[d] = jnp.concatenate([after(a, sums[0]) for a in across[d]])
            cots[d + 1] = swap(cots[d], "centers", nc, 1)
        for d in range(2, nc - 1):
            group = (kernels[d], points[d], cots[d])
            sums = backward(center_pos, coefficients, spread, [group], before=sums)
        group = (kernels[nc - 1], points[nc - 1], cots[nc - 1])
        return finish(center_pos, coefficients, spread, group, sums)

    return jax.shard_map(
        per_device,
        mesh=mesh,
        in_specs=(
            P(("groups", "points"), None),
            P(("groups", "points"), None),
            P(("groups", "points"), None),
            P("groups"),
            P(("groups", "points", "centers"), None),
            P(("groups", "points", "centers"), None),
            P(("groups", "points", "centers")),
        ),
        out_specs=(
            P(("groups", "points", "centers"), None),
            P(("groups", "points", "centers"), None),
        ),
        check_vma=False,
    )
```

```python
import math

import jax
import jax.numpy as jnp
from jax import lax
from jax.experimental import pallas as pl
from jax.experimental.pallas import tpu as pltpu
from jax.sharding import PartitionSpec as P

F32, BF16 = jnp.float32, jnp.bfloat16
HBM = pl.BlockSpec(memory_space=pltpu.HBM)
VMEM = pl.BlockSpec(memory_space=pltpu.VMEM)
NT = (((1,), (1,)), ((), ()))
LOG2E = math.log2(math.e)
COVER = pl.CostEstimate(flops=1 << 34, bytes_accessed=1 << 20, transcendentals=1 << 20)
BRIEF = pl.CostEstimate(flops=1, bytes_accessed=1, transcendentals=0)


def swap(a, axis, size, d):
    return lax.ppermute(a, axis, [(i, i ^ d) for i in range(size)])


def after(a, *others):
    return lax.optimization_barrier((a, *others))[0]


def lane_groups(a):
    total = None
    for k in range(0, a.shape[1], 128):
        part = jnp.square(a[:, k : k + 128].astype(F32))
        total = part if total is None else total + part
    return total


def half_sq_row(a):
    return 0.5 * jnp.sum(lane_groups(a).T, axis=0, keepdims=True)


def half_sq_column(a):
    return 0.5 * jnp.sum(lane_groups(a), axis=1, keepdims=True)


def column(row):
    return jnp.broadcast_to(row, (128, row.shape[1])).T


def params(mib):
    return pltpu.CompilerParams(vmem_limit_bytes=mib << 20)


def pack(center_pos, coefficients, spread, delta):
    n, in_width = center_pos.shape
    out_width = coefficients.shape[1]
    across = in_width // out_width
    q = n // across

    def body(pos_ref, coef_ref, spread_ref, delta_ref, own_pos, out_ref, row_ref, own_spread, own_coef):
        row_ref[...] = delta_ref[...]
        own_spread[...] = spread_ref[...]
        own_coef[...] = coef_ref[...]
        pos = pos_ref[...]
        own_pos[...] = pos
        for k in range(across):
            out_ref[:q, k * out_width : (k + 1) * out_width] = coef_ref[k * q : (k + 1) * q]
        half = half_sq_row(pos)
        high = half.astype(BF16)
        rest = half - high.astype(F32)
        middle = rest.astype(BF16)
        low = (rest - middle.astype(F32)).astype(BF16)
        rows = [r.astype(F32) for r in (spread_ref[...], high, middle, low)]
        tail = jnp.concatenate(rows + [jnp.zeros((12, n), F32)]).astype(BF16)
        if n < in_width:
            tail = jnp.concatenate([tail, jnp.zeros((16, in_width - n), BF16)], axis=1)
        out_ref[q:] = tail

    return pl.pallas_call(
        body,
        out_shape=(
            jax.ShapeDtypeStruct((n, in_width), BF16),
            jax.ShapeDtypeStruct((q + 16, in_width), BF16),
            jax.ShapeDtypeStruct((1, delta.shape[0]), F32),
            jax.ShapeDtypeStruct((1, n), BF16),
            jax.ShapeDtypeStruct((n, out_width), BF16),
        ),
        in_specs=[VMEM] * 4,
        out_specs=(VMEM,) * 5,
        compiler_params=params(16),
        cost_estimate=BRIEF,
        name="pack",
    )(center_pos, coefficients, spread.reshape(1, n), delta.reshape(1, -1))


def take(arrays, offsets, piece):
    def body(*refs):
        ins, outs, sems = refs[: len(arrays)], refs[len(arrays) : -1], refs[-1]
        made = []
        for k, d in enumerate(offsets):
            start = pl.multiple_of((lax.axis_index("centers") ^ d) * piece, piece)
            made.append(pltpu.make_async_copy(ins[k].at[pl.ds(start, piece)], outs[k], sems.at[k]))
            made[-1].start()
        for copy in made:
            copy.wait()

    return pl.pallas_call(
        body,
        out_shape=tuple(jax.ShapeDtypeStruct((piece, a.shape[1]), a.dtype) for a in arrays),
        in_specs=[HBM] * len(arrays),
        out_specs=(VMEM,) * len(arrays),
        scratch_shapes=[pltpu.SemaphoreType.DMA((len(arrays),))],
        compiler_params=params(16),
        cost_estimate=BRIEF,
        name="take",
    )(*arrays)


def partial_pred(x, refs, total):
    in_width = x.shape[1]
    row_sq = half_sq_column(x)
    for pos_ref, side_ref in zip(refs[::2], refs[1::2]):
        n, q = pos_ref.shape[0], side_ref.shape[0] - 16
        out_width = q * in_width // n
        packed = side_ref[:q]
        coef = jnp.concatenate([packed[:, k : k + out_width] for k in range(0, in_width, out_width)])
        tail = side_ref[q:, :n].astype(F32)
        center_sq = tail[1:2] + tail[2:3] + tail[3:4]
        rate = tail[0:1] * (-2.0 * LOG2E / in_width)
        cross = lax.dot_general(x, pos_ref[...], NT, preferred_element_type=F32)
        power = (row_sq + center_sq - cross) * rate
        kernel = jnp.exp2(power).astype(BF16)
        new = jnp.dot(kernel, coef, preferred_element_type=F32)
        total = new if total is None else total + new
    return total


def own_values(pos_ref, spread_ref, refs):
    pos = pos_ref[...]
    center_sq = half_sq_column(pos)
    rate = column(spread_ref[...].astype(F32) * (-2.0 * LOG2E / pos.shape[1]))[:, :1]
    for ref in refs:
        step = min(256, ref.shape[0])
        for start in range(0, ref.shape[0], step):
            x = ref[start : start + step]
            cross = lax.dot_general(pos, x, NT, preferred_element_type=F32)
            power = (center_sq + half_sq_row(x) - cross) * rate
            yield jnp.exp2(power).astype(BF16)


def store_values(pos_ref, spread_ref, refs, out_ref):
    at = 0
    for part in own_values(pos_ref, spread_ref, refs):
        out_ref[:, at : at + part.shape[1]] = part
        at += part.shape[1]


def forward(rows, centers, out_width, cost):
    counts = [r.shape[0] for r in rows]

    def body(*refs):
        row_refs, refs, outs = refs[: len(rows)], refs[len(rows) : -len(rows)], refs[-len(rows) :]
        x = jnp.concatenate([ref[...] for ref in row_refs])
        total = partial_pred(x, refs, None)
        at = 0
        for ref, count in zip(outs, counts):
            ref[...] = total[at : at + count]
            at += count

    return pl.pallas_call(
        body,
        out_shape=tuple(jax.ShapeDtypeStruct((count, out_width), F32) for count in counts),
        in_specs=[VMEM] * (len(rows) + len(centers)),
        out_specs=(VMEM,) * len(rows),
        compiler_params=params(24),
        cost_estimate=cost,
        name="forward",
    )(*rows, *centers)


def own_kernel(center_pos, spread, blocks):
    n = spread.shape[1]
    points = sum(b.shape[0] for b in blocks)

    def body(pos_ref, spread_ref, *refs):
        store_values(pos_ref, spread_ref, refs[:-1], refs[-1])

    return pl.pallas_call(
        body,
        out_shape=jax.ShapeDtypeStruct((n, points), BF16),
        in_specs=[VMEM] * (2 + len(blocks)),
        out_specs=VMEM,
        compiler_params=params(16),
        cost_estimate=BRIEF,
        name="own_kernel",
    )(center_pos, spread, *blocks)


def own_rows(rows, centers, out_width, received, center_pos, spread, more):
    n = spread.shape[1]
    ends = [1, 1 + len(centers)]
    ends.append(ends[-1] + len(received))

    def body(*refs):
        outs, refs = refs[-1 - len(more) :], refs[: -1 - len(more)]
        total = None
        for ref in refs[ends[1] : ends[2]]:
            total = ref[...] if total is None else total + ref[...]
        outs[0][...] = partial_pred(refs[0][...], refs[1 : ends[1]], total)
        pos_ref, spread_ref, *block_refs = refs[ends[2] :]
        for k, blocks in enumerate(more):
            store_values(pos_ref, spread_ref, block_refs[: len(blocks)], outs[1 + k])
            del block_refs[: len(blocks)]

    ins = [rows, *centers, *received, center_pos, spread]
    ins += [block for blocks in more for block in blocks]
    return pl.pallas_call(
        body,
        out_shape=(jax.ShapeDtypeStruct((rows.shape[0], out_width), F32),)
        + tuple(jax.ShapeDtypeStruct((n, sum(b.shape[0] for b in blocks)), BF16) for blocks in more),
        in_specs=[VMEM] * len(ins),
        out_specs=(VMEM,) * (1 + len(more)),
        compiler_params=params(16),
        cost_estimate=COVER,
        name="own_rows",
    )(*ins)


def cotangent(parts, saved, target, delta):
    def body(*refs):
        saved_ref, target_ref, delta_ref, out_ref = refs[-4:]
        pred = refs[0][...]
        for ref in refs[1:-4]:
            pred += ref[...]
        residual = pred + saved_ref[...] - target_ref[...]
        ratio = residual / delta_ref[...]
        out_ref[...] = (residual / jnp.sqrt(1.0 + ratio * ratio)).astype(BF16)

    return pl.pallas_call(
        body,
        out_shape=jax.ShapeDtypeStruct(saved.shape, BF16),
        in_specs=[VMEM] * (len(parts) + 3),
        out_specs=VMEM,
        compiler_params=params(16),
        cost_estimate=BRIEF,
        name="cotangent",
    )(*parts, saved, target, delta)


def group_terms(coef, kernel, x, cot):
    mixing = lax.dot_general(coef, cot, NT, preferred_element_type=F32)
    weights = (kernel.astype(F32) * mixing).astype(BF16)
    lanes = weights[:, :128].astype(F32)
    for k in range(128, kernel.shape[1], 128):
        lanes += weights[:, k : k + 128].astype(F32)
    return (
        jnp.dot(weights, x, preferred_element_type=F32),
        jnp.dot(kernel, cot, preferred_element_type=F32),
        lanes,
    )


def backward(center_pos, coefficients, spread, groups, before=None, more=()):
    (n, out_width), in_width = coefficients.shape, center_pos.shape[1]
    flat = []
    for kernel, xs, cot in groups:
        flat += [*xs, cot] if kernel is None else [kernel, *xs, cot]
    carried = [] if before is None else list(before)
    outs = 3 + len(more)
    wanted = [block for blocks in more for block in blocks]

    def body(pos_ref, coef_ref, spread_ref, *refs):
        refs, out_refs = list(refs[:-outs]), refs[-outs:]
        coef = coef_ref[...]
        sums = [ref[...] for ref in refs[len(flat) : len(flat) + 3]] if carried else None
        block_refs = refs[len(flat) + len(carried) :]
        for k, blocks in enumerate(more):
            store_values(pos_ref, spread_ref, block_refs[: len(blocks)], out_refs[3 + k])
            del block_refs[: len(blocks)]
        for given, xs, _ in groups:
            kernel = None if given is None else refs.pop(0)[...]
            x_refs = [refs.pop(0) for _ in xs]
            if given is None:
                kernel = jnp.concatenate(list(own_values(pos_ref, spread_ref, x_refs)), axis=1)
            x = jnp.concatenate([ref[...] for ref in x_refs])
            terms = group_terms(coef, kernel, x, refs.pop(0)[...])
            sums = terms if sums is None else [a + b for a, b in zip(sums, terms)]
        for ref, value in zip(out_refs[:3], sums):
            ref[...] = value

    return pl.pallas_call(
        body,
        out_shape=tuple(jax.ShapeDtypeStruct((n, width), F32) for width in (in_width, out_width, 128))
        + tuple(jax.ShapeDtypeStruct((n, sum(b.shape[0] for b in blocks)), BF16) for blocks in more),
        in_specs=[VMEM] * (3 + len(flat) + len(carried) + len(wanted)),
        out_specs=(VMEM,) * outs,
        compiler_params=params(24),
        cost_estimate=COVER if more else BRIEF,
        name="backward",
    )(center_pos, coefficients, spread, *flat, *carried, *wanted)


def finish(center_pos, coefficients, spread, group, before):
    (n, out_width), in_width = coefficients.shape, center_pos.shape[1]
    kernel, xs, cot = group
    step = min(n, 256)

    def body(pos_ref, coef_ref, spread_ref, kernel_ref, cot_ref, *refs):
        x_refs, refs = refs[: len(xs)], refs[len(xs) :]
        moment_ref, grad_ref, lanes_ref, centers_out, coef_out, centers_buf, coef_buf, sems = refs
        x = jnp.concatenate([ref[...] for ref in x_refs])
        cot = cot_ref[...]
        scale = column(spread_ref[...].astype(F32)) * (2.0 / in_width)
        made = []
        for k, start in enumerate(range(0, n, step)):
            rows = slice(start, start + step)
            moment, grad, lanes = group_terms(coef_ref[rows], kernel_ref[rows], x, cot)
            coef_buf[rows] = grad_ref[rows] + grad
            moment += moment_ref[rows]
            total = jnp.sum(lanes_ref[rows] + lanes, axis=1, keepdims=True)
            for at in range(0, in_width, 128):
                pos = pos_ref[rows, at : at + 128].astype(F32)
                centers_buf[rows, at : at + 128] = scale[rows] * (moment[:, at : at + 128] - total * pos)
            pairs = [(centers_buf, centers_out), (coef_buf, coef_out)]
            for j, (src, dst) in enumerate(pairs):
                copy = pltpu.make_async_copy(src.at[rows], dst.at[rows], sems.at[2 * k + j])
                copy.start()
                made.append(copy)
        for copy in made:
            copy.wait()

    ins = [center_pos, coefficients, spread, kernel, cot, *xs, *before]
    return pl.pallas_call(
        body,
        out_shape=tuple(jax.ShapeDtypeStruct((n, width), F32) for width in (in_width, out_width)),
        in_specs=[VMEM] * len(ins),
        out_specs=(HBM, HBM),
        scratch_shapes=[
            pltpu.VMEM((n, in_width), F32),
            pltpu.VMEM((n, out_width), F32),
            pltpu.SemaphoreType.DMA((2 * pl.cdiv(n, step),)),
        ],
        compiler_params=params(24),
        cost_estimate=BRIEF,
        name="finish",
    )(*ins)


def solution(mesh):
    nz, nc = mesh.shape["points"], mesh.shape["centers"]

    def per_device(train_points, saved_preds, targets, huber_delta, center_pos, coefficients, spread):
        n_rows = train_points.shape[0]
        n, out_width = coefficients.shape
        piece = n_rows // nc

        own = lax.dynamic_slice_in_dim(train_points, lax.axis_index("centers") * piece, piece)

        layer = {0: own}
        for dz in range(2, nz, 2):
            layer[dz] = swap(own, "points", nz, dz)
        layer[1] = swap(own, "points", nz, 1)

        pos, side = {1: swap(center_pos, "centers", nc, 1)}, {}
        for d in range(2, nc, 2):
            pos[d] = swap(center_pos, "centers", nc, d)
        center_pos, side[0], delta, spread, coefficients = pack(
            after(center_pos, own), coefficients, spread, huber_delta
        )
        pos[0], side[1] = center_pos, swap(side[0], "centers", nc, 1)
        for d in range(2, nc, 2):
            side[d] = swap(side[0], "centers", nc, d)
        for dz in range(3, nz, 2):
            layer[dz] = swap(layer[dz - 1], "points", nz, 1)
        saved, target, *local = take(
            [saved_preds, targets] + [train_points] * (nc - 1), [0, 0, *range(1, nc)], piece
        )
        local = [own, *local]
        for d in range(2, nc, 2):
            pos[d + 1] = swap(after(pos[d], layer[1], saved), "centers", nc, 1)
            side[d + 1] = swap(after(side[d], layer[2], side[1]), "centers", nc, 1)
        centers = [a for d in range(nc) for a in (pos[d], side[d])]

        early = {0: jnp.concatenate([layer[dz] for dz in range(1, nz - 1)])}
        early[1] = swap(after(early[0], side[nc - 1]), "centers", nc, 1)

        first, second = [*range(2, nz, 2), 1], range(3, nz, 2)
        rows = [layer[dz] for dz in first]
        parts = dict(zip(first, forward(rows, centers, out_width, BRIEF)))
        rows = [after(layer[dz], *parts.values(), early[1]) for dz in second]
        received = {dz: swap(parts[dz], "points", nz, dz) for dz in first}
        parts.update(zip(second, forward(rows, centers, out_width, COVER)))
        soon = [received[dz] for dz in range(2, nz, 2)]
        received = [received[1]] + [swap(parts[dz], "points", nz, dz) for dz in second]
        last = parts[nz - 1]
        kernels, late = {1: None}, {0: layer[nz - 1]}
        parts[0], kernels[0] = own_rows(
            after(own, last),
            centers,
            out_width,
            soon,
            center_pos,
            spread,
            [[local[0], early[0], late[0]]],
        )
        for d in range(2, nc, 2):
            early[d] = swap(after(early[0], last), "centers", nc, d)
            late[d] = swap(after(late[0], parts[0]), "centers", nc, d)
            early[d + 1] = swap(after(early[d], parts[0]), "centers", nc, 1)
        late[1] = swap(after(late[0], parts[0]), "centers", nc, 1)
        cot = cotangent([parts[0], *received], saved, target, delta)

        far = {dz: swap(cot, "points", nz, dz) for dz in range(2, nz, 2)}
        far[1] = swap(cot, "points", nz, 1)
        far.update({dz: swap(far[dz - 1], "points", nz, 1) for dz in range(3, nz, 2)})
        ahead = {d: swap(cot, "centers", nc, d) for d in range(2, nc, 2)}
        far[1] = after(far[1], *ahead.values())
        far = jnp.concatenate([far[dz] for dz in range(1, nz)])
        cots = {0: jnp.concatenate([cot, far])}
        across = {}
        for d in range(2, nc, 2):
            across[d] = [ahead[d], swap(far, "centers", nc, d)]
            late[d + 1] = swap(after(late[d], far), "centers", nc, 1)
        cots[1] = swap(cots[0], "centers", nc, 1)

        points = {d: [local[d], early[d], late[d]] for d in range(nc)}
        groups = [(kernels[d], points[d], cots[d]) for d in (0, 1)]
        *sums, kernels[2], kernels[3] = backward(
            center_pos, coefficients, spread, groups, more=[points[2], points[3]]
        )
        for d in range(4, nc):
            kernels[d] = own_kernel(center_pos, spread, points[d])
        for d in range(2, nc, 2):
            cots[d] = jnp.concatenate([after(a, sums[0]) for a in across[d]])
            cots[d + 1] = swap(cots[d], "centers", nc, 1)
        for d in range(2, nc - 1):
            group = (kernels[d], points[d], cots[d])
            sums = backward(center_pos, coefficients, spread, [group], before=sums)
        group = (kernels[nc - 1], points[nc - 1], cots[nc - 1])
        return finish(center_pos, coefficients, spread, group, sums)

    return jax.shard_map(
        per_device,
        mesh=mesh,
        in_specs=(
            P(("groups", "points"), None),
            P(("groups", "points"), None),
            P(("groups", "points"), None),
            P("groups"),
            P(("groups", "points", "centers"), None),
            P(("groups", "points", "centers"), None),
            P(("groups", "points", "centers")),
        ),
        out_specs=(
            P(("groups", "points", "centers"), None),
            P(("groups", "points", "centers"), None),
        ),
        check_vma=False,
    )
```

```python
import math

import jax
import jax.numpy as jnp
from jax import lax
from jax.experimental import pallas as pl
from jax.experimental.pallas import tpu as pltpu
from jax.sharding import PartitionSpec as P

F32, BF16 = jnp.float32, jnp.bfloat16
HBM = pl.BlockSpec(memory_space=pltpu.HBM)
VMEM = pl.BlockSpec(memory_space=pltpu.VMEM)
NT = (((1,), (1,)), ((), ()))
LOG2E = math.log2(math.e)
COVER = pl.CostEstimate(flops=1 << 34, bytes_accessed=1 << 20, transcendentals=1 << 20)
BRIEF = pl.CostEstimate(flops=1, bytes_accessed=1, transcendentals=0)


def swap(a, axis, size, d):
    return lax.ppermute(a, axis, [(i, i ^ d) for i in range(size)])


def after(a, *others):
    return lax.optimization_barrier((a, *others))[0]


def lane_groups(a):
    total = None
    for k in range(0, a.shape[1], 128):
        part = jnp.square(a[:, k : k + 128].astype(F32))
        total = part if total is None else total + part
    return total


def half_sq_row(a):
    return 0.5 * jnp.sum(lane_groups(a).T, axis=0, keepdims=True)


def half_sq_column(a):
    return 0.5 * jnp.sum(lane_groups(a), axis=1, keepdims=True)


def column(row):
    return jnp.broadcast_to(row, (128, row.shape[1])).T


def params(mib):
    return pltpu.CompilerParams(vmem_limit_bytes=mib << 20)


def pack(center_pos, coefficients, spread, delta):
    n, in_width = center_pos.shape
    out_width = coefficients.shape[1]
    across = in_width // out_width
    q = n // across

    def body(pos_ref, coef_ref, spread_ref, delta_ref, own_pos, out_ref, row_ref, own_spread, own_coef):
        row_ref[...] = delta_ref[...]
        own_spread[...] = spread_ref[...]
        own_coef[...] = coef_ref[...]
        pos = pos_ref[...]
        own_pos[...] = pos
        for k in range(across):
            out_ref[:q, k * out_width : (k + 1) * out_width] = coef_ref[k * q : (k + 1) * q]
        half = half_sq_row(pos)
        high = half.astype(BF16)
        rest = half - high.astype(F32)
        middle = rest.astype(BF16)
        low = (rest - middle.astype(F32)).astype(BF16)
        rows = [r.astype(F32) for r in (spread_ref[...], high, middle, low)]
        tail = jnp.concatenate(rows + [jnp.zeros((12, n), F32)]).astype(BF16)
        if n < in_width:
            tail = jnp.concatenate([tail, jnp.zeros((16, in_width - n), BF16)], axis=1)
        out_ref[q:] = tail

    return pl.pallas_call(
        body,
        out_shape=(
            jax.ShapeDtypeStruct((n, in_width), BF16),
            jax.ShapeDtypeStruct((q + 16, in_width), BF16),
            jax.ShapeDtypeStruct((1, delta.shape[0]), F32),
            jax.ShapeDtypeStruct((1, n), BF16),
            jax.ShapeDtypeStruct((n, out_width), BF16),
        ),
        in_specs=[VMEM] * 4,
        out_specs=(VMEM,) * 5,
        compiler_params=params(16),
        cost_estimate=BRIEF,
        name="pack",
    )(center_pos, coefficients, spread.reshape(1, n), delta.reshape(1, -1))


def take(arrays, offsets, piece):
    def body(*refs):
        ins, outs, sems = refs[: len(arrays)], refs[len(arrays) : -1], refs[-1]
        made = []
        for k, d in enumerate(offsets):
            start = pl.multiple_of((lax.axis_index("centers") ^ d) * piece, piece)
            made.append(pltpu.make_async_copy(ins[k].at[pl.ds(start, piece)], outs[k], sems.at[k]))
            made[-1].start()
        for copy in made:
            copy.wait()

    return pl.pallas_call(
        body,
        out_shape=tuple(jax.ShapeDtypeStruct((piece, a.shape[1]), a.dtype) for a in arrays),
        in_specs=[HBM] * len(arrays),
        out_specs=(VMEM,) * len(arrays),
        scratch_shapes=[pltpu.SemaphoreType.DMA((len(arrays),))],
        compiler_params=params(16),
        cost_estimate=BRIEF,
        name="take",
    )(*arrays)


def partial_pred(x, refs, total):
    in_width = x.shape[1]
    row_sq = half_sq_column(x)
    for pos_ref, side_ref in zip(refs[::2], refs[1::2]):
        n, q = pos_ref.shape[0], side_ref.shape[0] - 16
        out_width = q * in_width // n
        packed = side_ref[:q]
        coef = jnp.concatenate([packed[:, k : k + out_width] for k in range(0, in_width, out_width)])
        tail = side_ref[q:, :n].astype(F32)
        center_sq = tail[1:2] + tail[2:3] + tail[3:4]
        rate = tail[0:1] * (-2.0 * LOG2E / in_width)
        cross = lax.dot_general(x, pos_ref[...], NT, preferred_element_type=F32)
        power = (row_sq + center_sq - cross) * rate
        kernel = jnp.exp2(power).astype(BF16)
        new = jnp.dot(kernel, coef, preferred_element_type=F32)
        total = new if total is None else total + new
    return total


def own_values(pos_ref, spread_ref, refs):
    pos = pos_ref[...]
    center_sq = half_sq_column(pos)
    rate = column(spread_ref[...].astype(F32) * (-2.0 * LOG2E / pos.shape[1]))[:, :1]
    for ref in refs:
        step = min(256, ref.shape[0])
        for start in range(0, ref.shape[0], step):
            x = ref[start : start + step]
            cross = lax.dot_general(pos, x, NT, preferred_element_type=F32)
            power = (center_sq + half_sq_row(x) - cross) * rate
            yield jnp.exp2(power).astype(BF16)


def store_values(pos_ref, spread_ref, refs, out_ref):
    at = 0
    for part in own_values(pos_ref, spread_ref, refs):
        out_ref[:, at : at + part.shape[1]] = part
        at += part.shape[1]


def forward(rows, centers, out_width, cost):
    counts = [r.shape[0] for r in rows]

    def body(*refs):
        row_refs, refs, outs = refs[: len(rows)], refs[len(rows) : -len(rows)], refs[-len(rows) :]
        x = jnp.concatenate([ref[...] for ref in row_refs])
        total = partial_pred(x, refs, None)
        at = 0
        for ref, count in zip(outs, counts):
            ref[...] = total[at : at + count]
            at += count

    return pl.pallas_call(
        body,
        out_shape=tuple(jax.ShapeDtypeStruct((count, out_width), F32) for count in counts),
        in_specs=[VMEM] * (len(rows) + len(centers)),
        out_specs=(VMEM,) * len(rows),
        compiler_params=params(24),
        cost_estimate=cost,
        name="forward",
    )(*rows, *centers)


def own_kernel(center_pos, spread, blocks):
    n = spread.shape[1]
    points = sum(b.shape[0] for b in blocks)

    def body(pos_ref, spread_ref, *refs):
        store_values(pos_ref, spread_ref, refs[:-1], refs[-1])

    return pl.pallas_call(
        body,
        out_shape=jax.ShapeDtypeStruct((n, points), BF16),
        in_specs=[VMEM] * (2 + len(blocks)),
        out_specs=VMEM,
        compiler_params=params(16),
        cost_estimate=BRIEF,
        name="own_kernel",
    )(center_pos, spread, *blocks)


def own_rows(rows, centers, out_width, received, center_pos, spread, more):
    n = spread.shape[1]
    ends = [1, 1 + len(centers)]
    ends.append(ends[-1] + len(received))

    def body(*refs):
        outs, refs = refs[-1 - len(more) :], refs[: -1 - len(more)]
        total = None
        for ref in refs[ends[1] : ends[2]]:
            total = ref[...] if total is None else total + ref[...]
        outs[0][...] = partial_pred(refs[0][...], refs[1 : ends[1]], total)
        pos_ref, spread_ref, *block_refs = refs[ends[2] :]
        for k, blocks in enumerate(more):
            store_values(pos_ref, spread_ref, block_refs[: len(blocks)], outs[1 + k])
            del block_refs[: len(blocks)]

    ins = [rows, *centers, *received, center_pos, spread]
    ins += [block for blocks in more for block in blocks]
    return pl.pallas_call(
        body,
        out_shape=(jax.ShapeDtypeStruct((rows.shape[0], out_width), F32),)
        + tuple(jax.ShapeDtypeStruct((n, sum(b.shape[0] for b in blocks)), BF16) for blocks in more),
        in_specs=[VMEM] * len(ins),
        out_specs=(VMEM,) * (1 + len(more)),
        compiler_params=params(16),
        cost_estimate=COVER,
        name="own_rows",
    )(*ins)


def cotangent(parts, saved, target, delta):
    def body(*refs):
        saved_ref, target_ref, delta_ref, out_ref = refs[-4:]
        pred = refs[0][...]
        for ref in refs[1:-4]:
            pred += ref[...]
        residual = pred + saved_ref[...] - target_ref[...]
        ratio = residual / delta_ref[...]
        out_ref[...] = (residual / jnp.sqrt(1.0 + ratio * ratio)).astype(BF16)

    return pl.pallas_call(
        body,
        out_shape=jax.ShapeDtypeStruct(saved.shape, BF16),
        in_specs=[VMEM] * (len(parts) + 3),
        out_specs=VMEM,
        compiler_params=params(16),
        cost_estimate=BRIEF,
        name="cotangent",
    )(*parts, saved, target, delta)


def group_terms(coef, kernel, x, cot):
    mixing = lax.dot_general(coef, cot, NT, preferred_element_type=F32)
    weights = (kernel.astype(F32) * mixing).astype(BF16)
    lanes = weights[:, :128].astype(F32)
    for k in range(128, kernel.shape[1], 128):
        lanes += weights[:, k : k + 128].astype(F32)
    return (
        jnp.dot(weights, x, preferred_element_type=F32),
        jnp.dot(kernel, cot, preferred_element_type=F32),
        lanes,
    )


def backward(center_pos, coefficients, spread, groups, before=None, more=()):
    (n, out_width), in_width = coefficients.shape, center_pos.shape[1]
    flat = []
    for kernel, xs, cot in groups:
        flat += [*xs, cot] if kernel is None else [kernel, *xs, cot]
    carried = [] if before is None else list(before)
    outs = 3 + len(more)
    wanted = [block for blocks in more for block in blocks]

    def body(pos_ref, coef_ref, spread_ref, *refs):
        refs, out_refs = list(refs[:-outs]), refs[-outs:]
        coef = coef_ref[...]
        sums = [ref[...] for ref in refs[len(flat) : len(flat) + 3]] if carried else None
        block_refs = refs[len(flat) + len(carried) :]
        for k, blocks in enumerate(more):
            store_values(pos_ref, spread_ref, block_refs[: len(blocks)], out_refs[3 + k])
            del block_refs[: len(blocks)]
        for given, xs, _ in groups:
            kernel = None if given is None else refs.pop(0)[...]
            x_refs = [refs.pop(0) for _ in xs]
            if given is None:
                kernel = jnp.concatenate(list(own_values(pos_ref, spread_ref, x_refs)), axis=1)
            x = jnp.concatenate([ref[...] for ref in x_refs])
            terms = group_terms(coef, kernel, x, refs.pop(0)[...])
            sums = terms if sums is None else [a + b for a, b in zip(sums, terms)]
        for ref, value in zip(out_refs[:3], sums):
            ref[...] = value

    return pl.pallas_call(
        body,
        out_shape=tuple(jax.ShapeDtypeStruct((n, width), F32) for width in (in_width, out_width, 128))
        + tuple(jax.ShapeDtypeStruct((n, sum(b.shape[0] for b in blocks)), BF16) for blocks in more),
        in_specs=[VMEM] * (3 + len(flat) + len(carried) + len(wanted)),
        out_specs=(VMEM,) * outs,
        compiler_params=params(24),
        cost_estimate=COVER if more else BRIEF,
        name="backward",
    )(center_pos, coefficients, spread, *flat, *carried, *wanted)


def finish(center_pos, coefficients, spread, group, before):
    (n, out_width), in_width = coefficients.shape, center_pos.shape[1]
    kernel, xs, cot = group
    step = min(n, 256)

    def body(pos_ref, coef_ref, spread_ref, kernel_ref, cot_ref, *refs):
        x_refs, refs = refs[: len(xs)], refs[len(xs) :]
        moment_ref, grad_ref, lanes_ref, centers_out, coef_out, centers_buf, coef_buf, sems = refs
        x = jnp.concatenate([ref[...] for ref in x_refs])
        cot = cot_ref[...]
        scale = column(spread_ref[...].astype(F32)) * (2.0 / in_width)
        made = []
        for k, start in enumerate(range(0, n, step)):
            rows = slice(start, start + step)
            moment, grad, lanes = group_terms(coef_ref[rows], kernel_ref[rows], x, cot)
            coef_buf[rows] = grad_ref[rows] + grad
            moment += moment_ref[rows]
            total = jnp.sum(lanes_ref[rows] + lanes, axis=1, keepdims=True)
            for at in range(0, in_width, 128):
                pos = pos_ref[rows, at : at + 128].astype(F32)
                centers_buf[rows, at : at + 128] = scale[rows] * (moment[:, at : at + 128] - total * pos)
            pairs = [(centers_buf, centers_out), (coef_buf, coef_out)]
            for j, (src, dst) in enumerate(pairs):
                copy = pltpu.make_async_copy(src.at[rows], dst.at[rows], sems.at[2 * k + j])
                copy.start()
                made.append(copy)
        for copy in made:
            copy.wait()

    ins = [center_pos, coefficients, spread, kernel, cot, *xs, *before]
    return pl.pallas_call(
        body,
        out_shape=tuple(jax.ShapeDtypeStruct((n, width), F32) for width in (in_width, out_width)),
        in_specs=[VMEM] * len(ins),
        out_specs=(HBM, HBM),
        scratch_shapes=[
            pltpu.VMEM((n, in_width), F32),
            pltpu.VMEM((n, out_width), F32),
            pltpu.SemaphoreType.DMA((2 * pl.cdiv(n, step),)),
        ],
        compiler_params=params(24),
        cost_estimate=BRIEF,
        name="finish",
    )(*ins)


def solution(mesh):
    nz, nc = mesh.shape["points"], mesh.shape["centers"]

    def per_device(train_points, saved_preds, targets, huber_delta, center_pos, coefficients, spread):
        n_rows = train_points.shape[0]
        n, out_width = coefficients.shape
        piece = n_rows // nc

        own = lax.dynamic_slice_in_dim(train_points, lax.axis_index("centers") * piece, piece)

        layer = {0: own}
        for dz in range(2, nz, 2):
            layer[dz] = swap(own, "points", nz, dz)
        layer[1] = swap(own, "points", nz, 1)

        pos, side = {1: swap(center_pos, "centers", nc, 1)}, {}
        for d in range(2, nc, 2):
            pos[d] = swap(center_pos, "centers", nc, d)
        center_pos, side[0], delta, spread, coefficients = pack(
            after(center_pos, own), coefficients, spread, huber_delta
        )
        pos[0], side[1] = center_pos, swap(side[0], "centers", nc, 1)
        for d in range(2, nc, 2):
            side[d] = swap(side[0], "centers", nc, d)
        for dz in range(3, nz, 2):
            layer[dz] = swap(layer[dz - 1], "points", nz, 1)
        saved, target, *local = take(
            [saved_preds, targets] + [train_points] * (nc - 1), [0, 0, *range(1, nc)], piece
        )
        local = [own, *local]
        for d in range(2, nc, 2):
            pos[d + 1] = swap(after(pos[d], layer[1], saved), "centers", nc, 1)
            side[d + 1] = swap(after(side[d], layer[2], side[1]), "centers", nc, 1)
        centers = [a for d in range(nc) for a in (pos[d], side[d])]

        early = {0: jnp.concatenate([layer[dz] for dz in range(1, nz - 1)])}
        early[1] = swap(after(early[0], side[nc - 1]), "centers", nc, 1)

        first, second = [*range(2, nz, 2), 1], range(3, nz, 2)
        rows = [layer[dz] for dz in first]
        parts = dict(zip(first, forward(rows, centers, out_width, BRIEF)))
        rows = [after(layer[dz], *parts.values(), early[1]) for dz in second]
        received = {dz: swap(parts[dz], "points", nz, dz) for dz in first}
        parts.update(zip(second, forward(rows, centers, out_width, COVER)))
        soon = [received[dz] for dz in range(2, nz, 2)]
        received = [received[1]] + [swap(parts[dz], "points", nz, dz) for dz in second]
        last = parts[nz - 1]
        kernels, late = {1: None}, {0: layer[nz - 1]}
        parts[0], kernels[0] = own_rows(
            after(own, last),
            centers,
            out_width,
            soon,
            center_pos,
            spread,
            [[local[0], early[0], late[0]]],
        )
        for d in range(2, nc, 2):
            early[d] = swap(after(early[0], side[d]), "centers", nc, d)
            late[d] = swap(after(late[0], last, *soon), "centers", nc, d)
            early[d + 1] = swap(after(early[d], parts[0]), "centers", nc, 1)
        late[1] = swap(after(late[0], parts[0]), "centers", nc, 1)
        cot = cotangent([parts[0], *received], saved, target, delta)

        far = {dz: swap(cot, "points", nz, dz) for dz in range(2, nz, 2)}
        far[1] = swap(cot, "points", nz, 1)
        far.update({dz: swap(far[dz - 1], "points", nz, 1) for dz in range(3, nz, 2)})
        ahead = {d: swap(after(cot, late[d]), "centers", nc, d) for d in range(2, nc, 2)}
        far[1] = after(far[1], *ahead.values())
        far = jnp.concatenate([far[dz] for dz in range(1, nz)])
        cots = {0: jnp.concatenate([cot, far])}
        across = {}
        for d in range(2, nc, 2):
            across[d] = [ahead[d], swap(far, "centers", nc, d)]
            late[d + 1] = swap(after(late[d], far), "centers", nc, 1)
        cots[1] = swap(cots[0], "centers", nc, 1)

        points = {d: [local[d], early[d], late[d]] for d in range(nc)}
        groups = [(kernels[d], points[d], cots[d]) for d in (0, 1)]
        *sums, kernels[2], kernels[3] = backward(
            center_pos, coefficients, spread, groups, more=[points[2], points[3]]
        )
        for d in range(4, nc):
            kernels[d] = own_kernel(center_pos, spread, points[d])
        for d in range(2, nc, 2):
            cots[d] = jnp.concatenate([after(a, sums[0]) for a in across[d]])
            cots[d + 1] = swap(cots[d], "centers", nc, 1)
        for d in range(2, nc - 1):
            group = (kernels[d], points[d], cots[d])
            sums = backward(center_pos, coefficients, spread, [group], before=sums)
        group = (kernels[nc - 1], points[nc - 1], cots[nc - 1])
        return finish(center_pos, coefficients, spread, group, sums)

    return jax.shard_map(
        per_device,
        mesh=mesh,
        in_specs=(
            P(("groups", "points"), None),
            P(("groups", "points"), None),
            P(("groups", "points"), None),
            P("groups"),
            P(("groups", "points", "centers"), None),
            P(("groups", "points", "centers"), None),
            P(("groups", "points", "centers")),
        ),
        out_specs=(
            P(("groups", "points", "centers"), None),
            P(("groups", "points", "centers"), None),
        ),
        check_vma=False,
    )
```

```python
import math

import jax
import jax.numpy as jnp
from jax import lax
from jax.experimental import pallas as pl
from jax.experimental.pallas import tpu as pltpu
from jax.sharding import PartitionSpec as P

F32, BF16 = jnp.float32, jnp.bfloat16
HBM = pl.BlockSpec(memory_space=pltpu.HBM)
VMEM = pl.BlockSpec(memory_space=pltpu.VMEM)
NT = (((1,), (1,)), ((), ()))
LOG2E = math.log2(math.e)
COVER = pl.CostEstimate(flops=1 << 34, bytes_accessed=1 << 20, transcendentals=1 << 20)
BRIEF = pl.CostEstimate(flops=1, bytes_accessed=1, transcendentals=0)


def swap(a, axis, size, d):
    return lax.ppermute(a, axis, [(i, i ^ d) for i in range(size)])


def after(a, *others):
    return lax.optimization_barrier((a, *others))[0]


def lane_groups(a):
    total = None
    for k in range(0, a.shape[1], 128):
        part = jnp.square(a[:, k : k + 128].astype(F32))
        total = part if total is None else total + part
    return total


def half_sq_row(a):
    return 0.5 * jnp.sum(lane_groups(a).T, axis=0, keepdims=True)


def half_sq_column(a):
    return 0.5 * jnp.sum(lane_groups(a), axis=1, keepdims=True)


def column(row):
    return jnp.broadcast_to(row, (128, row.shape[1])).T


def params(mib):
    return pltpu.CompilerParams(vmem_limit_bytes=mib << 20)


def pack(center_pos, coefficients, spread, delta):
    n, in_width = center_pos.shape
    out_width = coefficients.shape[1]
    across = in_width // out_width
    q = n // across

    def body(pos_ref, coef_ref, spread_ref, delta_ref, own_pos, out_ref, row_ref, own_spread, own_coef):
        row_ref[...] = delta_ref[...]
        own_spread[...] = spread_ref[...]
        own_coef[...] = coef_ref[...]
        pos = pos_ref[...]
        own_pos[...] = pos
        for k in range(across):
            out_ref[:q, k * out_width : (k + 1) * out_width] = coef_ref[k * q : (k + 1) * q]
        half = half_sq_row(pos)
        high = half.astype(BF16)
        rest = half - high.astype(F32)
        middle = rest.astype(BF16)
        low = (rest - middle.astype(F32)).astype(BF16)
        rows = [r.astype(F32) for r in (spread_ref[...], high, middle, low)]
        tail = jnp.concatenate(rows + [jnp.zeros((12, n), F32)]).astype(BF16)
        if n < in_width:
            tail = jnp.concatenate([tail, jnp.zeros((16, in_width - n), BF16)], axis=1)
        out_ref[q:] = tail

    return pl.pallas_call(
        body,
        out_shape=(
            jax.ShapeDtypeStruct((n, in_width), BF16),
            jax.ShapeDtypeStruct((q + 16, in_width), BF16),
            jax.ShapeDtypeStruct((1, delta.shape[0]), F32),
            jax.ShapeDtypeStruct((1, n), BF16),
            jax.ShapeDtypeStruct((n, out_width), BF16),
        ),
        in_specs=[VMEM] * 4,
        out_specs=(VMEM,) * 5,
        compiler_params=params(16),
        cost_estimate=BRIEF,
        name="pack",
    )(center_pos, coefficients, spread.reshape(1, n), delta.reshape(1, -1))


def take(arrays, offsets, piece):
    def body(*refs):
        ins, outs, sems = refs[: len(arrays)], refs[len(arrays) : -1], refs[-1]
        made = []
        for k, d in enumerate(offsets):
            start = pl.multiple_of((lax.axis_index("centers") ^ d) * piece, piece)
            made.append(pltpu.make_async_copy(ins[k].at[pl.ds(start, piece)], outs[k], sems.at[k]))
            made[-1].start()
        for copy in made:
            copy.wait()

    return pl.pallas_call(
        body,
        out_shape=tuple(jax.ShapeDtypeStruct((piece, a.shape[1]), a.dtype) for a in arrays),
        in_specs=[HBM] * len(arrays),
        out_specs=(VMEM,) * len(arrays),
        scratch_shapes=[pltpu.SemaphoreType.DMA((len(arrays),))],
        compiler_params=params(16),
        cost_estimate=BRIEF,
        name="take",
    )(*arrays)


def partial_pred(x, refs, total):
    in_width = x.shape[1]
    row_sq = half_sq_column(x)
    for pos_ref, side_ref in zip(refs[::2], refs[1::2]):
        n, q = pos_ref.shape[0], side_ref.shape[0] - 16
        out_width = q * in_width // n
        packed = side_ref[:q]
        coef = jnp.concatenate([packed[:, k : k + out_width] for k in range(0, in_width, out_width)])
        tail = side_ref[q:, :n].astype(F32)
        center_sq = tail[1:2] + tail[2:3] + tail[3:4]
        rate = tail[0:1] * (-2.0 * LOG2E / in_width)
        cross = lax.dot_general(x, pos_ref[...], NT, preferred_element_type=F32)
        power = (row_sq + center_sq - cross) * rate
        kernel = jnp.exp2(power).astype(BF16)
        new = jnp.dot(kernel, coef, preferred_element_type=F32)
        total = new if total is None else total + new
    return total


def own_values(pos_ref, spread_ref, refs):
    pos = pos_ref[...]
    center_sq = half_sq_column(pos)
    rate = column(spread_ref[...].astype(F32) * (-2.0 * LOG2E / pos.shape[1]))[:, :1]
    for ref in refs:
        step = min(256, ref.shape[0])
        for start in range(0, ref.shape[0], step):
            x = ref[start : start + step]
            cross = lax.dot_general(pos, x, NT, preferred_element_type=F32)
            power = (center_sq + half_sq_row(x) - cross) * rate
            yield jnp.exp2(power).astype(BF16)


def store_values(pos_ref, spread_ref, refs, out_ref):
    at = 0
    for part in own_values(pos_ref, spread_ref, refs):
        out_ref[:, at : at + part.shape[1]] = part
        at += part.shape[1]


def forward(rows, centers, out_width, cost):
    counts = [r.shape[0] for r in rows]

    def body(*refs):
        row_refs, refs, outs = refs[: len(rows)], refs[len(rows) : -len(rows)], refs[-len(rows) :]
        x = jnp.concatenate([ref[...] for ref in row_refs])
        total = partial_pred(x, refs, None)
        at = 0
        for ref, count in zip(outs, counts):
            ref[...] = total[at : at + count]
            at += count

    return pl.pallas_call(
        body,
        out_shape=tuple(jax.ShapeDtypeStruct((count, out_width), F32) for count in counts),
        in_specs=[VMEM] * (len(rows) + len(centers)),
        out_specs=(VMEM,) * len(rows),
        compiler_params=params(24),
        cost_estimate=cost,
        name="forward",
    )(*rows, *centers)


def own_kernel(center_pos, spread, blocks):
    n = spread.shape[1]
    points = sum(b.shape[0] for b in blocks)

    def body(pos_ref, spread_ref, *refs):
        store_values(pos_ref, spread_ref, refs[:-1], refs[-1])

    return pl.pallas_call(
        body,
        out_shape=jax.ShapeDtypeStruct((n, points), BF16),
        in_specs=[VMEM] * (2 + len(blocks)),
        out_specs=VMEM,
        compiler_params=params(16),
        cost_estimate=BRIEF,
        name="own_kernel",
    )(center_pos, spread, *blocks)


def own_rows(rows, centers, out_width, received, center_pos, spread, more):
    n = spread.shape[1]
    ends = [1, 1 + len(centers)]
    ends.append(ends[-1] + len(received))

    def body(*refs):
        outs, refs = refs[-1 - len(more) :], refs[: -1 - len(more)]
        total = None
        for ref in refs[ends[1] : ends[2]]:
            total = ref[...] if total is None else total + ref[...]
        outs[0][...] = partial_pred(refs[0][...], refs[1 : ends[1]], total)
        pos_ref, spread_ref, *block_refs = refs[ends[2] :]
        for k, blocks in enumerate(more):
            store_values(pos_ref, spread_ref, block_refs[: len(blocks)], outs[1 + k])
            del block_refs[: len(blocks)]

    ins = [rows, *centers, *received, center_pos, spread]
    ins += [block for blocks in more for block in blocks]
    return pl.pallas_call(
        body,
        out_shape=(jax.ShapeDtypeStruct((rows.shape[0], out_width), F32),)
        + tuple(jax.ShapeDtypeStruct((n, sum(b.shape[0] for b in blocks)), BF16) for blocks in more),
        in_specs=[VMEM] * len(ins),
        out_specs=(VMEM,) * (1 + len(more)),
        compiler_params=params(16),
        cost_estimate=COVER,
        name="own_rows",
    )(*ins)


def cotangent(parts, saved, target, delta):
    def body(*refs):
        saved_ref, target_ref, delta_ref, out_ref = refs[-4:]
        pred = refs[0][...]
        for ref in refs[1:-4]:
            pred += ref[...]
        residual = pred + saved_ref[...] - target_ref[...]
        ratio = residual / delta_ref[...]
        out_ref[...] = (residual / jnp.sqrt(1.0 + ratio * ratio)).astype(BF16)

    return pl.pallas_call(
        body,
        out_shape=jax.ShapeDtypeStruct(saved.shape, BF16),
        in_specs=[VMEM] * (len(parts) + 3),
        out_specs=VMEM,
        compiler_params=params(16),
        cost_estimate=BRIEF,
        name="cotangent",
    )(*parts, saved, target, delta)


def group_terms(coef, kernel, x, cot):
    mixing = lax.dot_general(coef, cot, NT, preferred_element_type=F32)
    weights = (kernel.astype(F32) * mixing).astype(BF16)
    lanes = weights[:, :128].astype(F32)
    for k in range(128, kernel.shape[1], 128):
        lanes += weights[:, k : k + 128].astype(F32)
    return (
        jnp.dot(weights, x, preferred_element_type=F32),
        jnp.dot(kernel, cot, preferred_element_type=F32),
        lanes,
    )


def backward(center_pos, coefficients, spread, groups, before=None, more=()):
    (n, out_width), in_width = coefficients.shape, center_pos.shape[1]
    flat = []
    for kernel, xs, cot in groups:
        flat += [*xs, cot] if kernel is None else [kernel, *xs, cot]
    carried = [] if before is None else list(before)
    outs = 3 + len(more)
    wanted = [block for blocks in more for block in blocks]

    def body(pos_ref, coef_ref, spread_ref, *refs):
        refs, out_refs = list(refs[:-outs]), refs[-outs:]
        coef = coef_ref[...]
        sums = [ref[...] for ref in refs[len(flat) : len(flat) + 3]] if carried else None
        block_refs = refs[len(flat) + len(carried) :]
        for k, blocks in enumerate(more):
            store_values(pos_ref, spread_ref, block_refs[: len(blocks)], out_refs[3 + k])
            del block_refs[: len(blocks)]
        for given, xs, _ in groups:
            kernel = None if given is None else refs.pop(0)[...]
            x_refs = [refs.pop(0) for _ in xs]
            if given is None:
                kernel = jnp.concatenate(list(own_values(pos_ref, spread_ref, x_refs)), axis=1)
            x = jnp.concatenate([ref[...] for ref in x_refs])
            terms = group_terms(coef, kernel, x, refs.pop(0)[...])
            sums = terms if sums is None else [a + b for a, b in zip(sums, terms)]
        for ref, value in zip(out_refs[:3], sums):
            ref[...] = value

    return pl.pallas_call(
        body,
        out_shape=tuple(jax.ShapeDtypeStruct((n, width), F32) for width in (in_width, out_width, 128))
        + tuple(jax.ShapeDtypeStruct((n, sum(b.shape[0] for b in blocks)), BF16) for blocks in more),
        in_specs=[VMEM] * (3 + len(flat) + len(carried) + len(wanted)),
        out_specs=(VMEM,) * outs,
        compiler_params=params(24),
        cost_estimate=COVER if more else BRIEF,
        name="backward",
    )(center_pos, coefficients, spread, *flat, *carried, *wanted)


def finish(center_pos, coefficients, spread, group, before):
    (n, out_width), in_width = coefficients.shape, center_pos.shape[1]
    kernel, xs, cot = group
    step = min(n, 256)

    def body(pos_ref, coef_ref, spread_ref, kernel_ref, cot_ref, *refs):
        x_refs, refs = refs[: len(xs)], refs[len(xs) :]
        moment_ref, grad_ref, lanes_ref, centers_out, coef_out, centers_buf, coef_buf, sems = refs
        x = jnp.concatenate([ref[...] for ref in x_refs])
        cot = cot_ref[...]
        scale = column(spread_ref[...].astype(F32)) * (2.0 / in_width)
        made = []
        for k, start in enumerate(range(0, n, step)):
            rows = slice(start, start + step)
            moment, grad, lanes = group_terms(coef_ref[rows], kernel_ref[rows], x, cot)
            coef_buf[rows] = grad_ref[rows] + grad
            moment += moment_ref[rows]
            total = jnp.sum(lanes_ref[rows] + lanes, axis=1, keepdims=True)
            for at in range(0, in_width, 128):
                pos = pos_ref[rows, at : at + 128].astype(F32)
                centers_buf[rows, at : at + 128] = scale[rows] * (moment[:, at : at + 128] - total * pos)
            pairs = [(centers_buf, centers_out), (coef_buf, coef_out)]
            for j, (src, dst) in enumerate(pairs):
                copy = pltpu.make_async_copy(src.at[rows], dst.at[rows], sems.at[2 * k + j])
                copy.start()
                made.append(copy)
        for copy in made:
            copy.wait()

    ins = [center_pos, coefficients, spread, kernel, cot, *xs, *before]
    return pl.pallas_call(
        body,
        out_shape=tuple(jax.ShapeDtypeStruct((n, width), F32) for width in (in_width, out_width)),
        in_specs=[VMEM] * len(ins),
        out_specs=(HBM, HBM),
        scratch_shapes=[
            pltpu.VMEM((n, in_width), F32),
            pltpu.VMEM((n, out_width), F32),
            pltpu.SemaphoreType.DMA((2 * pl.cdiv(n, step),)),
        ],
        compiler_params=params(24),
        cost_estimate=BRIEF,
        name="finish",
    )(*ins)


def solution(mesh):
    nz, nc = mesh.shape["points"], mesh.shape["centers"]

    def per_device(train_points, saved_preds, targets, huber_delta, center_pos, coefficients, spread):
        n_rows = train_points.shape[0]
        n, out_width = coefficients.shape
        piece = n_rows // nc

        own = lax.dynamic_slice_in_dim(train_points, lax.axis_index("centers") * piece, piece)

        layer = {0: own}
        for dz in range(2, nz, 2):
            layer[dz] = swap(own, "points", nz, dz)
        layer[1] = swap(own, "points", nz, 1)

        pos, side = {1: swap(center_pos, "centers", nc, 1)}, {}
        for d in range(2, nc, 2):
            pos[d] = swap(center_pos, "centers", nc, d)
        center_pos, side[0], delta, spread, coefficients = pack(
            after(center_pos, own), coefficients, spread, huber_delta
        )
        pos[0], side[1] = center_pos, swap(side[0], "centers", nc, 1)
        for d in range(2, nc, 2):
            side[d] = swap(side[0], "centers", nc, d)
        for dz in range(3, nz, 2):
            layer[dz] = swap(layer[dz - 1], "points", nz, 1)
        saved, target, *local = take(
            [saved_preds, targets] + [train_points] * (nc - 1), [0, 0, *range(1, nc)], piece
        )
        local = [own, *local]
        for d in range(2, nc, 2):
            pos[d + 1] = swap(after(pos[d], layer[1], layer[2], side[1], side[d], saved), "centers", nc, 1)
            side[d + 1] = swap(after(side[d], layer[2], side[1]), "centers", nc, 1)
        centers = [a for d in range(nc) for a in (pos[d], side[d])]

        early = {0: jnp.concatenate([layer[dz] for dz in range(1, nz - 1)])}

        first, second = range(2, nz, 2), range(3, nz, 2)
        parts = dict(zip(first, forward([layer[dz] for dz in first], centers, out_width, BRIEF)))
        received = {dz: swap(parts[dz], "points", nz, dz) for dz in first}
        rows = [after(layer[1], *parts.values())]
        (parts[1],) = forward(rows, centers, out_width, COVER)
        received[1] = swap(parts[1], "points", nz, 1)
        rows = [after(layer[dz], *parts.values()) for dz in second]
        parts.update(zip(second, forward(rows, centers, out_width, COVER)))
        soon = [received[dz] for dz in range(2, nz, 2)]
        received = [received[1]] + [swap(parts[dz], "points", nz, dz) for dz in second]
        last = parts[nz - 1]
        kernels, late = {1: None}, {0: layer[nz - 1]}
        parts[0], kernels[0] = own_rows(
            after(own, last),
            centers,
            out_width,
            soon,
            center_pos,
            spread,
            [[local[0], early[0], late[0]]],
        )
        for d in range(2, nc, 2):
            early[d] = swap(after(early[0], side[d]), "centers", nc, d)
            late[d] = swap(after(late[0], last, *soon), "centers", nc, d)
            early[d + 1] = swap(after(early[d], parts[0]), "centers", nc, 1)
        early[1] = swap(after(early[0], parts[0]), "centers", nc, 1)
        late[1] = swap(after(late[0], parts[0]), "centers", nc, 1)
        cot = cotangent([parts[0], *received], saved, target, delta)

        far = {dz: swap(cot, "points", nz, dz) for dz in range(2, nz, 2)}
        far[1] = swap(cot, "points", nz, 1)
        far.update({dz: swap(far[dz - 1], "points", nz, 1) for dz in range(3, nz, 2)})
        ahead = {d: swap(after(cot, late[d]), "centers", nc, d) for d in range(2, nc, 2)}
        far[1] = after(far[1], *ahead.values())
        far = jnp.concatenate([far[dz] for dz in range(1, nz)])
        cots = {0: jnp.concatenate([cot, far])}
        across = {}
        for d in range(2, nc, 2):
            across[d] = [ahead[d], swap(far, "centers", nc, d)]
            late[d + 1] = swap(after(late[d], far), "centers", nc, 1)
        cots[1] = swap(cots[0], "centers", nc, 1)

        points = {d: [local[d], early[d], late[d]] for d in range(nc)}
        groups = [(kernels[d], points[d], cots[d]) for d in (0, 1)]
        *sums, kernels[2], kernels[3] = backward(
            center_pos, coefficients, spread, groups, more=[points[2], points[3]]
        )
        for d in range(4, nc):
            kernels[d] = own_kernel(center_pos, spread, points[d])
        for d in range(2, nc, 2):
            cots[d] = jnp.concatenate([after(a, sums[0]) for a in across[d]])
            cots[d + 1] = swap(cots[d], "centers", nc, 1)
        for d in range(2, nc - 1):
            group = (kernels[d], points[d], cots[d])
            sums = backward(center_pos, coefficients, spread, [group], before=sums)
        group = (kernels[nc - 1], points[nc - 1], cots[nc - 1])
        return finish(center_pos, coefficients, spread, group, sums)

    return jax.shard_map(
        per_device,
        mesh=mesh,
        in_specs=(
            P(("groups", "points"), None),
            P(("groups", "points"), None),
            P(("groups", "points"), None),
            P("groups"),
            P(("groups", "points", "centers"), None),
            P(("groups", "points", "centers"), None),
            P(("groups", "points", "centers")),
        ),
        out_specs=(
            P(("groups", "points", "centers"), None),
            P(("groups", "points", "centers"), None),
        ),
        check_vma=False,
    )
```

```python
import math

import jax
import jax.numpy as jnp
from jax import lax
from jax.experimental import pallas as pl
from jax.experimental.pallas import tpu as pltpu
from jax.sharding import PartitionSpec as P

F32, BF16 = jnp.float32, jnp.bfloat16
HBM = pl.BlockSpec(memory_space=pltpu.HBM)
VMEM = pl.BlockSpec(memory_space=pltpu.VMEM)
NT = (((1,), (1,)), ((), ()))
LOG2E = math.log2(math.e)
COVER = pl.CostEstimate(flops=1 << 34, bytes_accessed=1 << 20, transcendentals=1 << 20)
BRIEF = pl.CostEstimate(flops=1, bytes_accessed=1, transcendentals=0)


def swap(a, axis, size, d):
    return lax.ppermute(a, axis, [(i, i ^ d) for i in range(size)])


def after(a, *others):
    return lax.optimization_barrier((a, *others))[0]


def lane_groups(a):
    total = None
    for k in range(0, a.shape[1], 128):
        part = jnp.square(a[:, k : k + 128].astype(F32))
        total = part if total is None else total + part
    return total


def half_sq_row(a):
    return 0.5 * jnp.sum(lane_groups(a).T, axis=0, keepdims=True)


def half_sq_column(a):
    return 0.5 * jnp.sum(lane_groups(a), axis=1, keepdims=True)


def column(row):
    return jnp.broadcast_to(row, (128, row.shape[1])).T


def params(mib):
    return pltpu.CompilerParams(vmem_limit_bytes=mib << 20)


def pack(center_pos, coefficients, spread, delta):
    n, in_width = center_pos.shape
    out_width = coefficients.shape[1]
    across = in_width // out_width
    q = n // across

    def body(pos_ref, coef_ref, spread_ref, delta_ref, own_pos, out_ref, row_ref, own_spread, own_coef):
        row_ref[...] = delta_ref[...]
        own_spread[...] = spread_ref[...]
        own_coef[...] = coef_ref[...]
        pos = pos_ref[...]
        own_pos[...] = pos
        for k in range(across):
            out_ref[:q, k * out_width : (k + 1) * out_width] = coef_ref[k * q : (k + 1) * q]
        half = half_sq_row(pos)
        high = half.astype(BF16)
        rest = half - high.astype(F32)
        middle = rest.astype(BF16)
        low = (rest - middle.astype(F32)).astype(BF16)
        rows = [r.astype(F32) for r in (spread_ref[...], high, middle, low)]
        tail = jnp.concatenate(rows + [jnp.zeros((12, n), F32)]).astype(BF16)
        if n < in_width:
            tail = jnp.concatenate([tail, jnp.zeros((16, in_width - n), BF16)], axis=1)
        out_ref[q:] = tail

    return pl.pallas_call(
        body,
        out_shape=(
            jax.ShapeDtypeStruct((n, in_width), BF16),
            jax.ShapeDtypeStruct((q + 16, in_width), BF16),
            jax.ShapeDtypeStruct((1, delta.shape[0]), F32),
            jax.ShapeDtypeStruct((1, n), BF16),
            jax.ShapeDtypeStruct((n, out_width), BF16),
        ),
        in_specs=[VMEM] * 4,
        out_specs=(VMEM,) * 5,
        compiler_params=params(16),
        cost_estimate=BRIEF,
        name="pack",
    )(center_pos, coefficients, spread.reshape(1, n), delta.reshape(1, -1))


def take(arrays, offsets, piece):
    def body(*refs):
        ins, outs, sems = refs[: len(arrays)], refs[len(arrays) : -1], refs[-1]
        made = []
        for k, d in enumerate(offsets):
            start = pl.multiple_of((lax.axis_index("centers") ^ d) * piece, piece)
            made.append(pltpu.make_async_copy(ins[k].at[pl.ds(start, piece)], outs[k], sems.at[k]))
            made[-1].start()
        for copy in made:
            copy.wait()

    return pl.pallas_call(
        body,
        out_shape=tuple(jax.ShapeDtypeStruct((piece, a.shape[1]), a.dtype) for a in arrays),
        in_specs=[HBM] * len(arrays),
        out_specs=(VMEM,) * len(arrays),
        scratch_shapes=[pltpu.SemaphoreType.DMA((len(arrays),))],
        compiler_params=params(16),
        cost_estimate=BRIEF,
        name="take",
    )(*arrays)


def partial_pred(x, refs, total):
    in_width = x.shape[1]
    row_sq = half_sq_column(x)
    for pos_ref, side_ref in zip(refs[::2], refs[1::2]):
        n, q = pos_ref.shape[0], side_ref.shape[0] - 16
        out_width = q * in_width // n
        packed = side_ref[:q]
        coef = jnp.concatenate([packed[:, k : k + out_width] for k in range(0, in_width, out_width)])
        tail = side_ref[q:, :n].astype(F32)
        center_sq = tail[1:2] + tail[2:3] + tail[3:4]
        rate = tail[0:1] * (-2.0 * LOG2E / in_width)
        cross = lax.dot_general(x, pos_ref[...], NT, preferred_element_type=F32)
        power = (row_sq + center_sq - cross) * rate
        kernel = jnp.exp2(power).astype(BF16)
        new = jnp.dot(kernel, coef, preferred_element_type=F32)
        total = new if total is None else total + new
    return total


def own_values(pos_ref, spread_ref, refs):
    pos = pos_ref[...]
    center_sq = half_sq_column(pos)
    rate = column(spread_ref[...].astype(F32) * (-2.0 * LOG2E / pos.shape[1]))[:, :1]
    for ref in refs:
        step = min(256, ref.shape[0])
        for start in range(0, ref.shape[0], step):
            x = ref[start : start + step]
            cross = lax.dot_general(pos, x, NT, preferred_element_type=F32)
            power = (center_sq + half_sq_row(x) - cross) * rate
            yield jnp.exp2(power).astype(BF16)


def store_values(pos_ref, spread_ref, refs, out_ref):
    at = 0
    for part in own_values(pos_ref, spread_ref, refs):
        out_ref[:, at : at + part.shape[1]] = part
        at += part.shape[1]


def forward(rows, centers, out_width, cost):
    counts = [r.shape[0] for r in rows]

    def body(*refs):
        row_refs, refs, outs = refs[: len(rows)], refs[len(rows) : -len(rows)], refs[-len(rows) :]
        x = jnp.concatenate([ref[...] for ref in row_refs])
        total = partial_pred(x, refs, None)
        at = 0
        for ref, count in zip(outs, counts):
            ref[...] = total[at : at + count]
            at += count

    return pl.pallas_call(
        body,
        out_shape=tuple(jax.ShapeDtypeStruct((count, out_width), F32) for count in counts),
        in_specs=[VMEM] * (len(rows) + len(centers)),
        out_specs=(VMEM,) * len(rows),
        compiler_params=params(24),
        cost_estimate=cost,
        name="forward",
    )(*rows, *centers)


def own_kernel(center_pos, spread, blocks):
    n = spread.shape[1]
    points = sum(b.shape[0] for b in blocks)

    def body(pos_ref, spread_ref, *refs):
        store_values(pos_ref, spread_ref, refs[:-1], refs[-1])

    return pl.pallas_call(
        body,
        out_shape=jax.ShapeDtypeStruct((n, points), BF16),
        in_specs=[VMEM] * (2 + len(blocks)),
        out_specs=VMEM,
        compiler_params=params(16),
        cost_estimate=BRIEF,
        name="own_kernel",
    )(center_pos, spread, *blocks)


def own_rows(rows, centers, out_width, received, center_pos, spread, more):
    n = spread.shape[1]
    ends = [1, 1 + len(centers)]
    ends.append(ends[-1] + len(received))

    def body(*refs):
        outs, refs = refs[-1 - len(more) :], refs[: -1 - len(more)]
        total = None
        for ref in refs[ends[1] : ends[2]]:
            total = ref[...] if total is None else total + ref[...]
        outs[0][...] = partial_pred(refs[0][...], refs[1 : ends[1]], total)
        pos_ref, spread_ref, *block_refs = refs[ends[2] :]
        for k, blocks in enumerate(more):
            store_values(pos_ref, spread_ref, block_refs[: len(blocks)], outs[1 + k])
            del block_refs[: len(blocks)]

    ins = [rows, *centers, *received, center_pos, spread]
    ins += [block for blocks in more for block in blocks]
    return pl.pallas_call(
        body,
        out_shape=(jax.ShapeDtypeStruct((rows.shape[0], out_width), F32),)
        + tuple(jax.ShapeDtypeStruct((n, sum(b.shape[0] for b in blocks)), BF16) for blocks in more),
        in_specs=[VMEM] * len(ins),
        out_specs=(VMEM,) * (1 + len(more)),
        compiler_params=params(16),
        cost_estimate=COVER,
        name="own_rows",
    )(*ins)


def cotangent(parts, saved, target, delta):
    def body(*refs):
        saved_ref, target_ref, delta_ref, out_ref = refs[-4:]
        pred = refs[0][...]
        for ref in refs[1:-4]:
            pred += ref[...]
        residual = pred + saved_ref[...] - target_ref[...]
        ratio = residual / delta_ref[...]
        out_ref[...] = (residual / jnp.sqrt(1.0 + ratio * ratio)).astype(BF16)

    return pl.pallas_call(
        body,
        out_shape=jax.ShapeDtypeStruct(saved.shape, BF16),
        in_specs=[VMEM] * (len(parts) + 3),
        out_specs=VMEM,
        compiler_params=params(16),
        cost_estimate=BRIEF,
        name="cotangent",
    )(*parts, saved, target, delta)


def group_terms(coef, kernel, x, cot):
    mixing = lax.dot_general(coef, cot, NT, preferred_element_type=F32)
    weights = (kernel.astype(F32) * mixing).astype(BF16)
    lanes = weights[:, :128].astype(F32)
    for k in range(128, kernel.shape[1], 128):
        lanes += weights[:, k : k + 128].astype(F32)
    return (
        jnp.dot(weights, x, preferred_element_type=F32),
        jnp.dot(kernel, cot, preferred_element_type=F32),
        lanes,
    )


def backward(center_pos, coefficients, spread, groups, before=None, more=()):
    (n, out_width), in_width = coefficients.shape, center_pos.shape[1]
    flat = []
    for kernel, xs, cot in groups:
        flat += [*xs, cot] if kernel is None else [kernel, *xs, cot]
    carried = [] if before is None else list(before)
    outs = 3 + len(more)
    wanted = [block for blocks in more for block in blocks]

    def body(pos_ref, coef_ref, spread_ref, *refs):
        refs, out_refs = list(refs[:-outs]), refs[-outs:]
        coef = coef_ref[...]
        sums = [ref[...] for ref in refs[len(flat) : len(flat) + 3]] if carried else None
        block_refs = refs[len(flat) + len(carried) :]
        for k, blocks in enumerate(more):
            store_values(pos_ref, spread_ref, block_refs[: len(blocks)], out_refs[3 + k])
            del block_refs[: len(blocks)]
        for given, xs, _ in groups:
            kernel = None if given is None else refs.pop(0)[...]
            x_refs = [refs.pop(0) for _ in xs]
            if given is None:
                kernel = jnp.concatenate(list(own_values(pos_ref, spread_ref, x_refs)), axis=1)
            x = jnp.concatenate([ref[...] for ref in x_refs])
            terms = group_terms(coef, kernel, x, refs.pop(0)[...])
            sums = terms if sums is None else [a + b for a, b in zip(sums, terms)]
        for ref, value in zip(out_refs[:3], sums):
            ref[...] = value

    return pl.pallas_call(
        body,
        out_shape=tuple(jax.ShapeDtypeStruct((n, width), F32) for width in (in_width, out_width, 128))
        + tuple(jax.ShapeDtypeStruct((n, sum(b.shape[0] for b in blocks)), BF16) for blocks in more),
        in_specs=[VMEM] * (3 + len(flat) + len(carried) + len(wanted)),
        out_specs=(VMEM,) * outs,
        compiler_params=params(24),
        cost_estimate=COVER if more else BRIEF,
        name="backward",
    )(center_pos, coefficients, spread, *flat, *carried, *wanted)


def finish(center_pos, coefficients, spread, group, before):
    (n, out_width), in_width = coefficients.shape, center_pos.shape[1]
    kernel, xs, cot = group
    step = min(n, 256)

    def body(pos_ref, coef_ref, spread_ref, kernel_ref, cot_ref, *refs):
        x_refs, refs = refs[: len(xs)], refs[len(xs) :]
        moment_ref, grad_ref, lanes_ref, centers_out, coef_out, centers_buf, coef_buf, sems = refs
        x = jnp.concatenate([ref[...] for ref in x_refs])
        cot = cot_ref[...]
        scale = column(spread_ref[...].astype(F32)) * (2.0 / in_width)
        made = []
        for k, start in enumerate(range(0, n, step)):
            rows = slice(start, start + step)
            moment, grad, lanes = group_terms(coef_ref[rows], kernel_ref[rows], x, cot)
            coef_buf[rows] = grad_ref[rows] + grad
            moment += moment_ref[rows]
            total = jnp.sum(lanes_ref[rows] + lanes, axis=1, keepdims=True)
            for at in range(0, in_width, 128):
                pos = pos_ref[rows, at : at + 128].astype(F32)
                centers_buf[rows, at : at + 128] = scale[rows] * (moment[:, at : at + 128] - total * pos)
            pairs = [(centers_buf, centers_out), (coef_buf, coef_out)]
            for j, (src, dst) in enumerate(pairs):
                copy = pltpu.make_async_copy(src.at[rows], dst.at[rows], sems.at[2 * k + j])
                copy.start()
                made.append(copy)
        for copy in made:
            copy.wait()

    ins = [center_pos, coefficients, spread, kernel, cot, *xs, *before]
    return pl.pallas_call(
        body,
        out_shape=tuple(jax.ShapeDtypeStruct((n, width), F32) for width in (in_width, out_width)),
        in_specs=[VMEM] * len(ins),
        out_specs=(HBM, HBM),
        scratch_shapes=[
            pltpu.VMEM((n, in_width), F32),
            pltpu.VMEM((n, out_width), F32),
            pltpu.SemaphoreType.DMA((2 * pl.cdiv(n, step),)),
        ],
        compiler_params=params(24),
        cost_estimate=BRIEF,
        name="finish",
    )(*ins)


def solution(mesh):
    nz, nc = mesh.shape["points"], mesh.shape["centers"]

    def per_device(train_points, saved_preds, targets, huber_delta, center_pos, coefficients, spread):
        n_rows = train_points.shape[0]
        n, out_width = coefficients.shape
        piece = n_rows // nc

        own = lax.dynamic_slice_in_dim(train_points, lax.axis_index("centers") * piece, piece)

        layer = {0: own}
        for dz in range(2, nz, 2):
            layer[dz] = swap(own, "points", nz, dz)
        layer[1] = swap(own, "points", nz, 1)

        pos, side = {1: swap(center_pos, "centers", nc, 1)}, {}
        for d in range(2, nc, 2):
            pos[d] = swap(center_pos, "centers", nc, d)
        center_pos, side[0], delta, spread, coefficients = pack(
            after(center_pos, own), coefficients, spread, huber_delta
        )
        pos[0], side[1] = center_pos, swap(side[0], "centers", nc, 1)
        for d in range(2, nc, 2):
            side[d] = swap(side[0], "centers", nc, d)
        for dz in range(3, nz, 2):
            layer[dz] = swap(layer[dz - 1], "points", nz, 1)
        saved, target, *local = take(
            [saved_preds, targets] + [train_points] * (nc - 1), [0, 0, *range(1, nc)], piece
        )
        local = [own, *local]
        for d in range(2, nc, 2):
            pos[d + 1] = swap(after(pos[d], layer[1], layer[2], side[1], side[d], saved), "centers", nc, 1)
            side[d + 1] = swap(after(side[d], layer[2], side[1]), "centers", nc, 1)
        centers = [a for d in range(nc) for a in (pos[d], side[d])]

        early = {0: jnp.concatenate([layer[dz] for dz in range(1, nz - 1)])}

        first, second = range(2, nz, 2), range(3, nz, 2)
        parts = dict(zip(first, forward([layer[dz] for dz in first], centers, out_width, BRIEF)))
        received = {dz: swap(parts[dz], "points", nz, dz) for dz in first}
        rows = [after(layer[1], *parts.values())]
        (parts[1],) = forward(rows, centers, out_width, COVER)
        received[1] = swap(parts[1], "points", nz, 1)
        rows = [after(layer[dz], *parts.values()) for dz in second]
        parts.update(zip(second, forward(rows, centers, out_width, COVER)))
        soon = list(received.values())
        received = [swap(parts[dz], "points", nz, dz) for dz in second]
        last = parts[nz - 1]
        kernels, late = {1: None}, {0: layer[nz - 1]}
        parts[0], kernels[0] = own_rows(
            after(own, last),
            centers,
            out_width,
            soon,
            center_pos,
            spread,
            [[local[0], early[0], late[0]]],
        )
        for d in range(2, nc, 2):
            early[d] = swap(after(early[0], side[d]), "centers", nc, d)
            late[d] = swap(after(late[0], last, *soon), "centers", nc, d)
            early[d + 1] = swap(after(early[d], parts[0]), "centers", nc, 1)
        early[1] = swap(after(early[0], parts[0]), "centers", nc, 1)
        late[1] = swap(after(late[0], parts[0]), "centers", nc, 1)
        cot = cotangent([parts[0], *received], saved, target, delta)

        far = {dz: swap(cot, "points", nz, dz) for dz in range(2, nz, 2)}
        far[1] = swap(cot, "points", nz, 1)
        far.update({dz: swap(far[dz - 1], "points", nz, 1) for dz in range(3, nz, 2)})
        ahead = {d: swap(after(cot, late[d]), "centers", nc, d) for d in range(2, nc, 2)}
        far[1] = after(far[1], *ahead.values())
        far = jnp.concatenate([far[dz] for dz in range(1, nz)])
        cots = {0: jnp.concatenate([cot, far])}
        across = {}
        for d in range(2, nc, 2):
            across[d] = [ahead[d], swap(far, "centers", nc, d)]
            late[d + 1] = swap(after(late[d], far), "centers", nc, 1)
        cots[1] = swap(cots[0], "centers", nc, 1)

        points = {d: [local[d], early[d], late[d]] for d in range(nc)}
        groups = [(kernels[d], points[d], cots[d]) for d in (0, 1)]
        *sums, kernels[2], kernels[3] = backward(
            center_pos, coefficients, spread, groups, more=[points[2], points[3]]
        )
        for d in range(4, nc):
            kernels[d] = own_kernel(center_pos, spread, points[d])
        for d in range(2, nc, 2):
            cots[d] = jnp.concatenate([after(a, sums[0]) for a in across[d]])
            cots[d + 1] = swap(cots[d], "centers", nc, 1)
        for d in range(2, nc - 1):
            group = (kernels[d], points[d], cots[d])
            sums = backward(center_pos, coefficients, spread, [group], before=sums)
        group = (kernels[nc - 1], points[nc - 1], cots[nc - 1])
        return finish(center_pos, coefficients, spread, group, sums)

    return jax.shard_map(
        per_device,
        mesh=mesh,
        in_specs=(
            P(("groups", "points"), None),
            P(("groups", "points"), None),
            P(("groups", "points"), None),
            P("groups"),
            P(("groups", "points", "centers"), None),
            P(("groups", "points", "centers"), None),
            P(("groups", "points", "centers")),
        ),
        out_specs=(
            P(("groups", "points", "centers"), None),
            P(("groups", "points", "centers"), None),
        ),
        check_vma=False,
    )
```

```python
import math

import jax
import jax.numpy as jnp
from jax import lax
from jax.experimental import pallas as pl
from jax.experimental.pallas import tpu as pltpu
from jax.sharding import PartitionSpec as P

F32, BF16 = jnp.float32, jnp.bfloat16
HBM = pl.BlockSpec(memory_space=pltpu.HBM)
VMEM = pl.BlockSpec(memory_space=pltpu.VMEM)
NT = (((1,), (1,)), ((), ()))
LOG2E = math.log2(math.e)
COVER = pl.CostEstimate(flops=1 << 34, bytes_accessed=1 << 20, transcendentals=1 << 20)
BRIEF = pl.CostEstimate(flops=1, bytes_accessed=1, transcendentals=0)


def swap(a, axis, size, d):
    return lax.ppermute(a, axis, [(i, i ^ d) for i in range(size)])


def after(a, *others):
    return lax.optimization_barrier((a, *others))[0]


def lane_groups(a):
    total = None
    for k in range(0, a.shape[1], 128):
        part = jnp.square(a[:, k : k + 128].astype(F32))
        total = part if total is None else total + part
    return total


def half_sq_row(a):
    return 0.5 * jnp.sum(lane_groups(a).T, axis=0, keepdims=True)


def half_sq_column(a):
    return 0.5 * jnp.sum(lane_groups(a), axis=1, keepdims=True)


def column(row):
    return jnp.broadcast_to(row, (128, row.shape[1])).T


def params(mib):
    return pltpu.CompilerParams(vmem_limit_bytes=mib << 20)


def pack(center_pos, coefficients, spread, delta):
    n, in_width = center_pos.shape
    out_width = coefficients.shape[1]
    across = in_width // out_width
    q = n // across

    def body(pos_ref, coef_ref, spread_ref, delta_ref, own_pos, out_ref, row_ref, own_spread, own_coef):
        row_ref[...] = delta_ref[...]
        own_spread[...] = spread_ref[...]
        own_coef[...] = coef_ref[...]
        pos = pos_ref[...]
        own_pos[...] = pos
        for k in range(across):
            out_ref[:q, k * out_width : (k + 1) * out_width] = coef_ref[k * q : (k + 1) * q]
        half = half_sq_row(pos)
        high = half.astype(BF16)
        rest = half - high.astype(F32)
        middle = rest.astype(BF16)
        low = (rest - middle.astype(F32)).astype(BF16)
        rows = [r.astype(F32) for r in (spread_ref[...], high, middle, low)]
        tail = jnp.concatenate(rows + [jnp.zeros((12, n), F32)]).astype(BF16)
        if n < in_width:
            tail = jnp.concatenate([tail, jnp.zeros((16, in_width - n), BF16)], axis=1)
        out_ref[q:] = tail

    return pl.pallas_call(
        body,
        out_shape=(
            jax.ShapeDtypeStruct((n, in_width), BF16),
            jax.ShapeDtypeStruct((q + 16, in_width), BF16),
            jax.ShapeDtypeStruct((1, delta.shape[0]), F32),
            jax.ShapeDtypeStruct((1, n), BF16),
            jax.ShapeDtypeStruct((n, out_width), BF16),
        ),
        in_specs=[VMEM] * 4,
        out_specs=(VMEM,) * 5,
        compiler_params=params(16),
        cost_estimate=BRIEF,
        name="pack",
    )(center_pos, coefficients, spread.reshape(1, n), delta.reshape(1, -1))


def take(arrays, offsets, piece):
    def body(*refs):
        ins, outs, sems = refs[: len(arrays)], refs[len(arrays) : -1], refs[-1]
        made = []
        for k, d in enumerate(offsets):
            start = pl.multiple_of((lax.axis_index("centers") ^ d) * piece, piece)
            made.append(pltpu.make_async_copy(ins[k].at[pl.ds(start, piece)], outs[k], sems.at[k]))
            made[-1].start()
        for copy in made:
            copy.wait()

    return pl.pallas_call(
        body,
        out_shape=tuple(jax.ShapeDtypeStruct((piece, a.shape[1]), a.dtype) for a in arrays),
        in_specs=[HBM] * len(arrays),
        out_specs=(VMEM,) * len(arrays),
        scratch_shapes=[pltpu.SemaphoreType.DMA((len(arrays),))],
        compiler_params=params(16),
        cost_estimate=BRIEF,
        name="take",
    )(*arrays)


def partial_pred(x, refs, total):
    in_width = x.shape[1]
    row_sq = half_sq_column(x)
    for pos_ref, side_ref in zip(refs[::2], refs[1::2]):
        n, q = pos_ref.shape[0], side_ref.shape[0] - 16
        out_width = q * in_width // n
        packed = side_ref[:q]
        coef = jnp.concatenate([packed[:, k : k + out_width] for k in range(0, in_width, out_width)])
        tail = side_ref[q:, :n].astype(F32)
        center_sq = tail[1:2] + tail[2:3] + tail[3:4]
        rate = tail[0:1] * (-2.0 * LOG2E / in_width)
        cross = lax.dot_general(x, pos_ref[...], NT, preferred_element_type=F32)
        power = (row_sq + center_sq - cross) * rate
        kernel = jnp.exp2(power).astype(BF16)
        new = jnp.dot(kernel, coef, preferred_element_type=F32)
        total = new if total is None else total + new
    return total


def own_values(pos_ref, spread_ref, refs):
    pos = pos_ref[...]
    center_sq = half_sq_column(pos)
    rate = column(spread_ref[...].astype(F32) * (-2.0 * LOG2E / pos.shape[1]))[:, :1]
    for ref in refs:
        step = min(256, ref.shape[0])
        for start in range(0, ref.shape[0], step):
            x = ref[start : start + step]
            cross = lax.dot_general(pos, x, NT, preferred_element_type=F32)
            power = (center_sq + half_sq_row(x) - cross) * rate
            yield jnp.exp2(power).astype(BF16)


def store_values(pos_ref, spread_ref, refs, out_ref):
    at = 0
    for part in own_values(pos_ref, spread_ref, refs):
        out_ref[:, at : at + part.shape[1]] = part
        at += part.shape[1]


def forward(rows, centers, out_width, cost):
    counts = [r.shape[0] for r in rows]

    def body(*refs):
        row_refs, refs, outs = refs[: len(rows)], refs[len(rows) : -len(rows)], refs[-len(rows) :]
        x = jnp.concatenate([ref[...] for ref in row_refs])
        total = partial_pred(x, refs, None)
        at = 0
        for ref, count in zip(outs, counts):
            ref[...] = total[at : at + count]
            at += count

    return pl.pallas_call(
        body,
        out_shape=tuple(jax.ShapeDtypeStruct((count, out_width), F32) for count in counts),
        in_specs=[VMEM] * (len(rows) + len(centers)),
        out_specs=(VMEM,) * len(rows),
        compiler_params=params(24),
        cost_estimate=cost,
        name="forward",
    )(*rows, *centers)


def own_kernel(center_pos, spread, blocks):
    n = spread.shape[1]
    points = sum(b.shape[0] for b in blocks)

    def body(pos_ref, spread_ref, *refs):
        store_values(pos_ref, spread_ref, refs[:-1], refs[-1])

    return pl.pallas_call(
        body,
        out_shape=jax.ShapeDtypeStruct((n, points), BF16),
        in_specs=[VMEM] * (2 + len(blocks)),
        out_specs=VMEM,
        compiler_params=params(16),
        cost_estimate=BRIEF,
        name="own_kernel",
    )(center_pos, spread, *blocks)


def own_rows(rows, centers, out_width, received, center_pos, spread, more):
    n = spread.shape[1]
    ends = [1, 1 + len(centers)]
    ends.append(ends[-1] + len(received))

    def body(*refs):
        outs, refs = refs[-1 - len(more) :], refs[: -1 - len(more)]
        total = None
        for ref in refs[ends[1] : ends[2]]:
            total = ref[...] if total is None else total + ref[...]
        outs[0][...] = partial_pred(refs[0][...], refs[1 : ends[1]], total)
        pos_ref, spread_ref, *block_refs = refs[ends[2] :]
        for k, blocks in enumerate(more):
            store_values(pos_ref, spread_ref, block_refs[: len(blocks)], outs[1 + k])
            del block_refs[: len(blocks)]

    ins = [rows, *centers, *received, center_pos, spread]
    ins += [block for blocks in more for block in blocks]
    return pl.pallas_call(
        body,
        out_shape=(jax.ShapeDtypeStruct((rows.shape[0], out_width), F32),)
        + tuple(jax.ShapeDtypeStruct((n, sum(b.shape[0] for b in blocks)), BF16) for blocks in more),
        in_specs=[VMEM] * len(ins),
        out_specs=(VMEM,) * (1 + len(more)),
        compiler_params=params(16),
        cost_estimate=COVER,
        name="own_rows",
    )(*ins)


def cotangent(parts, saved, target, delta):
    def body(*refs):
        saved_ref, target_ref, delta_ref, out_ref = refs[-4:]
        pred = refs[0][...]
        for ref in refs[1:-4]:
            pred += ref[...]
        residual = pred + saved_ref[...] - target_ref[...]
        ratio = residual / delta_ref[...]
        out_ref[...] = (residual / jnp.sqrt(1.0 + ratio * ratio)).astype(BF16)

    return pl.pallas_call(
        body,
        out_shape=jax.ShapeDtypeStruct(saved.shape, BF16),
        in_specs=[VMEM] * (len(parts) + 3),
        out_specs=VMEM,
        compiler_params=params(16),
        cost_estimate=BRIEF,
        name="cotangent",
    )(*parts, saved, target, delta)


def group_terms(coef, kernel, x, cot):
    mixing = lax.dot_general(coef, cot, NT, preferred_element_type=F32)
    weights = (kernel.astype(F32) * mixing).astype(BF16)
    lanes = weights[:, :128].astype(F32)
    for k in range(128, kernel.shape[1], 128):
        lanes += weights[:, k : k + 128].astype(F32)
    return (
        jnp.dot(weights, x, preferred_element_type=F32),
        jnp.dot(kernel, cot, preferred_element_type=F32),
        lanes,
    )


def backward(center_pos, coefficients, spread, groups, before=None, more=()):
    (n, out_width), in_width = coefficients.shape, center_pos.shape[1]
    flat = []
    for kernel, xs, cot in groups:
        flat += [*xs, cot] if kernel is None else [kernel, *xs, cot]
    carried = [] if before is None else list(before)
    outs = 3 + len(more)
    wanted = [block for blocks in more for block in blocks]

    def body(pos_ref, coef_ref, spread_ref, *refs):
        refs, out_refs = list(refs[:-outs]), refs[-outs:]
        coef = coef_ref[...]
        sums = [ref[...] for ref in refs[len(flat) : len(flat) + 3]] if carried else None
        block_refs = refs[len(flat) + len(carried) :]
        for k, blocks in enumerate(more):
            store_values(pos_ref, spread_ref, block_refs[: len(blocks)], out_refs[3 + k])
            del block_refs[: len(blocks)]
        for given, xs, _ in groups:
            kernel = None if given is None else refs.pop(0)[...]
            x_refs = [refs.pop(0) for _ in xs]
            if given is None:
                kernel = jnp.concatenate(list(own_values(pos_ref, spread_ref, x_refs)), axis=1)
            x = jnp.concatenate([ref[...] for ref in x_refs])
            terms = group_terms(coef, kernel, x, refs.pop(0)[...])
            sums = terms if sums is None else [a + b for a, b in zip(sums, terms)]
        for ref, value in zip(out_refs[:3], sums):
            ref[...] = value

    return pl.pallas_call(
        body,
        out_shape=tuple(jax.ShapeDtypeStruct((n, width), F32) for width in (in_width, out_width, 128))
        + tuple(jax.ShapeDtypeStruct((n, sum(b.shape[0] for b in blocks)), BF16) for blocks in more),
        in_specs=[VMEM] * (3 + len(flat) + len(carried) + len(wanted)),
        out_specs=(VMEM,) * outs,
        compiler_params=params(24),
        cost_estimate=COVER if more else BRIEF,
        name="backward",
    )(center_pos, coefficients, spread, *flat, *carried, *wanted)


def finish(center_pos, coefficients, spread, group, before):
    (n, out_width), in_width = coefficients.shape, center_pos.shape[1]
    kernel, xs, cot = group
    step = min(n, 256)

    def body(pos_ref, coef_ref, spread_ref, kernel_ref, cot_ref, *refs):
        x_refs, refs = refs[: len(xs)], refs[len(xs) :]
        moment_ref, grad_ref, lanes_ref, centers_out, coef_out, centers_buf, coef_buf, sems = refs
        x = jnp.concatenate([ref[...] for ref in x_refs])
        cot = cot_ref[...]
        scale = column(spread_ref[...].astype(F32)) * (2.0 / in_width)
        made = []
        for k, start in enumerate(range(0, n, step)):
            rows = slice(start, start + step)
            moment, grad, lanes = group_terms(coef_ref[rows], kernel_ref[rows], x, cot)
            coef_buf[rows] = grad_ref[rows] + grad
            moment += moment_ref[rows]
            total = jnp.sum(lanes_ref[rows] + lanes, axis=1, keepdims=True)
            for at in range(0, in_width, 128):
                pos = pos_ref[rows, at : at + 128].astype(F32)
                centers_buf[rows, at : at + 128] = scale[rows] * (moment[:, at : at + 128] - total * pos)
            pairs = [(centers_buf, centers_out), (coef_buf, coef_out)]
            for j, (src, dst) in enumerate(pairs):
                copy = pltpu.make_async_copy(src.at[rows], dst.at[rows], sems.at[2 * k + j])
                copy.start()
                made.append(copy)
        for copy in made:
            copy.wait()

    ins = [center_pos, coefficients, spread, kernel, cot, *xs, *before]
    return pl.pallas_call(
        body,
        out_shape=tuple(jax.ShapeDtypeStruct((n, width), F32) for width in (in_width, out_width)),
        in_specs=[VMEM] * len(ins),
        out_specs=(HBM, HBM),
        scratch_shapes=[
            pltpu.VMEM((n, in_width), F32),
            pltpu.VMEM((n, out_width), F32),
            pltpu.SemaphoreType.DMA((2 * pl.cdiv(n, step),)),
        ],
        compiler_params=params(24),
        cost_estimate=BRIEF,
        name="finish",
    )(*ins)


def solution(mesh):
    nz, nc = mesh.shape["points"], mesh.shape["centers"]

    def per_device(train_points, saved_preds, targets, huber_delta, center_pos, coefficients, spread):
        n_rows = train_points.shape[0]
        n, out_width = coefficients.shape
        piece = n_rows // nc

        own = lax.dynamic_slice_in_dim(train_points, lax.axis_index("centers") * piece, piece)

        layer = {0: own}
        for dz in range(2, nz, 2):
            layer[dz] = swap(own, "points", nz, dz)
        layer[1] = swap(own, "points", nz, 1)

        pos, side = {1: swap(center_pos, "centers", nc, 1)}, {}
        for d in range(2, nc, 2):
            pos[d] = swap(center_pos, "centers", nc, d)
        center_pos, side[0], delta, spread, coefficients = pack(
            after(center_pos, own), coefficients, spread, huber_delta
        )
        pos[0], side[1] = center_pos, swap(side[0], "centers", nc, 1)
        for d in range(2, nc, 2):
            side[d] = swap(side[0], "centers", nc, d)
        for dz in range(3, nz, 2):
            layer[dz] = swap(layer[dz - 1], "points", nz, 1)
        saved, target, *local = take(
            [saved_preds, targets] + [train_points] * (nc - 1), [0, 0, *range(1, nc)], piece
        )
        local = [own, *local]
        for d in range(2, nc, 2):
            pos[d + 1] = swap(after(pos[d], layer[1], layer[2], side[1], side[d], saved), "centers", nc, 1)
            side[d + 1] = swap(after(side[d], layer[2], side[1]), "centers", nc, 1)
        centers = [a for d in range(nc) for a in (pos[d], side[d])]

        early = {0: jnp.concatenate([layer[dz] for dz in range(1, nz - 1)])}

        first, second = range(2, nz, 2), range(3, nz, 2)
        parts = dict(zip(first, forward([layer[dz] for dz in first], centers, out_width, BRIEF)))
        received = {dz: swap(parts[dz], "points", nz, dz) for dz in first}
        rows = [after(layer[1], *parts.values())]
        (parts[1],) = forward(rows, centers, out_width, COVER)
        received[1] = swap(parts[1], "points", nz, 1)
        rows = [after(layer[dz], *parts.values()) for dz in second]
        parts.update(zip(second, forward(rows, centers, out_width, COVER)))
        soon = list(received.values())
        received = [swap(parts[dz], "points", nz, dz) for dz in second]
        last = parts[nz - 1]
        kernels, late = {1: None}, {0: layer[nz - 1]}
        parts[0], kernels[0] = own_rows(
            after(own, last),
            centers,
            out_width,
            soon,
            center_pos,
            spread,
            [[local[0], early[0], late[0]]],
        )
        for d in range(2, nc, 2):
            early[d] = swap(after(early[0], side[d]), "centers", nc, d)
            late[d] = swap(after(late[0], last, *soon), "centers", nc, d)
            early[d + 1] = swap(after(early[d], parts[0]), "centers", nc, 1)
        early[1] = swap(after(early[0], parts[0]), "centers", nc, 1)
        late[1] = swap(after(late[0], parts[0]), "centers", nc, 1)
        cot = cotangent([parts[0], *received], saved, target, delta)

        far = {dz: swap(cot, "points", nz, dz) for dz in range(2, nz, 2)}
        far[1] = swap(cot, "points", nz, 1)
        for d in range(2, nc, 2):
            kernels[d] = own_kernel(center_pos, spread, [local[d], early[d], late[d]])
        held = [kernels[d] for d in range(2, nc, 2)]
        far.update({dz: swap(after(far[dz - 1], *held), "points", nz, 1) for dz in range(3, nz, 2)})
        ahead = {d: swap(after(cot, late[d]), "centers", nc, d) for d in range(2, nc, 2)}
        far[1] = after(far[1], *ahead.values())
        far = jnp.concatenate([far[dz] for dz in range(1, nz)])
        cots = {0: jnp.concatenate([cot, far])}
        across = {}
        for d in range(2, nc, 2):
            across[d] = [ahead[d], swap(far, "centers", nc, d)]
            late[d + 1] = swap(after(late[d], far), "centers", nc, 1)
        cots[1] = swap(cots[0], "centers", nc, 1)

        points = {d: [local[d], early[d], late[d]] for d in range(nc)}
        groups = [(kernels[d], points[d], cots[d]) for d in (0, 1)]
        *sums, kernels[3] = backward(
            center_pos, coefficients, spread, groups, more=[points[3]]
        )
        for d in range(5, nc, 2):
            kernels[d] = own_kernel(center_pos, spread, points[d])
        for d in range(2, nc, 2):
            cots[d] = jnp.concatenate([after(a, sums[0]) for a in across[d]])
            cots[d + 1] = swap(cots[d], "centers", nc, 1)
        for d in range(2, nc - 1):
            group = (kernels[d], points[d], cots[d])
            sums = backward(center_pos, coefficients, spread, [group], before=sums)
        group = (kernels[nc - 1], points[nc - 1], cots[nc - 1])
        return finish(center_pos, coefficients, spread, group, sums)

    return jax.shard_map(
        per_device,
        mesh=mesh,
        in_specs=(
            P(("groups", "points"), None),
            P(("groups", "points"), None),
            P(("groups", "points"), None),
            P("groups"),
            P(("groups", "points", "centers"), None),
            P(("groups", "points", "centers"), None),
            P(("groups", "points", "centers")),
        ),
        out_specs=(
            P(("groups", "points", "centers"), None),
            P(("groups", "points", "centers"), None),
        ),
        check_vma=False,
    )
```

```python
import math

import jax
import jax.numpy as jnp
from jax import lax
from jax.experimental import pallas as pl
from jax.experimental.pallas import tpu as pltpu
from jax.sharding import PartitionSpec as P

F32, BF16 = jnp.float32, jnp.bfloat16
HBM = pl.BlockSpec(memory_space=pltpu.HBM)
VMEM = pl.BlockSpec(memory_space=pltpu.VMEM)
NT = (((1,), (1,)), ((), ()))
LOG2E = math.log2(math.e)
COVER = pl.CostEstimate(flops=1 << 34, bytes_accessed=1 << 20, transcendentals=1 << 20)
BRIEF = pl.CostEstimate(flops=1, bytes_accessed=1, transcendentals=0)


def swap(a, axis, size, d):
    return lax.ppermute(a, axis, [(i, i ^ d) for i in range(size)])


def after(a, *others):
    return lax.optimization_barrier((a, *others))[0]


def lane_groups(a):
    total = None
    for k in range(0, a.shape[1], 128):
        part = jnp.square(a[:, k : k + 128].astype(F32))
        total = part if total is None else total + part
    return total


def half_sq_row(a):
    return 0.5 * jnp.sum(lane_groups(a).T, axis=0, keepdims=True)


def half_sq_column(a):
    return 0.5 * jnp.sum(lane_groups(a), axis=1, keepdims=True)


def column(row):
    return jnp.broadcast_to(row, (128, row.shape[1])).T


def params(mib):
    return pltpu.CompilerParams(vmem_limit_bytes=mib << 20)


def pack(center_pos, coefficients, spread, delta):
    n, in_width = center_pos.shape
    out_width = coefficients.shape[1]
    across = in_width // out_width
    q = n // across

    def body(pos_ref, coef_ref, spread_ref, delta_ref, own_pos, out_ref, row_ref, own_spread, own_coef):
        row_ref[...] = delta_ref[...]
        own_spread[...] = spread_ref[...]
        own_coef[...] = coef_ref[...]
        pos = pos_ref[...]
        own_pos[...] = pos
        for k in range(across):
            out_ref[:q, k * out_width : (k + 1) * out_width] = coef_ref[k * q : (k + 1) * q]
        half = half_sq_row(pos)
        high = half.astype(BF16)
        rest = half - high.astype(F32)
        middle = rest.astype(BF16)
        low = (rest - middle.astype(F32)).astype(BF16)
        rows = [r.astype(F32) for r in (spread_ref[...], high, middle, low)]
        tail = jnp.concatenate(rows + [jnp.zeros((12, n), F32)]).astype(BF16)
        if n < in_width:
            tail = jnp.concatenate([tail, jnp.zeros((16, in_width - n), BF16)], axis=1)
        out_ref[q:] = tail

    return pl.pallas_call(
        body,
        out_shape=(
            jax.ShapeDtypeStruct((n, in_width), BF16),
            jax.ShapeDtypeStruct((q + 16, in_width), BF16),
            jax.ShapeDtypeStruct((1, delta.shape[0]), F32),
            jax.ShapeDtypeStruct((1, n), BF16),
            jax.ShapeDtypeStruct((n, out_width), BF16),
        ),
        in_specs=[VMEM] * 4,
        out_specs=(VMEM,) * 5,
        compiler_params=params(16),
        cost_estimate=BRIEF,
        name="pack",
    )(center_pos, coefficients, spread.reshape(1, n), delta.reshape(1, -1))


def take(arrays, offsets, piece):
    def body(*refs):
        ins, outs, sems = refs[: len(arrays)], refs[len(arrays) : -1], refs[-1]
        made = []
        for k, d in enumerate(offsets):
            start = pl.multiple_of((lax.axis_index("centers") ^ d) * piece, piece)
            made.append(pltpu.make_async_copy(ins[k].at[pl.ds(start, piece)], outs[k], sems.at[k]))
            made[-1].start()
        for copy in made:
            copy.wait()

    return pl.pallas_call(
        body,
        out_shape=tuple(jax.ShapeDtypeStruct((piece, a.shape[1]), a.dtype) for a in arrays),
        in_specs=[HBM] * len(arrays),
        out_specs=(VMEM,) * len(arrays),
        scratch_shapes=[pltpu.SemaphoreType.DMA((len(arrays),))],
        compiler_params=params(16),
        cost_estimate=BRIEF,
        name="take",
    )(*arrays)


def partial_pred(x, refs, total):
    in_width = x.shape[1]
    row_sq = half_sq_column(x)
    for pos_ref, side_ref in zip(refs[::2], refs[1::2]):
        n, q = pos_ref.shape[0], side_ref.shape[0] - 16
        out_width = q * in_width // n
        packed = side_ref[:q]
        coef = jnp.concatenate([packed[:, k : k + out_width] for k in range(0, in_width, out_width)])
        tail = side_ref[q:, :n].astype(F32)
        center_sq = tail[1:2] + tail[2:3] + tail[3:4]
        rate = tail[0:1] * (-2.0 * LOG2E / in_width)
        cross = lax.dot_general(x, pos_ref[...], NT, preferred_element_type=F32)
        power = (row_sq + center_sq - cross) * rate
        kernel = jnp.exp2(power).astype(BF16)
        new = jnp.dot(kernel, coef, preferred_element_type=F32)
        total = new if total is None else total + new
    return total


def own_values(pos_ref, spread_ref, refs):
    pos = pos_ref[...]
    center_sq = half_sq_column(pos)
    rate = column(spread_ref[...].astype(F32) * (-2.0 * LOG2E / pos.shape[1]))[:, :1]
    for ref in refs:
        step = min(256, ref.shape[0])
        for start in range(0, ref.shape[0], step):
            x = ref[start : start + step]
            cross = lax.dot_general(pos, x, NT, preferred_element_type=F32)
            power = (center_sq + half_sq_row(x) - cross) * rate
            yield jnp.exp2(power).astype(BF16)


def store_values(pos_ref, spread_ref, refs, out_ref):
    at = 0
    for part in own_values(pos_ref, spread_ref, refs):
        out_ref[:, at : at + part.shape[1]] = part
        at += part.shape[1]


def forward(rows, centers, out_width, cost):
    counts = [r.shape[0] for r in rows]

    def body(*refs):
        row_refs, refs, outs = refs[: len(rows)], refs[len(rows) : -len(rows)], refs[-len(rows) :]
        x = jnp.concatenate([ref[...] for ref in row_refs])
        total = partial_pred(x, refs, None)
        at = 0
        for ref, count in zip(outs, counts):
            ref[...] = total[at : at + count]
            at += count

    return pl.pallas_call(
        body,
        out_shape=tuple(jax.ShapeDtypeStruct((count, out_width), F32) for count in counts),
        in_specs=[VMEM] * (len(rows) + len(centers)),
        out_specs=(VMEM,) * len(rows),
        compiler_params=params(24),
        cost_estimate=cost,
        name="forward",
    )(*rows, *centers)


def own_kernel(center_pos, spread, blocks):
    n = spread.shape[1]
    points = sum(b.shape[0] for b in blocks)

    def body(pos_ref, spread_ref, *refs):
        store_values(pos_ref, spread_ref, refs[:-1], refs[-1])

    return pl.pallas_call(
        body,
        out_shape=jax.ShapeDtypeStruct((n, points), BF16),
        in_specs=[VMEM] * (2 + len(blocks)),
        out_specs=VMEM,
        compiler_params=params(16),
        cost_estimate=BRIEF,
        name="own_kernel",
    )(center_pos, spread, *blocks)


def own_rows(rows, centers, out_width, received, center_pos, spread, more):
    n = spread.shape[1]
    ends = [1, 1 + len(centers)]
    ends.append(ends[-1] + len(received))

    def body(*refs):
        outs, refs = refs[-1 - len(more) :], refs[: -1 - len(more)]
        total = None
        for ref in refs[ends[1] : ends[2]]:
            total = ref[...] if total is None else total + ref[...]
        outs[0][...] = partial_pred(refs[0][...], refs[1 : ends[1]], total)
        pos_ref, spread_ref, *block_refs = refs[ends[2] :]
        for k, blocks in enumerate(more):
            store_values(pos_ref, spread_ref, block_refs[: len(blocks)], outs[1 + k])
            del block_refs[: len(blocks)]

    ins = [rows, *centers, *received, center_pos, spread]
    ins += [block for blocks in more for block in blocks]
    return pl.pallas_call(
        body,
        out_shape=(jax.ShapeDtypeStruct((rows.shape[0], out_width), F32),)
        + tuple(jax.ShapeDtypeStruct((n, sum(b.shape[0] for b in blocks)), BF16) for blocks in more),
        in_specs=[VMEM] * len(ins),
        out_specs=(VMEM,) * (1 + len(more)),
        compiler_params=params(16),
        cost_estimate=COVER,
        name="own_rows",
    )(*ins)


def cotangent(parts, saved, target, delta):
    def body(*refs):
        saved_ref, target_ref, delta_ref, out_ref = refs[-4:]
        pred = refs[0][...]
        for ref in refs[1:-4]:
            pred += ref[...]
        residual = pred + saved_ref[...] - target_ref[...]
        ratio = residual / delta_ref[...]
        out_ref[...] = (residual / jnp.sqrt(1.0 + ratio * ratio)).astype(BF16)

    return pl.pallas_call(
        body,
        out_shape=jax.ShapeDtypeStruct(saved.shape, BF16),
        in_specs=[VMEM] * (len(parts) + 3),
        out_specs=VMEM,
        compiler_params=params(16),
        cost_estimate=BRIEF,
        name="cotangent",
    )(*parts, saved, target, delta)


def group_terms(coef, kernel, x, cot):
    mixing = lax.dot_general(coef, cot, NT, preferred_element_type=F32)
    weights = (kernel.astype(F32) * mixing).astype(BF16)
    lanes = weights[:, :128].astype(F32)
    for k in range(128, kernel.shape[1], 128):
        lanes += weights[:, k : k + 128].astype(F32)
    return (
        jnp.dot(weights, x, preferred_element_type=F32),
        jnp.dot(kernel, cot, preferred_element_type=F32),
        lanes,
    )


def backward(center_pos, coefficients, spread, groups, before=None, more=()):
    (n, out_width), in_width = coefficients.shape, center_pos.shape[1]
    flat = []
    for kernel, xs, cot in groups:
        flat += [*xs, cot] if kernel is None else [kernel, *xs, cot]
    carried = [] if before is None else list(before)
    outs = 3 + len(more)
    wanted = [block for blocks in more for block in blocks]

    def body(pos_ref, coef_ref, spread_ref, *refs):
        refs, out_refs = list(refs[:-outs]), refs[-outs:]
        coef = coef_ref[...]
        sums = [ref[...] for ref in refs[len(flat) : len(flat) + 3]] if carried else None
        block_refs = refs[len(flat) + len(carried) :]
        for k, blocks in enumerate(more):
            store_values(pos_ref, spread_ref, block_refs[: len(blocks)], out_refs[3 + k])
            del block_refs[: len(blocks)]
        for given, xs, _ in groups:
            kernel = None if given is None else refs.pop(0)[...]
            x_refs = [refs.pop(0) for _ in xs]
            if given is None:
                kernel = jnp.concatenate(list(own_values(pos_ref, spread_ref, x_refs)), axis=1)
            x = jnp.concatenate([ref[...] for ref in x_refs])
            terms = group_terms(coef, kernel, x, refs.pop(0)[...])
            sums = terms if sums is None else [a + b for a, b in zip(sums, terms)]
        for ref, value in zip(out_refs[:3], sums):
            ref[...] = value

    return pl.pallas_call(
        body,
        out_shape=tuple(jax.ShapeDtypeStruct((n, width), F32) for width in (in_width, out_width, 128))
        + tuple(jax.ShapeDtypeStruct((n, sum(b.shape[0] for b in blocks)), BF16) for blocks in more),
        in_specs=[VMEM] * (3 + len(flat) + len(carried) + len(wanted)),
        out_specs=(VMEM,) * outs,
        compiler_params=params(24),
        cost_estimate=COVER if more else BRIEF,
        name="backward",
    )(center_pos, coefficients, spread, *flat, *carried, *wanted)


def finish(center_pos, coefficients, spread, group, before):
    (n, out_width), in_width = coefficients.shape, center_pos.shape[1]
    kernel, xs, cot = group
    step = min(n, 256)

    def body(pos_ref, coef_ref, spread_ref, kernel_ref, cot_ref, *refs):
        x_refs, refs = refs[: len(xs)], refs[len(xs) :]
        moment_ref, grad_ref, lanes_ref, centers_out, coef_out, centers_buf, coef_buf, sems = refs
        x = jnp.concatenate([ref[...] for ref in x_refs])
        cot = cot_ref[...]
        scale = column(spread_ref[...].astype(F32)) * (2.0 / in_width)
        made = []
        for k, start in enumerate(range(0, n, step)):
            rows = slice(start, start + step)
            moment, grad, lanes = group_terms(coef_ref[rows], kernel_ref[rows], x, cot)
            coef_buf[rows] = grad_ref[rows] + grad
            moment += moment_ref[rows]
            total = jnp.sum(lanes_ref[rows] + lanes, axis=1, keepdims=True)
            for at in range(0, in_width, 128):
                pos = pos_ref[rows, at : at + 128].astype(F32)
                centers_buf[rows, at : at + 128] = scale[rows] * (moment[:, at : at + 128] - total * pos)
            pairs = [(centers_buf, centers_out), (coef_buf, coef_out)]
            for j, (src, dst) in enumerate(pairs):
                copy = pltpu.make_async_copy(src.at[rows], dst.at[rows], sems.at[2 * k + j])
                copy.start()
                made.append(copy)
        for copy in made:
            copy.wait()

    ins = [center_pos, coefficients, spread, kernel, cot, *xs, *before]
    return pl.pallas_call(
        body,
        out_shape=tuple(jax.ShapeDtypeStruct((n, width), F32) for width in (in_width, out_width)),
        in_specs=[VMEM] * len(ins),
        out_specs=(HBM, HBM),
        scratch_shapes=[
            pltpu.VMEM((n, in_width), F32),
            pltpu.VMEM((n, out_width), F32),
            pltpu.SemaphoreType.DMA((2 * pl.cdiv(n, step),)),
        ],
        compiler_params=params(24),
        cost_estimate=BRIEF,
        name="finish",
    )(*ins)


def solution(mesh):
    nz, nc = mesh.shape["points"], mesh.shape["centers"]

    def per_device(train_points, saved_preds, targets, huber_delta, center_pos, coefficients, spread):
        n_rows = train_points.shape[0]
        n, out_width = coefficients.shape
        piece = n_rows // nc

        own = lax.dynamic_slice_in_dim(train_points, lax.axis_index("centers") * piece, piece)

        layer = {0: own}
        for dz in range(2, nz, 2):
            layer[dz] = swap(own, "points", nz, dz)
        layer[1] = swap(own, "points", nz, 1)

        pos, side = {1: swap(center_pos, "centers", nc, 1)}, {}
        for d in range(2, nc, 2):
            pos[d] = swap(center_pos, "centers", nc, d)
        center_pos, side[0], delta, spread, coefficients = pack(
            after(center_pos, own), coefficients, spread, huber_delta
        )
        pos[0], side[1] = center_pos, swap(side[0], "centers", nc, 1)
        for d in range(2, nc, 2):
            side[d] = swap(side[0], "centers", nc, d)
        for dz in range(3, nz, 2):
            layer[dz] = swap(layer[dz - 1], "points", nz, 1)
        saved, target, *local = take(
            [saved_preds, targets] + [train_points] * (nc - 1), [0, 0, *range(1, nc)], piece
        )
        local = [own, *local]
        for d in range(2, nc, 2):
            pos[d + 1] = swap(after(pos[d], layer[1], layer[2], side[1], side[d], saved), "centers", nc, 1)
            side[d + 1] = swap(after(side[d], layer[2], side[1]), "centers", nc, 1)
        centers = [a for d in range(nc) for a in (pos[d], side[d])]

        early = {0: jnp.concatenate([layer[dz] for dz in range(1, nz - 1)])}

        first, second = range(2, nz, 2), range(3, nz, 2)
        parts = dict(zip(first, forward([layer[dz] for dz in first], centers, out_width, BRIEF)))
        received = {dz: swap(parts[dz], "points", nz, dz) for dz in first}
        rows = [after(layer[1], *parts.values())]
        (parts[1],) = forward(rows, centers, out_width, COVER)
        received[1] = swap(parts[1], "points", nz, 1)
        rows = [after(layer[dz], *parts.values()) for dz in second]
        parts.update(zip(second, forward(rows, centers, out_width, COVER)))
        soon = list(received.values())
        received = [swap(parts[dz], "points", nz, dz) for dz in second]
        last = parts[nz - 1]
        kernels, late = {1: None}, {0: layer[nz - 1]}
        parts[0], kernels[0] = own_rows(
            after(own, last),
            centers,
            out_width,
            soon,
            center_pos,
            spread,
            [[local[0], early[0], late[0]]],
        )
        for d in range(2, nc, 2):
            early[d] = swap(after(early[0], side[d]), "centers", nc, d)
            late[d] = swap(after(late[0], last, *soon), "centers", nc, d)
            early[d + 1] = swap(after(early[d], parts[0]), "centers", nc, 1)
        early[1] = swap(after(early[0], parts[0]), "centers", nc, 1)
        late[1] = swap(after(late[0], parts[0]), "centers", nc, 1)
        cot = cotangent([parts[0], *received], saved, target, delta)

        far = {dz: swap(cot, "points", nz, dz) for dz in (*range(2, nz), 1)}
        ahead = {d: swap(after(cot, late[d]), "centers", nc, d) for d in range(2, nc, 2)}
        far[1] = after(far[1], *ahead.values())
        far = jnp.concatenate([far[dz] for dz in range(1, nz)])
        cots = {0: jnp.concatenate([cot, far])}
        across = {}
        for d in range(2, nc, 2):
            across[d] = [ahead[d], swap(far, "centers", nc, d)]
            late[d + 1] = swap(after(late[d], far), "centers", nc, 1)
        cots[1] = swap(cots[0], "centers", nc, 1)

        points = {d: [local[d], early[d], late[d]] for d in range(nc)}
        groups = [(kernels[d], points[d], cots[d]) for d in (0, 1)]
        *sums, kernels[2], kernels[3] = backward(
            center_pos, coefficients, spread, groups, more=[points[2], points[3]]
        )
        for d in range(4, nc):
            kernels[d] = own_kernel(center_pos, spread, points[d])
        for d in range(2, nc, 2):
            cots[d] = jnp.concatenate([after(a, sums[0]) for a in across[d]])
            cots[d + 1] = swap(cots[d], "centers", nc, 1)
        for d in range(2, nc - 1):
            group = (kernels[d], points[d], cots[d])
            sums = backward(center_pos, coefficients, spread, [group], before=sums)
        group = (kernels[nc - 1], points[nc - 1], cots[nc - 1])
        return finish(center_pos, coefficients, spread, group, sums)

    return jax.shard_map(
        per_device,
        mesh=mesh,
        in_specs=(
            P(("groups", "points"), None),
            P(("groups", "points"), None),
            P(("groups", "points"), None),
            P("groups"),
            P(("groups", "points", "centers"), None),
            P(("groups", "points", "centers"), None),
            P(("groups", "points", "centers")),
        ),
        out_specs=(
            P(("groups", "points", "centers"), None),
            P(("groups", "points", "centers"), None),
        ),
        check_vma=False,
    )
```

```python
import math

import jax
import jax.numpy as jnp
from jax import lax
from jax.experimental import pallas as pl
from jax.experimental.pallas import tpu as pltpu
from jax.sharding import PartitionSpec as P

F32, BF16 = jnp.float32, jnp.bfloat16
HBM = pl.BlockSpec(memory_space=pltpu.HBM)
VMEM = pl.BlockSpec(memory_space=pltpu.VMEM)
NT = (((1,), (1,)), ((), ()))
LOG2E = math.log2(math.e)
COVER = pl.CostEstimate(flops=1 << 34, bytes_accessed=1 << 20, transcendentals=1 << 20)
BRIEF = pl.CostEstimate(flops=1, bytes_accessed=1, transcendentals=0)


def swap(a, axis, size, d):
    return lax.ppermute(a, axis, [(i, i ^ d) for i in range(size)])


def after(a, *others):
    return lax.optimization_barrier((a, *others))[0]


def lane_groups(a):
    total = None
    for k in range(0, a.shape[1], 128):
        part = jnp.square(a[:, k : k + 128].astype(F32))
        total = part if total is None else total + part
    return total


def half_sq_row(a):
    return 0.5 * jnp.sum(lane_groups(a).T, axis=0, keepdims=True)


def half_sq_column(a):
    return 0.5 * jnp.sum(lane_groups(a), axis=1, keepdims=True)


def column(row):
    return jnp.broadcast_to(row, (128, row.shape[1])).T


def params(mib):
    return pltpu.CompilerParams(vmem_limit_bytes=mib << 20)


def pack(center_pos, coefficients, spread, delta):
    n, in_width = center_pos.shape
    out_width = coefficients.shape[1]
    across = in_width // out_width
    q = n // across

    def body(pos_ref, coef_ref, spread_ref, delta_ref, own_pos, out_ref, row_ref, own_spread, own_coef):
        row_ref[...] = delta_ref[...]
        own_spread[...] = spread_ref[...]
        own_coef[...] = coef_ref[...]
        pos = pos_ref[...]
        own_pos[...] = pos
        for k in range(across):
            out_ref[:q, k * out_width : (k + 1) * out_width] = coef_ref[k * q : (k + 1) * q]
        half = half_sq_row(pos)
        high = half.astype(BF16)
        rest = half - high.astype(F32)
        middle = rest.astype(BF16)
        low = (rest - middle.astype(F32)).astype(BF16)
        rows = [r.astype(F32) for r in (spread_ref[...], high, middle, low)]
        tail = jnp.concatenate(rows + [jnp.zeros((12, n), F32)]).astype(BF16)
        if n < in_width:
            tail = jnp.concatenate([tail, jnp.zeros((16, in_width - n), BF16)], axis=1)
        out_ref[q:] = tail

    return pl.pallas_call(
        body,
        out_shape=(
            jax.ShapeDtypeStruct((n, in_width), BF16),
            jax.ShapeDtypeStruct((q + 16, in_width), BF16),
            jax.ShapeDtypeStruct((1, delta.shape[0]), F32),
            jax.ShapeDtypeStruct((1, n), BF16),
            jax.ShapeDtypeStruct((n, out_width), BF16),
        ),
        in_specs=[VMEM] * 4,
        out_specs=(VMEM,) * 5,
        compiler_params=params(16),
        cost_estimate=BRIEF,
        name="pack",
    )(center_pos, coefficients, spread.reshape(1, n), delta.reshape(1, -1))


def take(arrays, offsets, piece):
    def body(*refs):
        ins, outs, sems = refs[: len(arrays)], refs[len(arrays) : -1], refs[-1]
        made = []
        for k, d in enumerate(offsets):
            start = pl.multiple_of((lax.axis_index("centers") ^ d) * piece, piece)
            made.append(pltpu.make_async_copy(ins[k].at[pl.ds(start, piece)], outs[k], sems.at[k]))
            made[-1].start()
        for copy in made:
            copy.wait()

    return pl.pallas_call(
        body,
        out_shape=tuple(jax.ShapeDtypeStruct((piece, a.shape[1]), a.dtype) for a in arrays),
        in_specs=[HBM] * len(arrays),
        out_specs=(VMEM,) * len(arrays),
        scratch_shapes=[pltpu.SemaphoreType.DMA((len(arrays),))],
        compiler_params=params(16),
        cost_estimate=BRIEF,
        name="take",
    )(*arrays)


def partial_pred(x, refs, total):
    in_width = x.shape[1]
    row_sq = half_sq_column(x)
    for pos_ref, side_ref in zip(refs[::2], refs[1::2]):
        n, q = pos_ref.shape[0], side_ref.shape[0] - 16
        out_width = q * in_width // n
        packed = side_ref[:q]
        coef = jnp.concatenate([packed[:, k : k + out_width] for k in range(0, in_width, out_width)])
        tail = side_ref[q:, :n].astype(F32)
        center_sq = tail[1:2] + tail[2:3] + tail[3:4]
        rate = tail[0:1] * (-2.0 * LOG2E / in_width)
        cross = lax.dot_general(x, pos_ref[...], NT, preferred_element_type=F32)
        power = (row_sq + center_sq - cross) * rate
        kernel = jnp.exp2(power).astype(BF16)
        new = jnp.dot(kernel, coef, preferred_element_type=F32)
        total = new if total is None else total + new
    return total


def own_values(pos_ref, spread_ref, refs):
    pos = pos_ref[...]
    center_sq = half_sq_column(pos)
    rate = column(spread_ref[...].astype(F32) * (-2.0 * LOG2E / pos.shape[1]))[:, :1]
    for ref in refs:
        step = min(256, ref.shape[0])
        for start in range(0, ref.shape[0], step):
            x = ref[start : start + step]
            cross = lax.dot_general(pos, x, NT, preferred_element_type=F32)
            power = (center_sq + half_sq_row(x) - cross) * rate
            yield jnp.exp2(power).astype(BF16)


def store_values(pos_ref, spread_ref, refs, out_ref):
    at = 0
    for part in own_values(pos_ref, spread_ref, refs):
        out_ref[:, at : at + part.shape[1]] = part
        at += part.shape[1]


def forward(rows, centers, out_width, cost):
    counts = [r.shape[0] for r in rows]

    def body(*refs):
        row_refs, refs, outs = refs[: len(rows)], refs[len(rows) : -len(rows)], refs[-len(rows) :]
        x = jnp.concatenate([ref[...] for ref in row_refs])
        total = partial_pred(x, refs, None)
        at = 0
        for ref, count in zip(outs, counts):
            ref[...] = total[at : at + count]
            at += count

    return pl.pallas_call(
        body,
        out_shape=tuple(jax.ShapeDtypeStruct((count, out_width), F32) for count in counts),
        in_specs=[VMEM] * (len(rows) + len(centers)),
        out_specs=(VMEM,) * len(rows),
        compiler_params=params(24),
        cost_estimate=cost,
        name="forward",
    )(*rows, *centers)


def own_kernel(center_pos, spread, blocks):
    n = spread.shape[1]
    points = sum(b.shape[0] for b in blocks)

    def body(pos_ref, spread_ref, *refs):
        store_values(pos_ref, spread_ref, refs[:-1], refs[-1])

    return pl.pallas_call(
        body,
        out_shape=jax.ShapeDtypeStruct((n, points), BF16),
        in_specs=[VMEM] * (2 + len(blocks)),
        out_specs=VMEM,
        compiler_params=params(16),
        cost_estimate=BRIEF,
        name="own_kernel",
    )(center_pos, spread, *blocks)


def own_rows(rows, centers, out_width, received, center_pos, spread, more):
    n = spread.shape[1]
    ends = [1, 1 + len(centers)]
    ends.append(ends[-1] + len(received))

    def body(*refs):
        outs, refs = refs[-1 - len(more) :], refs[: -1 - len(more)]
        total = None
        for ref in refs[ends[1] : ends[2]]:
            total = ref[...] if total is None else total + ref[...]
        outs[0][...] = partial_pred(refs[0][...], refs[1 : ends[1]], total)
        pos_ref, spread_ref, *block_refs = refs[ends[2] :]
        for k, blocks in enumerate(more):
            store_values(pos_ref, spread_ref, block_refs[: len(blocks)], outs[1 + k])
            del block_refs[: len(blocks)]

    ins = [rows, *centers, *received, center_pos, spread]
    ins += [block for blocks in more for block in blocks]
    return pl.pallas_call(
        body,
        out_shape=(jax.ShapeDtypeStruct((rows.shape[0], out_width), F32),)
        + tuple(jax.ShapeDtypeStruct((n, sum(b.shape[0] for b in blocks)), BF16) for blocks in more),
        in_specs=[VMEM] * len(ins),
        out_specs=(VMEM,) * (1 + len(more)),
        compiler_params=params(16),
        cost_estimate=COVER,
        name="own_rows",
    )(*ins)


def cotangent(parts, saved, target, delta):
    def body(*refs):
        saved_ref, target_ref, delta_ref, out_ref = refs[-4:]
        pred = refs[0][...]
        for ref in refs[1:-4]:
            pred += ref[...]
        residual = pred + saved_ref[...] - target_ref[...]
        ratio = residual / delta_ref[...]
        out_ref[...] = (residual / jnp.sqrt(1.0 + ratio * ratio)).astype(BF16)

    return pl.pallas_call(
        body,
        out_shape=jax.ShapeDtypeStruct(saved.shape, BF16),
        in_specs=[VMEM] * (len(parts) + 3),
        out_specs=VMEM,
        compiler_params=params(16),
        cost_estimate=BRIEF,
        name="cotangent",
    )(*parts, saved, target, delta)


def group_terms(coef, kernel, x, cot):
    mixing = lax.dot_general(coef, cot, NT, preferred_element_type=F32)
    weights = (kernel.astype(F32) * mixing).astype(BF16)
    lanes = weights[:, :128].astype(F32)
    for k in range(128, kernel.shape[1], 128):
        lanes += weights[:, k : k + 128].astype(F32)
    return (
        jnp.dot(weights, x, preferred_element_type=F32),
        jnp.dot(kernel, cot, preferred_element_type=F32),
        lanes,
    )


def backward(center_pos, coefficients, spread, groups, before=None, more=()):
    (n, out_width), in_width = coefficients.shape, center_pos.shape[1]
    flat = []
    for kernel, xs, cot in groups:
        flat += [*xs, cot] if kernel is None else [kernel, *xs, cot]
    carried = [] if before is None else list(before)
    outs = 3 + len(more)
    wanted = [block for blocks in more for block in blocks]

    def body(pos_ref, coef_ref, spread_ref, *refs):
        refs, out_refs = list(refs[:-outs]), refs[-outs:]
        coef = coef_ref[...]
        sums = [ref[...] for ref in refs[len(flat) : len(flat) + 3]] if carried else None
        block_refs = refs[len(flat) + len(carried) :]
        for k, blocks in enumerate(more):
            store_values(pos_ref, spread_ref, block_refs[: len(blocks)], out_refs[3 + k])
            del block_refs[: len(blocks)]
        for given, xs, _ in groups:
            kernel = None if given is None else refs.pop(0)[...]
            x_refs = [refs.pop(0) for _ in xs]
            if given is None:
                kernel = jnp.concatenate(list(own_values(pos_ref, spread_ref, x_refs)), axis=1)
            x = jnp.concatenate([ref[...] for ref in x_refs])
            terms = group_terms(coef, kernel, x, refs.pop(0)[...])
            sums = terms if sums is None else [a + b for a, b in zip(sums, terms)]
        for ref, value in zip(out_refs[:3], sums):
            ref[...] = value

    return pl.pallas_call(
        body,
        out_shape=tuple(jax.ShapeDtypeStruct((n, width), F32) for width in (in_width, out_width, 128))
        + tuple(jax.ShapeDtypeStruct((n, sum(b.shape[0] for b in blocks)), BF16) for blocks in more),
        in_specs=[VMEM] * (3 + len(flat) + len(carried) + len(wanted)),
        out_specs=(VMEM,) * outs,
        compiler_params=params(24),
        cost_estimate=COVER if more else BRIEF,
        name="backward",
    )(center_pos, coefficients, spread, *flat, *carried, *wanted)


def finish(center_pos, coefficients, spread, group, before):
    (n, out_width), in_width = coefficients.shape, center_pos.shape[1]
    kernel, xs, cot = group
    step = min(n, 256)

    def body(pos_ref, coef_ref, spread_ref, kernel_ref, cot_ref, *refs):
        x_refs, refs = refs[: len(xs)], refs[len(xs) :]
        moment_ref, grad_ref, lanes_ref, centers_out, coef_out, centers_buf, coef_buf, sems = refs
        x = jnp.concatenate([ref[...] for ref in x_refs])
        cot = cot_ref[...]
        scale = column(spread_ref[...].astype(F32)) * (2.0 / in_width)
        made = []
        for k, start in enumerate(range(0, n, step)):
            rows = slice(start, start + step)
            moment, grad, lanes = group_terms(coef_ref[rows], kernel_ref[rows], x, cot)
            coef_buf[rows] = grad_ref[rows] + grad
            moment += moment_ref[rows]
            total = jnp.sum(lanes_ref[rows] + lanes, axis=1, keepdims=True)
            for at in range(0, in_width, 128):
                pos = pos_ref[rows, at : at + 128].astype(F32)
                centers_buf[rows, at : at + 128] = scale[rows] * (moment[:, at : at + 128] - total * pos)
            pairs = [(centers_buf, centers_out), (coef_buf, coef_out)]
            for j, (src, dst) in enumerate(pairs):
                copy = pltpu.make_async_copy(src.at[rows], dst.at[rows], sems.at[2 * k + j])
                copy.start()
                made.append(copy)
        for copy in made:
            copy.wait()

    ins = [center_pos, coefficients, spread, kernel, cot, *xs, *before]
    return pl.pallas_call(
        body,
        out_shape=tuple(jax.ShapeDtypeStruct((n, width), F32) for width in (in_width, out_width)),
        in_specs=[VMEM] * len(ins),
        out_specs=(HBM, HBM),
        scratch_shapes=[
            pltpu.VMEM((n, in_width), F32),
            pltpu.VMEM((n, out_width), F32),
            pltpu.SemaphoreType.DMA((2 * pl.cdiv(n, step),)),
        ],
        compiler_params=params(24),
        cost_estimate=BRIEF,
        name="finish",
    )(*ins)


def solution(mesh):
    nz, nc = mesh.shape["points"], mesh.shape["centers"]

    def per_device(train_points, saved_preds, targets, huber_delta, center_pos, coefficients, spread):
        n_rows = train_points.shape[0]
        n, out_width = coefficients.shape
        piece = n_rows // nc

        own = lax.dynamic_slice_in_dim(train_points, lax.axis_index("centers") * piece, piece)

        layer = {0: own}
        for dz in range(2, nz, 2):
            layer[dz] = swap(own, "points", nz, dz)
        layer[1] = swap(own, "points", nz, 1)

        pos, side = {1: swap(center_pos, "centers", nc, 1)}, {}
        for d in range(2, nc, 2):
            pos[d] = swap(center_pos, "centers", nc, d)
        center_pos, side[0], delta, spread, coefficients = pack(
            after(center_pos, own), coefficients, spread, huber_delta
        )
        pos[0], side[1] = center_pos, swap(side[0], "centers", nc, 1)
        for d in range(2, nc, 2):
            side[d] = swap(side[0], "centers", nc, d)
        for dz in range(3, nz, 2):
            layer[dz] = swap(layer[dz - 1], "points", nz, 1)
        saved, target, *local = take(
            [saved_preds, targets] + [train_points] * (nc - 1), [0, 0, *range(1, nc)], piece
        )
        local = [own, *local]
        for d in range(2, nc, 2):
            pos[d + 1] = swap(after(pos[d], layer[1], layer[2], side[1], side[d], saved), "centers", nc, 1)
            side[d + 1] = swap(after(side[d], layer[2], side[1]), "centers", nc, 1)
        centers = [a for d in range(nc) for a in (pos[d], side[d])]

        early = {0: jnp.concatenate([layer[dz] for dz in range(1, nz - 1)])}

        first, second = range(2, nz, 2), range(3, nz, 2)
        parts = dict(zip(first, forward([layer[dz] for dz in first], centers, out_width, BRIEF)))
        received = {dz: swap(parts[dz], "points", nz, dz) for dz in first}
        rows = [after(layer[1], *parts.values())]
        (parts[1],) = forward(rows, centers, out_width, COVER)
        received[1] = swap(parts[1], "points", nz, 1)
        rows = [after(layer[dz], *parts.values()) for dz in second]
        parts.update(zip(second, forward(rows, centers, out_width, COVER)))
        soon = list(received.values())
        received = [swap(parts[dz], "points", nz, dz) for dz in second]
        last = parts[nz - 1]
        kernels, late = {1: None}, {0: layer[nz - 1]}
        parts[0], kernels[0] = own_rows(
            after(own, last),
            centers,
            out_width,
            soon,
            center_pos,
            spread,
            [[local[0], early[0], late[0]]],
        )
        for d in range(2, nc, 2):
            early[d] = swap(after(early[0], side[d + 1]), "centers", nc, d)
            late[d] = swap(after(late[0], last, *soon), "centers", nc, d)
            early[d + 1] = swap(after(early[d], parts[0]), "centers", nc, 1)
        early[1] = swap(after(early[0], parts[0]), "centers", nc, 1)
        late[1] = swap(after(late[0], parts[0]), "centers", nc, 1)
        cot = cotangent([parts[0], *received], saved, target, delta)

        far = {dz: swap(cot, "points", nz, dz) for dz in range(2, nz, 2)}
        far[1] = swap(cot, "points", nz, 1)
        for d in range(2, nc, 2):
            kernels[d] = own_kernel(center_pos, spread, [local[d], early[d], late[d]])
        held = [kernels[d] for d in range(2, nc, 2)]
        far.update({dz: swap(after(far[dz - 1], *held), "points", nz, 1) for dz in range(3, nz, 2)})
        ahead = {d: swap(after(cot, late[d]), "centers", nc, d) for d in range(2, nc, 2)}
        far[1] = after(far[1], *ahead.values())
        far = jnp.concatenate([far[dz] for dz in range(1, nz)])
        cots = {0: jnp.concatenate([cot, far])}
        across = {}
        for d in range(2, nc, 2):
            across[d] = [ahead[d], swap(far, "centers", nc, d)]
            late[d + 1] = swap(after(late[d], far), "centers", nc, 1)
        cots[1] = swap(cots[0], "centers", nc, 1)

        points = {d: [local[d], early[d], late[d]] for d in range(nc)}
        groups = [(kernels[d], points[d], cots[d]) for d in (0, 1)]
        *sums, kernels[3] = backward(
            center_pos, coefficients, spread, groups, more=[points[3]]
        )
        for d in range(5, nc, 2):
            kernels[d] = own_kernel(center_pos, spread, points[d])
        for d in range(2, nc, 2):
            cots[d] = jnp.concatenate([after(a, sums[0]) for a in across[d]])
            cots[d + 1] = swap(cots[d], "centers", nc, 1)
        for d in range(2, nc - 1):
            group = (kernels[d], points[d], cots[d])
            sums = backward(center_pos, coefficients, spread, [group], before=sums)
        group = (kernels[nc - 1], points[nc - 1], cots[nc - 1])
        return finish(center_pos, coefficients, spread, group, sums)

    return jax.shard_map(
        per_device,
        mesh=mesh,
        in_specs=(
            P(("groups", "points"), None),
            P(("groups", "points"), None),
            P(("groups", "points"), None),
            P("groups"),
            P(("groups", "points", "centers"), None),
            P(("groups", "points", "centers"), None),
            P(("groups", "points", "centers")),
        ),
        out_specs=(
            P(("groups", "points", "centers"), None),
            P(("groups", "points", "centers"), None),
        ),
        check_vma=False,
    )
```

```python
import math

import jax
import jax.numpy as jnp
from jax import lax
from jax.experimental import pallas as pl
from jax.experimental.pallas import tpu as pltpu
from jax.sharding import PartitionSpec as P

F32, BF16 = jnp.float32, jnp.bfloat16
HBM = pl.BlockSpec(memory_space=pltpu.HBM)
VMEM = pl.BlockSpec(memory_space=pltpu.VMEM)
NT = (((1,), (1,)), ((), ()))
LOG2E = math.log2(math.e)
COVER = pl.CostEstimate(flops=1 << 34, bytes_accessed=1 << 20, transcendentals=1 << 20)
BRIEF = pl.CostEstimate(flops=1, bytes_accessed=1, transcendentals=0)


def swap(a, axis, size, d):
    return lax.ppermute(a, axis, [(i, i ^ d) for i in range(size)])


def after(a, *others):
    return lax.optimization_barrier((a, *others))[0]


def lane_groups(a):
    total = None
    for k in range(0, a.shape[1], 128):
        part = jnp.square(a[:, k : k + 128].astype(F32))
        total = part if total is None else total + part
    return total


def half_sq_row(a):
    return 0.5 * jnp.sum(lane_groups(a).T, axis=0, keepdims=True)


def half_sq_column(a):
    return 0.5 * jnp.sum(lane_groups(a), axis=1, keepdims=True)


def column(row):
    return jnp.broadcast_to(row, (128, row.shape[1])).T


def params(mib):
    return pltpu.CompilerParams(vmem_limit_bytes=mib << 20)


def pack(center_pos, coefficients, spread, delta):
    n, in_width = center_pos.shape
    out_width = coefficients.shape[1]
    across = in_width // out_width
    q = n // across

    def body(pos_ref, coef_ref, spread_ref, delta_ref, own_pos, out_ref, row_ref, own_spread, own_coef):
        row_ref[...] = delta_ref[...]
        own_spread[...] = spread_ref[...]
        own_coef[...] = coef_ref[...]
        pos = pos_ref[...]
        own_pos[...] = pos
        for k in range(across):
            out_ref[:q, k * out_width : (k + 1) * out_width] = coef_ref[k * q : (k + 1) * q]
        half = half_sq_row(pos)
        high = half.astype(BF16)
        rest = half - high.astype(F32)
        middle = rest.astype(BF16)
        low = (rest - middle.astype(F32)).astype(BF16)
        rows = [r.astype(F32) for r in (spread_ref[...], high, middle, low)]
        tail = jnp.concatenate(rows + [jnp.zeros((12, n), F32)]).astype(BF16)
        if n < in_width:
            tail = jnp.concatenate([tail, jnp.zeros((16, in_width - n), BF16)], axis=1)
        out_ref[q:] = tail

    return pl.pallas_call(
        body,
        out_shape=(
            jax.ShapeDtypeStruct((n, in_width), BF16),
            jax.ShapeDtypeStruct((q + 16, in_width), BF16),
            jax.ShapeDtypeStruct((1, delta.shape[0]), F32),
            jax.ShapeDtypeStruct((1, n), BF16),
            jax.ShapeDtypeStruct((n, out_width), BF16),
        ),
        in_specs=[VMEM] * 4,
        out_specs=(VMEM,) * 5,
        compiler_params=params(16),
        cost_estimate=BRIEF,
        name="pack",
    )(center_pos, coefficients, spread.reshape(1, n), delta.reshape(1, -1))


def take(arrays, offsets, piece):
    def body(*refs):
        ins, outs, sems = refs[: len(arrays)], refs[len(arrays) : -1], refs[-1]
        made = []
        for k, d in enumerate(offsets):
            start = pl.multiple_of((lax.axis_index("centers") ^ d) * piece, piece)
            made.append(pltpu.make_async_copy(ins[k].at[pl.ds(start, piece)], outs[k], sems.at[k]))
            made[-1].start()
        for copy in made:
            copy.wait()

    return pl.pallas_call(
        body,
        out_shape=tuple(jax.ShapeDtypeStruct((piece, a.shape[1]), a.dtype) for a in arrays),
        in_specs=[HBM] * len(arrays),
        out_specs=(VMEM,) * len(arrays),
        scratch_shapes=[pltpu.SemaphoreType.DMA((len(arrays),))],
        compiler_params=params(16),
        cost_estimate=BRIEF,
        name="take",
    )(*arrays)


def partial_pred(x, refs, total):
    in_width = x.shape[1]
    row_sq = half_sq_column(x)
    for pos_ref, side_ref in zip(refs[::2], refs[1::2]):
        n, q = pos_ref.shape[0], side_ref.shape[0] - 16
        out_width = q * in_width // n
        packed = side_ref[:q]
        coef = jnp.concatenate([packed[:, k : k + out_width] for k in range(0, in_width, out_width)])
        tail = side_ref[q:, :n].astype(F32)
        center_sq = tail[1:2] + tail[2:3] + tail[3:4]
        rate = tail[0:1] * (-2.0 * LOG2E / in_width)
        cross = lax.dot_general(x, pos_ref[...], NT, preferred_element_type=F32)
        power = (row_sq + center_sq - cross) * rate
        kernel = jnp.exp2(power).astype(BF16)
        new = jnp.dot(kernel, coef, preferred_element_type=F32)
        total = new if total is None else total + new
    return total


def own_values(pos_ref, spread_ref, refs):
    pos = pos_ref[...]
    center_sq = half_sq_column(pos)
    rate = column(spread_ref[...].astype(F32) * (-2.0 * LOG2E / pos.shape[1]))[:, :1]
    for ref in refs:
        step = min(256, ref.shape[0])
        for start in range(0, ref.shape[0], step):
            x = ref[start : start + step]
            cross = lax.dot_general(pos, x, NT, preferred_element_type=F32)
            power = (center_sq + half_sq_row(x) - cross) * rate
            yield jnp.exp2(power).astype(BF16)


def store_values(pos_ref, spread_ref, refs, out_ref):
    at = 0
    for part in own_values(pos_ref, spread_ref, refs):
        out_ref[:, at : at + part.shape[1]] = part
        at += part.shape[1]


def forward(rows, centers, out_width, cost):
    counts = [r.shape[0] for r in rows]

    def body(*refs):
        row_refs, refs, outs = refs[: len(rows)], refs[len(rows) : -len(rows)], refs[-len(rows) :]
        x = jnp.concatenate([ref[...] for ref in row_refs])
        total = partial_pred(x, refs, None)
        at = 0
        for ref, count in zip(outs, counts):
            ref[...] = total[at : at + count]
            at += count

    return pl.pallas_call(
        body,
        out_shape=tuple(jax.ShapeDtypeStruct((count, out_width), F32) for count in counts),
        in_specs=[VMEM] * (len(rows) + len(centers)),
        out_specs=(VMEM,) * len(rows),
        compiler_params=params(24),
        cost_estimate=cost,
        name="forward",
    )(*rows, *centers)


def own_kernel(center_pos, spread, blocks):
    n = spread.shape[1]
    points = sum(b.shape[0] for b in blocks)

    def body(pos_ref, spread_ref, *refs):
        store_values(pos_ref, spread_ref, refs[:-1], refs[-1])

    return pl.pallas_call(
        body,
        out_shape=jax.ShapeDtypeStruct((n, points), BF16),
        in_specs=[VMEM] * (2 + len(blocks)),
        out_specs=VMEM,
        compiler_params=params(16),
        cost_estimate=BRIEF,
        name="own_kernel",
    )(center_pos, spread, *blocks)


def own_rows(rows, centers, out_width, received, center_pos, spread, more):
    n = spread.shape[1]
    ends = [1, 1 + len(centers)]
    ends.append(ends[-1] + len(received))

    def body(*refs):
        outs, refs = refs[-1 - len(more) :], refs[: -1 - len(more)]
        total = None
        for ref in refs[ends[1] : ends[2]]:
            total = ref[...] if total is None else total + ref[...]
        outs[0][...] = partial_pred(refs[0][...], refs[1 : ends[1]], total)
        pos_ref, spread_ref, *block_refs = refs[ends[2] :]
        for k, blocks in enumerate(more):
            store_values(pos_ref, spread_ref, block_refs[: len(blocks)], outs[1 + k])
            del block_refs[: len(blocks)]

    ins = [rows, *centers, *received, center_pos, spread]
    ins += [block for blocks in more for block in blocks]
    return pl.pallas_call(
        body,
        out_shape=(jax.ShapeDtypeStruct((rows.shape[0], out_width), F32),)
        + tuple(jax.ShapeDtypeStruct((n, sum(b.shape[0] for b in blocks)), BF16) for blocks in more),
        in_specs=[VMEM] * len(ins),
        out_specs=(VMEM,) * (1 + len(more)),
        compiler_params=params(16),
        cost_estimate=COVER,
        name="own_rows",
    )(*ins)


def cotangent(parts, saved, target, delta):
    def body(*refs):
        saved_ref, target_ref, delta_ref, out_ref = refs[-4:]
        pred = refs[0][...]
        for ref in refs[1:-4]:
            pred += ref[...]
        residual = pred + saved_ref[...] - target_ref[...]
        ratio = residual / delta_ref[...]
        out_ref[...] = (residual / jnp.sqrt(1.0 + ratio * ratio)).astype(BF16)

    return pl.pallas_call(
        body,
        out_shape=jax.ShapeDtypeStruct(saved.shape, BF16),
        in_specs=[VMEM] * (len(parts) + 3),
        out_specs=VMEM,
        compiler_params=params(16),
        cost_estimate=BRIEF,
        name="cotangent",
    )(*parts, saved, target, delta)


def group_terms(coef, kernel, x, cot):
    mixing = lax.dot_general(coef, cot, NT, preferred_element_type=F32)
    weights = (kernel.astype(F32) * mixing).astype(BF16)
    lanes = weights[:, :128].astype(F32)
    for k in range(128, kernel.shape[1], 128):
        lanes += weights[:, k : k + 128].astype(F32)
    return (
        jnp.dot(weights, x, preferred_element_type=F32),
        jnp.dot(kernel, cot, preferred_element_type=F32),
        lanes,
    )


def backward(center_pos, coefficients, spread, groups, before=None, more=()):
    (n, out_width), in_width = coefficients.shape, center_pos.shape[1]
    flat = []
    for kernel, xs, cot in groups:
        flat += [*xs, cot] if kernel is None else [kernel, *xs, cot]
    carried = [] if before is None else list(before)
    outs = 3 + len(more)
    wanted = [block for blocks in more for block in blocks]

    def body(pos_ref, coef_ref, spread_ref, *refs):
        refs, out_refs = list(refs[:-outs]), refs[-outs:]
        coef = coef_ref[...]
        sums = [ref[...] for ref in refs[len(flat) : len(flat) + 3]] if carried else None
        block_refs = refs[len(flat) + len(carried) :]
        for k, blocks in enumerate(more):
            store_values(pos_ref, spread_ref, block_refs[: len(blocks)], out_refs[3 + k])
            del block_refs[: len(blocks)]
        for given, xs, _ in groups:
            kernel = None if given is None else refs.pop(0)[...]
            x_refs = [refs.pop(0) for _ in xs]
            if given is None:
                kernel = jnp.concatenate(list(own_values(pos_ref, spread_ref, x_refs)), axis=1)
            x = jnp.concatenate([ref[...] for ref in x_refs])
            terms = group_terms(coef, kernel, x, refs.pop(0)[...])
            sums = terms if sums is None else [a + b for a, b in zip(sums, terms)]
        for ref, value in zip(out_refs[:3], sums):
            ref[...] = value

    return pl.pallas_call(
        body,
        out_shape=tuple(jax.ShapeDtypeStruct((n, width), F32) for width in (in_width, out_width, 128))
        + tuple(jax.ShapeDtypeStruct((n, sum(b.shape[0] for b in blocks)), BF16) for blocks in more),
        in_specs=[VMEM] * (3 + len(flat) + len(carried) + len(wanted)),
        out_specs=(VMEM,) * outs,
        compiler_params=params(24),
        cost_estimate=COVER if more else BRIEF,
        name="backward",
    )(center_pos, coefficients, spread, *flat, *carried, *wanted)


def finish(center_pos, coefficients, spread, group, before):
    (n, out_width), in_width = coefficients.shape, center_pos.shape[1]
    kernel, xs, cot = group
    step = min(n, 256)

    def body(pos_ref, coef_ref, spread_ref, kernel_ref, cot_ref, *refs):
        x_refs, refs = refs[: len(xs)], refs[len(xs) :]
        moment_ref, grad_ref, lanes_ref, centers_out, coef_out, centers_buf, coef_buf, sems = refs
        x = jnp.concatenate([ref[...] for ref in x_refs])
        cot = cot_ref[...]
        scale = column(spread_ref[...].astype(F32)) * (2.0 / in_width)
        made = []
        for k, start in enumerate(range(0, n, step)):
            rows = slice(start, start + step)
            moment, grad, lanes = group_terms(coef_ref[rows], kernel_ref[rows], x, cot)
            coef_buf[rows] = grad_ref[rows] + grad
            moment += moment_ref[rows]
            total = jnp.sum(lanes_ref[rows] + lanes, axis=1, keepdims=True)
            for at in range(0, in_width, 128):
                pos = pos_ref[rows, at : at + 128].astype(F32)
                centers_buf[rows, at : at + 128] = scale[rows] * (moment[:, at : at + 128] - total * pos)
            pairs = [(centers_buf, centers_out), (coef_buf, coef_out)]
            for j, (src, dst) in enumerate(pairs):
                copy = pltpu.make_async_copy(src.at[rows], dst.at[rows], sems.at[2 * k + j])
                copy.start()
                made.append(copy)
        for copy in made:
            copy.wait()

    ins = [center_pos, coefficients, spread, kernel, cot, *xs, *before]
    return pl.pallas_call(
        body,
        out_shape=tuple(jax.ShapeDtypeStruct((n, width), F32) for width in (in_width, out_width)),
        in_specs=[VMEM] * len(ins),
        out_specs=(HBM, HBM),
        scratch_shapes=[
            pltpu.VMEM((n, in_width), F32),
            pltpu.VMEM((n, out_width), F32),
            pltpu.SemaphoreType.DMA((2 * pl.cdiv(n, step),)),
        ],
        compiler_params=params(24),
        cost_estimate=BRIEF,
        name="finish",
    )(*ins)


def solution(mesh):
    nz, nc = mesh.shape["points"], mesh.shape["centers"]

    def per_device(train_points, saved_preds, targets, huber_delta, center_pos, coefficients, spread):
        n_rows = train_points.shape[0]
        n, out_width = coefficients.shape
        piece = n_rows // nc

        own = lax.dynamic_slice_in_dim(train_points, lax.axis_index("centers") * piece, piece)

        layer = {0: own}
        for dz in range(2, nz, 2):
            layer[dz] = swap(own, "points", nz, dz)
        layer[1] = swap(own, "points", nz, 1)

        pos, side = {1: swap(center_pos, "centers", nc, 1)}, {}
        for d in range(2, nc, 2):
            pos[d] = swap(center_pos, "centers", nc, d)
        center_pos, side[0], delta, spread, coefficients = pack(
            after(center_pos, own), coefficients, spread, huber_delta
        )
        pos[0], side[1] = center_pos, swap(side[0], "centers", nc, 1)
        for d in range(2, nc, 2):
            side[d] = swap(side[0], "centers", nc, d)
        for dz in range(3, nz, 2):
            layer[dz] = swap(layer[dz - 1], "points", nz, 1)
        saved, target, *local = take(
            [saved_preds, targets] + [train_points] * (nc - 1), [0, 0, *range(1, nc)], piece
        )
        local = [own, *local]
        for d in range(2, nc, 2):
            pos[d + 1] = swap(after(pos[d], layer[1], layer[2], side[1], side[d], saved), "centers", nc, 1)
            side[d + 1] = swap(after(side[d], layer[2], side[1]), "centers", nc, 1)
        centers = [a for d in range(nc) for a in (pos[d], side[d])]

        early = {0: jnp.concatenate([layer[dz] for dz in range(1, nz - 1)])}

        first, second = range(2, nz, 2), range(3, nz, 2)
        parts = dict(zip(first, forward([layer[dz] for dz in first], centers, out_width, BRIEF)))
        received = {dz: swap(parts[dz], "points", nz, dz) for dz in first}
        rows = [after(layer[1], *parts.values())]
        (parts[1],) = forward(rows, centers, out_width, COVER)
        received[1] = swap(parts[1], "points", nz, 1)
        rows = [after(layer[dz], *parts.values()) for dz in second]
        parts.update(zip(second, forward(rows, centers, out_width, COVER)))
        soon = list(received.values())
        received = [swap(parts[dz], "points", nz, dz) for dz in second]
        last = parts[nz - 1]
        kernels, late = {1: None}, {0: layer[nz - 1]}
        parts[0], kernels[0] = own_rows(
            after(own, last),
            centers,
            out_width,
            soon,
            center_pos,
            spread,
            [[local[0], early[0], late[0]]],
        )
        for d in range(2, nc, 2):
            early[d] = swap(after(early[0], side[d + 1]), "centers", nc, d)
            late[d] = swap(after(late[0], last, *soon), "centers", nc, d)
            early[d + 1] = swap(after(early[d], parts[0]), "centers", nc, 1)
        early[1] = swap(after(early[0], parts[0]), "centers", nc, 1)
        late[1] = swap(after(late[0], parts[0]), "centers", nc, 1)
        cot = cotangent([parts[0], *received], saved, target, delta)

        far = {dz: swap(cot, "points", nz, dz) for dz in (*range(2, nz), 1)}
        ahead = {d: swap(after(cot, late[d]), "centers", nc, d) for d in range(2, nc, 2)}
        far[1] = after(far[1], *ahead.values())
        far = jnp.concatenate([far[dz] for dz in range(1, nz)])
        cots = {0: jnp.concatenate([cot, far])}
        across = {}
        for d in range(2, nc, 2):
            across[d] = [ahead[d], swap(far, "centers", nc, d)]
            late[d + 1] = swap(after(late[d], far), "centers", nc, 1)
        cots[1] = swap(cots[0], "centers", nc, 1)

        points = {d: [local[d], early[d], late[d]] for d in range(nc)}
        groups = [(kernels[d], points[d], cots[d]) for d in (0, 1)]
        *sums, kernels[2], kernels[3] = backward(
            center_pos, coefficients, spread, groups, more=[points[2], points[3]]
        )
        for d in range(4, nc):
            kernels[d] = own_kernel(center_pos, spread, points[d])
        for d in range(2, nc, 2):
            cots[d] = jnp.concatenate([after(a, sums[0]) for a in across[d]])
            cots[d + 1] = swap(cots[d], "centers", nc, 1)
        for d in range(2, nc - 1):
            group = (kernels[d], points[d], cots[d])
            sums = backward(center_pos, coefficients, spread, [group], before=sums)
        group = (kernels[nc - 1], points[nc - 1], cots[nc - 1])
        return finish(center_pos, coefficients, spread, group, sums)

    return jax.shard_map(
        per_device,
        mesh=mesh,
        in_specs=(
            P(("groups", "points"), None),
            P(("groups", "points"), None),
            P(("groups", "points"), None),
            P("groups"),
            P(("groups", "points", "centers"), None),
            P(("groups", "points", "centers"), None),
            P(("groups", "points", "centers")),
        ),
        out_specs=(
            P(("groups", "points", "centers"), None),
            P(("groups", "points", "centers"), None),
        ),
        check_vma=False,
    )
```

```python
import math

import jax
import jax.numpy as jnp
from jax import lax
from jax.experimental import pallas as pl
from jax.experimental.pallas import tpu as pltpu
from jax.sharding import PartitionSpec as P

F32, BF16 = jnp.float32, jnp.bfloat16
HBM = pl.BlockSpec(memory_space=pltpu.HBM)
VMEM = pl.BlockSpec(memory_space=pltpu.VMEM)
NT = (((1,), (1,)), ((), ()))
LOG2E = math.log2(math.e)
COVER = pl.CostEstimate(flops=1 << 34, bytes_accessed=1 << 20, transcendentals=1 << 20)
BRIEF = pl.CostEstimate(flops=1, bytes_accessed=1, transcendentals=0)


def swap(a, axis, size, d):
    return lax.ppermute(a, axis, [(i, i ^ d) for i in range(size)])


def after(a, *others):
    return lax.optimization_barrier((a, *others))[0]


def lane_groups(a):
    total = None
    for k in range(0, a.shape[1], 128):
        part = jnp.square(a[:, k : k + 128].astype(F32))
        total = part if total is None else total + part
    return total


def half_sq_row(a):
    return 0.5 * jnp.sum(lane_groups(a).T, axis=0, keepdims=True)


def half_sq_column(a):
    return 0.5 * jnp.sum(lane_groups(a), axis=1, keepdims=True)


def column(row):
    return jnp.broadcast_to(row, (128, row.shape[1])).T


def params(mib):
    return pltpu.CompilerParams(vmem_limit_bytes=mib << 20)


def pack(center_pos, coefficients, spread, delta):
    n, in_width = center_pos.shape
    out_width = coefficients.shape[1]
    across = in_width // out_width
    q = n // across

    def body(pos_ref, coef_ref, spread_ref, delta_ref, own_pos, out_ref, row_ref, own_spread, own_coef):
        row_ref[...] = delta_ref[...]
        own_spread[...] = spread_ref[...]
        own_coef[...] = coef_ref[...]
        pos = pos_ref[...]
        own_pos[...] = pos
        for k in range(across):
            out_ref[:q, k * out_width : (k + 1) * out_width] = coef_ref[k * q : (k + 1) * q]
        half = half_sq_row(pos)
        high = half.astype(BF16)
        rest = half - high.astype(F32)
        middle = rest.astype(BF16)
        low = (rest - middle.astype(F32)).astype(BF16)
        rows = [r.astype(F32) for r in (spread_ref[...], high, middle, low)]
        tail = jnp.concatenate(rows + [jnp.zeros((12, n), F32)]).astype(BF16)
        if n < in_width:
            tail = jnp.concatenate([tail, jnp.zeros((16, in_width - n), BF16)], axis=1)
        out_ref[q:] = tail

    return pl.pallas_call(
        body,
        out_shape=(
            jax.ShapeDtypeStruct((n, in_width), BF16),
            jax.ShapeDtypeStruct((q + 16, in_width), BF16),
            jax.ShapeDtypeStruct((1, delta.shape[0]), F32),
            jax.ShapeDtypeStruct((1, n), BF16),
            jax.ShapeDtypeStruct((n, out_width), BF16),
        ),
        in_specs=[VMEM] * 4,
        out_specs=(VMEM,) * 5,
        compiler_params=params(16),
        cost_estimate=BRIEF,
        name="pack",
    )(center_pos, coefficients, spread.reshape(1, n), delta.reshape(1, -1))


def take(arrays, offsets, piece):
    def body(*refs):
        ins, outs, sems = refs[: len(arrays)], refs[len(arrays) : -1], refs[-1]
        made = []
        for k, d in enumerate(offsets):
            start = pl.multiple_of((lax.axis_index("centers") ^ d) * piece, piece)
            made.append(pltpu.make_async_copy(ins[k].at[pl.ds(start, piece)], outs[k], sems.at[k]))
            made[-1].start()
        for copy in made:
            copy.wait()

    return pl.pallas_call(
        body,
        out_shape=tuple(jax.ShapeDtypeStruct((piece, a.shape[1]), a.dtype) for a in arrays),
        in_specs=[HBM] * len(arrays),
        out_specs=(VMEM,) * len(arrays),
        scratch_shapes=[pltpu.SemaphoreType.DMA((len(arrays),))],
        compiler_params=params(16),
        cost_estimate=BRIEF,
        name="take",
    )(*arrays)


def partial_pred(x, refs, total):
    in_width = x.shape[1]
    row_sq = half_sq_column(x)
    for pos_ref, side_ref in zip(refs[::2], refs[1::2]):
        n, q = pos_ref.shape[0], side_ref.shape[0] - 16
        out_width = q * in_width // n
        packed = side_ref[:q]
        coef = jnp.concatenate([packed[:, k : k + out_width] for k in range(0, in_width, out_width)])
        tail = side_ref[q:, :n].astype(F32)
        center_sq = tail[1:2] + tail[2:3] + tail[3:4]
        rate = tail[0:1] * (-2.0 * LOG2E / in_width)
        cross = lax.dot_general(x, pos_ref[...], NT, preferred_element_type=F32)
        power = (row_sq + center_sq - cross) * rate
        kernel = jnp.exp2(power).astype(BF16)
        new = jnp.dot(kernel, coef, preferred_element_type=F32)
        total = new if total is None else total + new
    return total


def own_values(pos_ref, spread_ref, refs):
    pos = pos_ref[...]
    center_sq = half_sq_column(pos)
    rate = column(spread_ref[...].astype(F32) * (-2.0 * LOG2E / pos.shape[1]))[:, :1]
    for ref in refs:
        step = min(256, ref.shape[0])
        for start in range(0, ref.shape[0], step):
            x = ref[start : start + step]
            cross = lax.dot_general(pos, x, NT, preferred_element_type=F32)
            power = (center_sq + half_sq_row(x) - cross) * rate
            yield jnp.exp2(power).astype(BF16)


def store_values(pos_ref, spread_ref, refs, out_ref):
    at = 0
    for part in own_values(pos_ref, spread_ref, refs):
        out_ref[:, at : at + part.shape[1]] = part
        at += part.shape[1]


def forward(rows, centers, out_width, cost):
    counts = [r.shape[0] for r in rows]

    def body(*refs):
        row_refs, refs, outs = refs[: len(rows)], refs[len(rows) : -len(rows)], refs[-len(rows) :]
        x = jnp.concatenate([ref[...] for ref in row_refs])
        total = partial_pred(x, refs, None)
        at = 0
        for ref, count in zip(outs, counts):
            ref[...] = total[at : at + count]
            at += count

    return pl.pallas_call(
        body,
        out_shape=tuple(jax.ShapeDtypeStruct((count, out_width), F32) for count in counts),
        in_specs=[VMEM] * (len(rows) + len(centers)),
        out_specs=(VMEM,) * len(rows),
        compiler_params=params(24),
        cost_estimate=cost,
        name="forward",
    )(*rows, *centers)


def own_kernel(center_pos, spread, blocks):
    n = spread.shape[1]
    points = sum(b.shape[0] for b in blocks)

    def body(pos_ref, spread_ref, *refs):
        store_values(pos_ref, spread_ref, refs[:-1], refs[-1])

    return pl.pallas_call(
        body,
        out_shape=jax.ShapeDtypeStruct((n, points), BF16),
        in_specs=[VMEM] * (2 + len(blocks)),
        out_specs=VMEM,
        compiler_params=params(16),
        cost_estimate=BRIEF,
        name="own_kernel",
    )(center_pos, spread, *blocks)


def own_rows(rows, centers, out_width, received, center_pos, spread, more):
    n = spread.shape[1]
    ends = [1, 1 + len(centers)]
    ends.append(ends[-1] + len(received))

    def body(*refs):
        outs, refs = refs[-1 - len(more) :], refs[: -1 - len(more)]
        total = None
        for ref in refs[ends[1] : ends[2]]:
            total = ref[...] if total is None else total + ref[...]
        outs[0][...] = partial_pred(refs[0][...], refs[1 : ends[1]], total)
        pos_ref, spread_ref, *block_refs = refs[ends[2] :]
        for k, blocks in enumerate(more):
            store_values(pos_ref, spread_ref, block_refs[: len(blocks)], outs[1 + k])
            del block_refs[: len(blocks)]

    ins = [rows, *centers, *received, center_pos, spread]
    ins += [block for blocks in more for block in blocks]
    return pl.pallas_call(
        body,
        out_shape=(jax.ShapeDtypeStruct((rows.shape[0], out_width), F32),)
        + tuple(jax.ShapeDtypeStruct((n, sum(b.shape[0] for b in blocks)), BF16) for blocks in more),
        in_specs=[VMEM] * len(ins),
        out_specs=(VMEM,) * (1 + len(more)),
        compiler_params=params(16),
        cost_estimate=COVER,
        name="own_rows",
    )(*ins)


def cotangent(parts, saved, target, delta):
    def body(*refs):
        saved_ref, target_ref, delta_ref, out_ref = refs[-4:]
        pred = refs[0][...]
        for ref in refs[1:-4]:
            pred += ref[...]
        residual = pred + saved_ref[...] - target_ref[...]
        ratio = residual / delta_ref[...]
        out_ref[...] = (residual / jnp.sqrt(1.0 + ratio * ratio)).astype(BF16)

    return pl.pallas_call(
        body,
        out_shape=jax.ShapeDtypeStruct(saved.shape, BF16),
        in_specs=[VMEM] * (len(parts) + 3),
        out_specs=VMEM,
        compiler_params=params(16),
        cost_estimate=BRIEF,
        name="cotangent",
    )(*parts, saved, target, delta)


def group_terms(coef, kernel, x, cot):
    mixing = lax.dot_general(coef, cot, NT, preferred_element_type=F32)
    weights = (kernel.astype(F32) * mixing).astype(BF16)
    lanes = weights[:, :128].astype(F32)
    for k in range(128, kernel.shape[1], 128):
        lanes += weights[:, k : k + 128].astype(F32)
    return (
        jnp.dot(weights, x, preferred_element_type=F32),
        jnp.dot(kernel, cot, preferred_element_type=F32),
        lanes,
    )


def backward(center_pos, coefficients, spread, groups, before=None, more=()):
    (n, out_width), in_width = coefficients.shape, center_pos.shape[1]
    flat = []
    for kernel, xs, cot in groups:
        flat += [*xs, cot] if kernel is None else [kernel, *xs, cot]
    carried = [] if before is None else list(before)
    outs = 3 + len(more)
    wanted = [block for blocks in more for block in blocks]

    def body(pos_ref, coef_ref, spread_ref, *refs):
        refs, out_refs = list(refs[:-outs]), refs[-outs:]
        coef = coef_ref[...]
        sums = [ref[...] for ref in refs[len(flat) : len(flat) + 3]] if carried else None
        block_refs = refs[len(flat) + len(carried) :]
        for k, blocks in enumerate(more):
            store_values(pos_ref, spread_ref, block_refs[: len(blocks)], out_refs[3 + k])
            del block_refs[: len(blocks)]
        for given, xs, _ in groups:
            kernel = None if given is None else refs.pop(0)[...]
            x_refs = [refs.pop(0) for _ in xs]
            if given is None:
                kernel = jnp.concatenate(list(own_values(pos_ref, spread_ref, x_refs)), axis=1)
            x = jnp.concatenate([ref[...] for ref in x_refs])
            terms = group_terms(coef, kernel, x, refs.pop(0)[...])
            sums = terms if sums is None else [a + b for a, b in zip(sums, terms)]
        for ref, value in zip(out_refs[:3], sums):
            ref[...] = value

    return pl.pallas_call(
        body,
        out_shape=tuple(jax.ShapeDtypeStruct((n, width), F32) for width in (in_width, out_width, 128))
        + tuple(jax.ShapeDtypeStruct((n, sum(b.shape[0] for b in blocks)), BF16) for blocks in more),
        in_specs=[VMEM] * (3 + len(flat) + len(carried) + len(wanted)),
        out_specs=(VMEM,) * outs,
        compiler_params=params(24),
        cost_estimate=COVER if more else BRIEF,
        name="backward",
    )(center_pos, coefficients, spread, *flat, *carried, *wanted)


def finish(center_pos, coefficients, spread, group, before):
    (n, out_width), in_width = coefficients.shape, center_pos.shape[1]
    kernel, xs, cot = group
    step = min(n, 128)

    def body(pos_ref, coef_ref, spread_ref, kernel_ref, cot_ref, *refs):
        x_refs, refs = refs[: len(xs)], refs[len(xs) :]
        moment_ref, grad_ref, lanes_ref, centers_out, coef_out, centers_buf, coef_buf, sems = refs
        x = jnp.concatenate([ref[...] for ref in x_refs])
        cot = cot_ref[...]
        scale = column(spread_ref[...].astype(F32)) * (2.0 / in_width)
        made = []
        for k, start in enumerate(range(0, n, step)):
            rows = slice(start, start + step)
            moment, grad, lanes = group_terms(coef_ref[rows], kernel_ref[rows], x, cot)
            coef_buf[rows] = grad_ref[rows] + grad
            moment += moment_ref[rows]
            total = jnp.sum(lanes_ref[rows] + lanes, axis=1, keepdims=True)
            for at in range(0, in_width, 128):
                pos = pos_ref[rows, at : at + 128].astype(F32)
                centers_buf[rows, at : at + 128] = scale[rows] * (moment[:, at : at + 128] - total * pos)
            pairs = [(centers_buf, centers_out), (coef_buf, coef_out)]
            for j, (src, dst) in enumerate(pairs):
                copy = pltpu.make_async_copy(src.at[rows], dst.at[rows], sems.at[2 * k + j])
                copy.start()
                made.append(copy)
        for copy in made:
            copy.wait()

    ins = [center_pos, coefficients, spread, kernel, cot, *xs, *before]
    return pl.pallas_call(
        body,
        out_shape=tuple(jax.ShapeDtypeStruct((n, width), F32) for width in (in_width, out_width)),
        in_specs=[VMEM] * len(ins),
        out_specs=(HBM, HBM),
        scratch_shapes=[
            pltpu.VMEM((n, in_width), F32),
            pltpu.VMEM((n, out_width), F32),
            pltpu.SemaphoreType.DMA((2 * pl.cdiv(n, step),)),
        ],
        compiler_params=params(24),
        cost_estimate=BRIEF,
        name="finish",
    )(*ins)


def solution(mesh):
    nz, nc = mesh.shape["points"], mesh.shape["centers"]

    def per_device(train_points, saved_preds, targets, huber_delta, center_pos, coefficients, spread):
        n_rows = train_points.shape[0]
        n, out_width = coefficients.shape
        piece = n_rows // nc

        own = lax.dynamic_slice_in_dim(train_points, lax.axis_index("centers") * piece, piece)

        layer = {0: own}
        for dz in range(2, nz, 2):
            layer[dz] = swap(own, "points", nz, dz)
        layer[1] = swap(own, "points", nz, 1)

        pos, side = {1: swap(center_pos, "centers", nc, 1)}, {}
        for d in range(2, nc, 2):
            pos[d] = swap(center_pos, "centers", nc, d)
        center_pos, side[0], delta, spread, coefficients = pack(
            after(center_pos, own), coefficients, spread, huber_delta
        )
        pos[0], side[1] = center_pos, swap(side[0], "centers", nc, 1)
        for d in range(2, nc, 2):
            side[d] = swap(side[0], "centers", nc, d)
        for dz in range(3, nz, 2):
            layer[dz] = swap(layer[dz - 1], "points", nz, 1)
        saved, target, *local = take(
            [saved_preds, targets] + [train_points] * (nc - 1), [0, 0, *range(1, nc)], piece
        )
        local = [own, *local]
        for d in range(2, nc, 2):
            pos[d + 1] = swap(after(pos[d], layer[1], layer[2], side[1], side[d], saved), "centers", nc, 1)
            side[d + 1] = swap(after(side[d], layer[2], side[1]), "centers", nc, 1)
        centers = [a for d in range(nc) for a in (pos[d], side[d])]

        early = {0: jnp.concatenate([layer[dz] for dz in range(1, nz - 1)])}

        first, second = range(2, nz, 2), range(3, nz, 2)
        parts = dict(zip(first, forward([layer[dz] for dz in first], centers, out_width, BRIEF)))
        received = {dz: swap(parts[dz], "points", nz, dz) for dz in first}
        rows = [after(layer[1], *parts.values())]
        (parts[1],) = forward(rows, centers, out_width, COVER)
        received[1] = swap(parts[1], "points", nz, 1)
        rows = [after(layer[dz], *parts.values()) for dz in second]
        parts.update(zip(second, forward(rows, centers, out_width, COVER)))
        soon = list(received.values())
        received = [swap(parts[dz], "points", nz, dz) for dz in second]
        last = parts[nz - 1]
        kernels, late = {1: None}, {0: layer[nz - 1]}
        parts[0], kernels[0] = own_rows(
            after(own, last),
            centers,
            out_width,
            soon,
            center_pos,
            spread,
            [[local[0], early[0], late[0]]],
        )
        for d in range(2, nc, 2):
            early[d] = swap(after(early[0], side[d + 1]), "centers", nc, d)
            late[d] = swap(after(late[0], last, *soon), "centers", nc, d)
            early[d + 1] = swap(after(early[d], parts[0]), "centers", nc, 1)
        early[1] = swap(after(early[0], parts[0]), "centers", nc, 1)
        late[1] = swap(after(late[0], parts[0]), "centers", nc, 1)
        cot = cotangent([parts[0], *received], saved, target, delta)

        far = {dz: swap(cot, "points", nz, dz) for dz in range(2, nz, 2)}
        far[1] = swap(cot, "points", nz, 1)
        for d in range(2, nc, 2):
            kernels[d] = own_kernel(center_pos, spread, [local[d], early[d], late[d]])
        held = [kernels[d] for d in range(2, nc, 2)]
        far.update({dz: swap(after(far[dz - 1], *held), "points", nz, 1) for dz in range(3, nz, 2)})
        ahead = {d: swap(after(cot, late[d]), "centers", nc, d) for d in range(2, nc, 2)}
        far[1] = after(far[1], *ahead.values())
        far = jnp.concatenate([far[dz] for dz in range(1, nz)])
        cots = {0: jnp.concatenate([cot, far])}
        across = {}
        for d in range(2, nc, 2):
            across[d] = [ahead[d], swap(far, "centers", nc, d)]
            late[d + 1] = swap(after(late[d], far), "centers", nc, 1)
        cots[1] = swap(cots[0], "centers", nc, 1)

        points = {d: [local[d], early[d], late[d]] for d in range(nc)}
        groups = [(kernels[d], points[d], cots[d]) for d in (0, 1)]
        *sums, kernels[3] = backward(
            center_pos, coefficients, spread, groups, more=[points[3]]
        )
        for d in range(5, nc, 2):
            kernels[d] = own_kernel(center_pos, spread, points[d])
        for d in range(2, nc, 2):
            cots[d] = jnp.concatenate([after(a, sums[0]) for a in across[d]])
            cots[d + 1] = swap(cots[d], "centers", nc, 1)
        for d in range(2, nc - 1):
            group = (kernels[d], points[d], cots[d])
            sums = backward(center_pos, coefficients, spread, [group], before=sums)
        group = (kernels[nc - 1], points[nc - 1], cots[nc - 1])
        return finish(center_pos, coefficients, spread, group, sums)

    return jax.shard_map(
        per_device,
        mesh=mesh,
        in_specs=(
            P(("groups", "points"), None),
            P(("groups", "points"), None),
            P(("groups", "points"), None),
            P("groups"),
            P(("groups", "points", "centers"), None),
            P(("groups", "points", "centers"), None),
            P(("groups", "points", "centers")),
        ),
        out_specs=(
            P(("groups", "points", "centers"), None),
            P(("groups", "points", "centers"), None),
        ),
        check_vma=False,
    )
```
